512 devices in a mesh: ctx: 64 (over z, x), tp: 8 (over y, core).
Axes of the slice: x: 4, y: 4, z: 16, core: 2. Of those that a mesh axis runs over, the one named last changes fastest.
Arguments:
- outer_input: bfloat16 [4096, 8192], P('ctx', 'tp'), may hold values from -6 to 6
- inner_input: bfloat16 [4096, 8192], P('ctx', 'tp'), may hold values from -6 to 6
- value_input: bfloat16 [4096, 8192], P('ctx', 'tp'), may hold values from -6 to 6
- feature_taps: bfloat16 [3, 7, 8192], P(None, None, 'tp'), may hold values from -2 to 2
- medium_taps: bfloat16 [128, 512], P(None, 'tp'), may hold values from -0.5 to 0.5
- decay_rates: float32 [512, 16], P('tp'), may hold values from 1e-05 to 0.04
- residues: float32 [512, 16], P('tp'), may hold values from -4 to 4
- residual: bfloat16 [4096, 8192], P('ctx', 'tp'), may hold values from -72 to 72
- norm_gain: bfloat16 [8192], P('tp'), may hold values from 0.5 to 1.5
Outputs:
- normed: bfloat16 [4096, 8192], P('ctx', 'tp')
The draws below stay inside these ranges and needn't reach their ends.
All inputs are finite; a program needn't handle non-finite values.
Results may differ from the reference program's by a relative error of at most 0.0039.
Values may be sent and summed in bfloat16 or wider, within the bound.
No kernel may reach another device: no remote copies, remote signals or barrier semaphores. Data moves between devices by JAX's collectives and lax.ppermute only.
A program may use at most 128 MiB of HBM per device.

```python
import math
import jax
import jax.numpy as jnp
from jax import lax

D = 8192
GROUP = 16
MODES = 16
FEAT_TAPS = 7
MR_TAPS = 128
SEQ = 4096
GROUPS = 512


def draw_decay_rates(key, part):
    key_slow = jax.random.fold_in(jax.random.fold_in(key, 31), 0)
    log_low = math.log(1e-05)
    rates = jnp.exp(jax.random.uniform(key_slow, (GROUPS, MODES), minval=log_low, maxval=math.log(0.04)))
    return jnp.clip(rates, 1e-05, 0.04).astype(jnp.float32)


def draw_residual(key, part):
    key_base, key_column, key_row = jax.random.split(jax.random.fold_in(key, 41), 3)
    channel = jnp.arange(D, dtype=jnp.float32)
    ramp = jnp.sqrt(1.0 + 3.0 * channel / D)[None, :]
    column_scale = jnp.exp(jax.random.uniform(key_column, (1, D), minval=math.log(0.3), maxval=math.log(3.0)))
    row_scale = jnp.exp(jax.random.uniform(key_row, (SEQ, 1), minval=math.log(0.3), maxval=math.log(3.0)))
    base = jnp.clip(jax.random.normal(key_base, (SEQ, D)), -4.0, 4.0)
    return (base * row_scale * column_scale * ramp).astype(jnp.bfloat16)


def shard_levels(rng, extent, shards, least, largest):
    gain = 1.0
    for position, parts in shards:
        steps = jax.random.uniform(jax.random.fold_in(jax.random.fold_in(rng, 6), position), (parts,), jnp.float32, least / len(shards), largest / len(shards))
        gain = gain * jnp.repeat(jnp.exp(steps), extent[position] // parts).reshape((-1,) + (1,) * (len(extent) - 1 - position))
    return gain


def gaussian(key, extent, width, limit, cuts=(), kind=jnp.bfloat16):
    values = width * jax.random.normal(key, extent, jnp.float32)
    if cuts:
        values = values * shard_levels(key, extent, cuts, -0.22, 0.18)
    return jnp.clip(values, -limit, limit).astype(kind)


def setup_inputs(seed: int = 0) -> dict:
    streams_of = jax.random.split(jax.random.key(seed), 10)
    return {
        "outer_input": gaussian(streams_of[0], (SEQ, D), 1.0, 6.0, ((0, 64), (1, 8))),
        "inner_input": gaussian(streams_of[1], (SEQ, D), 1.0, 6.0, ((0, 64), (1, 8))),
        "value_input": gaussian(streams_of[2], (SEQ, D), 1.0, 6.0, ((0, 64), (1, 8))),
        "feature_taps": gaussian(streams_of[3], (3, FEAT_TAPS, D), FEAT_TAPS ** -0.5, 2.0, ((2, 8),)),
        "medium_taps": gaussian(streams_of[4], (MR_TAPS, GROUPS), MR_TAPS ** -0.5, 0.5, ((1, 8),)),
        "decay_rates": draw_decay_rates(jax.random.fold_in(streams_of[9], 71), 0),
        "residues": gaussian(streams_of[6], (GROUPS, MODES), 1.0, 4.0, ((0, 8),), jnp.float32),
        "residual": draw_residual(jax.random.fold_in(streams_of[9], 71), 0),
        "norm_gain": jnp.clip(1.0 + 0.1 * jax.random.normal(streams_of[8], (D,), jnp.float32), 0.5, 1.5).astype(jnp.bfloat16),
    }


def featurize(signal, tap_table):
    seq_rows = signal.shape[0]
    rim_rows = tap_table.shape[0] - 1
    padded = jnp.pad(signal.astype(jnp.float32), ((rim_rows, 0), (0, 0)))
    summed = jnp.zeros(signal.shape, jnp.float32)
    for offset in range(tap_table.shape[0]):
        window = padded[rim_rows - offset:rim_rows - offset + seq_rows]
        summed = summed + tap_table[offset].astype(jnp.float32)[None, :] * window
    return summed

def causal_conv(product, filters):
    seq_rows = product.shape[0]
    fft_length = 2 * seq_rows
    step_groups = max(1, GROUPS // 8)
    outputs = []
    for group_start in range(0, GROUPS, step_groups):
        group_end = min(GROUPS, group_start + step_groups)
        channel_block = product[:, group_start * GROUP:group_end * GROUP].astype(jnp.float32)
        spectrum = jnp.fft.rfft(channel_block, n=fft_length, axis=0)
        kernel = jnp.fft.rfft(filters[:, group_start:group_end], n=fft_length, axis=0)
        kernel = jnp.repeat(kernel, GROUP, axis=1)
        result = jnp.fft.irfft(spectrum * kernel, n=fft_length, axis=0)[:seq_rows]
        outputs.append(result.astype(jnp.float32))
    return jnp.concatenate(outputs, 1)

def reference(outer_input, inner_input, value_input, feature_taps, medium_taps, decay_rates, residues, residual, norm_gain):
    seq_rows = outer_input.shape[0]
    outer_feat = featurize(outer_input, feature_taps[0])
    inner_feat = featurize(inner_input, feature_taps[1])
    value_feat = featurize(value_input, feature_taps[2])
    product = (inner_feat * value_feat).astype(jnp.bfloat16)
    lag_rows = jnp.arange(seq_rows, dtype=jnp.int32).astype(jnp.float32)[:, None]
    mode_weight = residues * jnp.sqrt(2.0 * decay_rates / MODES)
    long_filter = jnp.zeros((seq_rows, GROUPS), jnp.float32)
    for mode_index in range(MODES):
        long_filter = long_filter + mode_weight[:, mode_index][None, :] * jnp.exp(-decay_rates[:, mode_index][None, :] * lag_rows)
    filters = long_filter.at[:MR_TAPS].add(medium_taps.astype(jnp.float32))
    mixed_conv = causal_conv(product, filters)
    hidden = residual.astype(jnp.float32) + outer_feat * mixed_conv
    square_sum = lax.optimization_barrier(jnp.sum(hidden * hidden, axis=1, keepdims=True))
    normed = (hidden * norm_gain.astype(jnp.float32)[None, :] / jnp.sqrt(square_sum / D + 1e-05)).astype(jnp.bfloat16)
    return normed
```

```python
import functools

import jax
import jax.numpy as jnp
from jax import lax
from jax.experimental import pallas as pl
from jax.experimental.pallas import tpu as pltpu
from jax.sharding import PartitionSpec as P

D = 8192
F32 = jnp.float32
BF16 = jnp.bfloat16
LANES = 128
HALO = 8


def iota(shape, axis):
    return lax.broadcasted_iota(jnp.int32, shape, axis)


def split(x):
    high = x.astype(BF16)
    return high, (x - high.astype(F32)).astype(BF16)


def tables_kernel(place, decay_ref, residue_ref, medium_ref, table_ref, step_ref):
    group = place[0]
    modes = decay_ref.shape[1]
    taps, groups = medium_ref.shape
    square = (LANES, LANES)
    block = LANES // 2
    row, lane = iota(square, 0), iota(square, 1)
    pick = iota((modes, LANES), 0) == iota((modes, LANES), 1) % modes
    eye = iota((modes, modes), 0) == iota((modes, modes), 1)

    def column(ref):
        line = ref[pl.ds(group, 1), :]
        return jnp.sum(jnp.where(eye, jnp.broadcast_to(line, (modes, modes)), 0.0), 1, keepdims=True)

    rate = column(decay_ref)
    weight = column(residue_ref) * jnp.sqrt(2.0 * rate / modes)

    def along_lanes(x):
        return jnp.sum(jnp.where(pick, x, 0.0), 0, keepdims=True)

    def along_rows(x):
        return jnp.sum(jnp.where(row == lane, along_lanes(x), 0.0), 1, keepdims=True)

    lag = iota((modes, LANES), 1).astype(F32)
    long_row = jnp.sum(weight * jnp.exp(-rate * lag), 0, keepdims=True)
    one_hot = (iota((8, groups), 1) == group).astype(BF16)
    medium_row = lax.dot_general(
        one_hot, medium_ref[...], (((1,), (1,)), ((), ())), preferred_element_type=F32
    )[:1]
    zero_row = jnp.zeros((1, LANES), F32)

    def toeplitz(filter_row):
        wide = jnp.concatenate([filter_row, zero_row], 1)
        wide = jnp.broadcast_to(wide, (LANES, 2 * LANES))
        return pltpu.roll(wide, 0, 1, stride=1, stride_axis=0)

    same = row // block == lane // block
    medium_wide = toeplitz(medium_row)
    near = jnp.where(same, medium_wide[:, :LANES] + toeplitz(long_row)[:, :LANES], 0.0)
    near_high, near_low = split(near)
    middle = jnp.concatenate([medium_wide[:, block:LANES], medium_wide[:, LANES : LANES + block]], 1)
    table_ref[0] = near_high
    table_ref[1] = near_low
    table_ref[2] = jnp.where(same, middle, 0.0).astype(BF16)
    table_ref[3] = jnp.where(same, medium_wide[:, LANES:], 0.0).astype(BF16)
    width = 2 * modes
    rate_lanes, rate_rows, weight_rows = along_lanes(rate), along_rows(rate), along_rows(weight)
    to_end = jnp.exp(-rate_lanes * (block - 1 - row % block).astype(F32))
    to_end = jnp.where(((lane // modes) % 2 == row // block) & (lane < 3 * width), to_end, 0.0)
    table_ref[4], table_ref[5] = split(to_end)
    from_start = weight_rows * jnp.exp(-rate_rows * (lane % block + 1).astype(F32))
    from_start = jnp.where(((row // modes) % 2 == lane // block) & (row < 3 * width), from_start, 0.0)
    start_high, start_low = split(from_start)
    table_ref[6] = jnp.where(row < 2 * width, start_high.astype(F32), start_low.astype(F32)).astype(BF16)
    step_ref[...] = jnp.broadcast_to(jnp.exp(-rate_lanes * block), step_ref.shape)


def featurized(tap_ref, which, tile, padded):
    taps = tap_ref.shape[1]
    rows = padded.shape[0] - HALO
    lanes = slice(tile * LANES, (tile + 1) * LANES)
    total = None
    for k in range(taps):
        term = tap_ref[which, k : k + 1, lanes].astype(F32) * padded[HALO - k : HALO - k + rows, :]
        total = term if total is None else total + term
    return total


def product_kernel(halo_ref, inner_ref, value_ref, tap_ref, out_ref, padded):
    rows, channels = inner_ref.shape
    for tile in range(channels // LANES):
        lanes = slice(tile * LANES, (tile + 1) * LANES)
        for n, ref in enumerate((inner_ref, value_ref)):
            padded[n, tile, :HALO] = halo_ref[HALO * (n + 1) : HALO * (n + 2), lanes].astype(F32)
            padded[n, tile, HALO:] = ref[:, lanes].astype(F32)
    for tile in range(channels // LANES):
        inner = featurized(tap_ref, 1, tile, padded.at[0, tile])
        value = featurized(tap_ref, 2, tile, padded.at[1, tile])
        product = (inner * value).astype(BF16).astype(F32)
        both = jnp.concatenate([product, pltpu.roll(product, LANES - 8, 1)], 0).T
        slabs = both.reshape(LANES // 16, 16, LANES)[:, :8].reshape(LANES // 2, LANES)
        out_ref[tile * (LANES // 2) : (tile + 1) * (LANES // 2)] = slabs.astype(BF16)


def conv_kernel(x_ref, table_ref, step_ref, out_ref, state):
    def dot(a, b):
        return jnp.dot(a, b, preferred_element_type=F32)

    rows = x_ref.shape[0]
    x = x_ref[...]
    local = dot(x, table_ref[4]) + dot(x, table_ref[5])
    step = step_ref[...]
    carry = jnp.zeros((8, LANES), F32)
    for block in range(rows // 8):
        state[8 * block : 8 * block + 8] = carry
        carry = carry * step + local[8 * block : 8 * block + 8]
    carried = state[...]
    high, low = split(carried)
    lane = iota(carried.shape, 1)
    width = 32
    second = (lane >= width) & (lane < 2 * width)
    mixed_state = jnp.where(second, low.astype(F32), high.astype(F32)).astype(BF16)
    wide = x.astype(F32)
    zeros = jnp.zeros((8, LANES), F32)
    before = jnp.concatenate([zeros, wide[:-8]], 0).astype(BF16)
    earlier = jnp.concatenate([zeros, zeros, wide[:-16]], 0).astype(BF16)
    mixed = dot(x, table_ref[0]) + dot(x, table_ref[1])
    mixed = mixed + dot(before, table_ref[2]) + dot(earlier, table_ref[3])
    out_ref[...] = (mixed + dot(mixed_state, table_ref[6])).astype(BF16)


def hidden_kernel(mixed_ref, halo_ref, outer_ref, tap_ref, residual_ref, hidden_ref, sum_ref, padded):
    rows, channels = outer_ref.shape
    for tile in range(channels // LANES):
        lanes = slice(tile * LANES, (tile + 1) * LANES)
        padded[tile, :HALO] = halo_ref[:HALO, lanes].astype(F32)
        padded[tile, HALO:] = outer_ref[:, lanes].astype(F32)
    squares = jnp.zeros((rows, LANES), F32)
    for tile in range(channels // LANES):
        lanes = slice(tile * LANES, (tile + 1) * LANES)
        slabs = mixed_ref[tile * (LANES // 2) : (tile + 1) * (LANES // 2)].astype(F32)
        other = pltpu.roll(slabs, LANES // 2, 1)
        groups = LANES // 16
        both = jnp.concatenate([slabs.reshape(groups, 8, LANES), other.reshape(groups, 8, LANES)], 1)
        mixed = both.reshape(LANES, LANES).T[:rows]
        outer = featurized(tap_ref, 0, tile, padded.at[tile])
        hidden = residual_ref[:, lanes].astype(F32) + outer * mixed
        hidden_ref[:, lanes] = hidden
        squares = squares + hidden * hidden
    tall = jnp.concatenate([squares, jnp.zeros_like(squares)], 0).T
    line = jnp.sum(tall, 0, keepdims=True)
    sum_ref[...] = jnp.broadcast_to(line, sum_ref.shape)


def norm_kernel(hidden_ref, sum_ref, gain_ref, out_ref):
    rows, channels = hidden_ref.shape
    parts = sum_ref[...].reshape(sum_ref.shape[0] // 8, 8, LANES)
    line = jnp.sum(parts, 0)
    scale = 1.0 / jnp.sqrt(line / D + 1e-05)
    tall = jnp.broadcast_to(scale[:1], (LANES, LANES)).T[:rows]
    for tile in range(channels // LANES):
        lanes = slice(tile * LANES, (tile + 1) * LANES)
        out_ref[:, lanes] = (hidden_ref[:, lanes] * gain_ref[:, lanes].astype(F32) * tall).astype(BF16)


def on_device(
    outer_input,
    inner_input,
    value_input,
    feature_taps,
    medium_taps,
    decay_rates,
    residues,
    residual,
    norm_gain,
):
    rows, channels = outer_input.shape
    groups, modes = decay_rates.shape
    size = lax.axis_size("ctx")
    parts = lax.axis_size("tp")
    tiles = channels // LANES
    call = pl.pallas_call
    vmem = pl.BlockSpec(memory_space=pltpu.VMEM)
    sent = jnp.concatenate([a[rows - HALO :] for a in (outer_input, inner_input, value_input)], 0)
    halo = lax.ppermute(sent, "ctx", [(i, i + 1) for i in range(size - 1)])
    place = lax.axis_index("ctx").reshape(1).astype(jnp.int32)
    table, step = call(
        tables_kernel,
        in_specs=[pl.BlockSpec(memory_space=pltpu.SMEM), vmem, vmem, vmem],
        out_specs=[vmem, vmem],
        out_shape=[
            jax.ShapeDtypeStruct((7, LANES, LANES), BF16),
            jax.ShapeDtypeStruct((8, LANES), F32),
        ],
        name="tables",
    )(place, decay_rates, residues, medium_taps)
    slab_rows = rows * channels // LANES
    slabs = call(
        product_kernel,
        out_shape=jax.ShapeDtypeStruct((slab_rows, LANES), BF16),
        scratch_shapes=[pltpu.VMEM((2, tiles, HALO + rows, LANES), F32)],
        name="product",
    )(halo, inner_input, value_input, feature_taps)
    slab = (size, slab_rows // size, LANES)
    arrived = lax.all_to_all(slabs.reshape(slab), "ctx", 0, 0)
    mixed = call(
        conv_kernel,
        out_shape=jax.ShapeDtypeStruct((slab_rows, LANES), BF16),
        scratch_shapes=[pltpu.VMEM((slab_rows, LANES), F32)],
        name="conv",
    )(arrived.reshape(slab_rows, LANES), table, step)
    returned = lax.all_to_all(mixed.reshape(slab), "ctx", 0, 0)
    hidden, sums = call(
        hidden_kernel,
        out_shape=[
            jax.ShapeDtypeStruct((rows, channels), F32),
            jax.ShapeDtypeStruct((8 * parts, LANES), F32),
        ],
        scratch_shapes=[pltpu.VMEM((tiles, HALO + rows, LANES), F32)],
        name="hidden",
    )(returned.reshape(slab_rows, LANES), halo, outer_input, feature_taps, residual)
    all_sums = lax.all_to_all(sums.reshape(parts, 8, LANES), "tp", 0, 0)
    return call(
        norm_kernel,
        out_shape=jax.ShapeDtypeStruct((rows, channels), BF16),
        name="norm",
    )(hidden, all_sums.reshape(8 * parts, LANES), norm_gain.reshape(1, channels))


def solution(mesh):
    return jax.shard_map(
        on_device,
        mesh=mesh,
        in_specs=(
            P("ctx", "tp"),
            P("ctx", "tp"),
            P("ctx", "tp"),
            P(None, None, "tp"),
            P(None, "tp"),
            P("tp", None),
            P("tp", None),
            P("ctx", "tp"),
            P("tp"),
        ),
        out_specs=P("ctx", "tp"),
        check_vma=False,
    )
```

```python
import functools

import jax
import jax.numpy as jnp
from jax import lax
from jax.experimental import pallas as pl
from jax.experimental.pallas import tpu as pltpu
from jax.sharding import PartitionSpec as P

D = 8192
F32 = jnp.float32
BF16 = jnp.bfloat16
LANES = 128
HALO = 8
NEAR = 16


def iota(shape, axis):
    return lax.broadcasted_iota(jnp.int32, shape, axis)


def in_vmem(*arrays):
    return [pltpu.with_memory_space_constraint(a, pltpu.VMEM) for a in arrays]


def split(x):
    high = x.astype(BF16)
    return high, (x - high.astype(F32)).astype(BF16)


def split_three(x, width):
    high, rest = split(x)
    middle, _ = split(x - high.astype(F32))
    low = x - high.astype(F32) - middle.astype(F32)
    copy = iota(x.shape, 1) // width
    part = jnp.where(copy == 0, high.astype(F32), jnp.where(copy == 1, middle.astype(F32), low))
    return jnp.where(copy < 3, part, 0.0).astype(BF16)


def join_three(parts, width):
    x = parts.astype(F32)
    x = x + pltpu.roll(x, width, 1)
    return x + pltpu.roll(x, 2 * width, 1)


def two_parts(x, width):
    high, low = split(x)
    copy = iota(x.shape, 1) // width
    return jnp.where(copy == 1, low.astype(F32), high.astype(F32)).astype(BF16)


def tables_kernel(place, decay_ref, residue_ref, medium_ref, table_ref, step_ref, jump_ref):
    modes, groups = decay_ref.shape
    square = (LANES, LANES)
    block = LANES // 2
    row, lane = iota(square, 0), iota(square, 1)
    same = row // block == lane // block
    pick = iota((modes, LANES), 0) == iota((modes, LANES), 1) % modes
    lag = iota((modes, LANES), 1).astype(F32)
    zero_row = jnp.zeros((1, LANES), F32)
    width = 2 * modes
    count = table_ref.shape[0]

    def along_lanes(x):
        return jnp.sum(jnp.where(pick, x, 0.0), 0, keepdims=True)

    def along_rows(x):
        return jnp.sum(jnp.where(row == lane, along_lanes(x), 0.0), 1, keepdims=True)

    def toeplitz(filter_row):
        wide = jnp.concatenate([filter_row, zero_row], 1)
        wide = jnp.broadcast_to(wide, (LANES, 2 * LANES))
        return pltpu.roll(wide, 0, 1, stride=1, stride_axis=0)

    for q in range(count):
        group = place[0] * count + q
        mine = iota((modes, groups), 1) == group
        rate = jnp.sum(jnp.where(mine, decay_ref[...], 0.0), 1, keepdims=True)
        weight = jnp.sum(jnp.where(mine, residue_ref[...], 0.0), 1, keepdims=True)
        weight = weight * jnp.sqrt(2.0 * rate / modes)
        long_row = jnp.sum(weight * jnp.exp(-rate * lag), 0, keepdims=True)
        chosen = iota(medium_ref.shape, 0) == group
        medium_row = jnp.sum(jnp.where(chosen, medium_ref[...].astype(F32), 0.0), 0, keepdims=True)
        medium_wide = toeplitz(medium_row)
        near = jnp.where(same, medium_wide[:, :LANES] + toeplitz(long_row)[:, :LANES], 0.0)
        table_ref[q, 0], table_ref[q, 1] = split(near)
        middle = [medium_wide[:, block:LANES], medium_wide[:, LANES : LANES + block]]
        table_ref[q, 2] = jnp.where(same, jnp.concatenate(middle, 1), 0.0).astype(BF16)
        table_ref[q, 3] = jnp.where(same, medium_wide[:, LANES:], 0.0).astype(BF16)
        rate_lanes, rate_rows, weight_rows = along_lanes(rate), along_rows(rate), along_rows(weight)
        to_end = jnp.exp(-rate_lanes * (block - 1 - row % block).astype(F32))
        kept = ((lane // modes) % 2 == row // block) & (lane < 3 * width)
        table_ref[q, 4], table_ref[q, 5] = split(jnp.where(kept, to_end, 0.0))
        from_start = weight_rows * jnp.exp(-rate_rows * (lane % block + 1).astype(F32))
        kept = ((row // modes) % 2 == lane // block) & (row < 3 * width)
        high, low = split(jnp.where(kept, from_start, 0.0))
        both = jnp.where(row < 2 * width, high.astype(F32), low.astype(F32))
        table_ref[q, 6] = both.astype(BF16)
        rows = slice(8 * q, 8 * q + 8)
        step_ref[rows] = jnp.broadcast_to(jnp.exp(-rate_lanes * block), (8, LANES))
        jump_ref[rows] = jnp.broadcast_to(jnp.exp(-rate_lanes * (block * NEAR)), (8, LANES))


def featurized(tap_ref, which, lanes, padded, rows):
    total = None
    for k in range(tap_ref.shape[1]):
        term = tap_ref[which, k : k + 1, lanes].astype(F32) * padded[HALO - k : HALO - k + rows, :]
        total = term if total is None else total + term
    return total


def tile_lanes(tile):
    return slice(tile * LANES, (tile + 1) * LANES)


def body_kernel(inner_ref, value_ref, tap_ref, out_ref, head_ref, padded):
    rows, channels = inner_ref.shape
    for tile in range(channels // LANES):
        lanes = tile_lanes(tile)
        feats = []
        for n, ref in enumerate((inner_ref, value_ref)):
            wide = ref[:, lanes].astype(F32)
            padded[n, tile] = wide
            head_ref[n, :, lanes] = wide[:HALO]
            feats.append(featurized(tap_ref, n + 1, lanes, padded.at[n, tile], rows - HALO))
        out_ref[:, lanes] = feats[0] * feats[1]


def product_kernel(halo_ref, head_ref, body_ref, tap_ref, out_ref, padded):
    channels = body_ref.shape[1]
    for tile in range(channels // LANES):
        lanes = tile_lanes(tile)
        feats = []
        for n in range(2):
            padded[n, tile, :HALO] = halo_ref[HALO * (n + 1) : HALO * (n + 2), lanes].astype(F32)
            padded[n, tile, HALO:] = head_ref[n, :, lanes]
            feats.append(featurized(tap_ref, n + 1, lanes, padded.at[n, tile], HALO))
        product = jnp.concatenate([feats[0] * feats[1], body_ref[:, lanes]], 0)
        product = product.astype(BF16).astype(F32)
        both = jnp.concatenate([product, pltpu.roll(product, LANES - 8, 1)], 0).T
        slabs = both.reshape(LANES // 16, 16, LANES)[:, :8].reshape(LANES // 2, LANES)
        out_ref[tile * (LANES // 2) : (tile + 1) * (LANES // 2)] = slabs.astype(BF16)


def outer_kernel(halo_ref, outer_ref, tap_ref, out_ref, padded):
    rows, channels = outer_ref.shape
    for tile in range(channels // LANES):
        lanes = tile_lanes(tile)
        padded[tile, :HALO] = halo_ref[:HALO, lanes].astype(F32)
        padded[tile, HALO:] = outer_ref[:, lanes].astype(F32)
        out_ref[:, lanes] = featurized(tap_ref, 0, lanes, padded.at[tile], rows)


def dot(a, b):
    return jnp.dot(a, b, preferred_element_type=F32)


def of_group(x, q, count):
    return x.reshape(x.shape[0] // (8 * count), count, 8, LANES)[:, q].reshape(-1, LANES)


def states_kernel(width, x_ref, table_ref, step_ref, state_ref, end_ref, send_ref):
    count = table_ref.shape[0]
    blocks = x_ref.shape[0] // (8 * count)
    wide = x_ref[...].astype(F32)
    ends = []
    for q in range(count):
        x = of_group(wide, q, count).astype(BF16)
        local = dot(x, table_ref[q, 4]) + dot(x, table_ref[q, 5])
        step = step_ref[8 * q : 8 * q + 8]
        carry = jnp.zeros((8, LANES), F32)
        for block in range(blocks):
            at = 8 * (count * block + q)
            state_ref[at : at + 8] = carry
            carry = carry * step + local[8 * block : 8 * block + 8]
        ends.append(carry)
    end = jnp.concatenate(ends, 0)
    end_ref[...] = end
    rows = 8 * count
    send_ref[:rows] = split_three(end, width)
    send_ref[rows:] = x_ref[(blocks - 2) * rows :]


def chain_kernel(width, got_ref, end_ref, jump_ref, send_ref, next_ref):
    rows = end_ref.shape[0]
    end = end_ref[...] + jump_ref[...] * join_three(got_ref[:rows], width)
    next_ref[:rows] = split_three(end, width)
    next_ref[rows:] = send_ref[rows:]


def local_kernel(width, x_ref, table_ref, state_ref, out_ref):
    count = table_ref.shape[0]
    wide = x_ref[...].astype(F32)
    states = state_ref[...]
    zeros = jnp.zeros((8, LANES), F32)
    for q in range(count):
        x = of_group(wide, q, count)
        before = jnp.concatenate([zeros, x[:-8]], 0).astype(BF16)
        earlier = jnp.concatenate([zeros, zeros, x[:-16]], 0).astype(BF16)
        x = x.astype(BF16)
        mixed = dot(x, table_ref[q, 0]) + dot(x, table_ref[q, 1])
        mixed = mixed + dot(before, table_ref[q, 2]) + dot(earlier, table_ref[q, 3])
        mixed = mixed + dot(two_parts(of_group(states, q, count), width), table_ref[q, 6])
        for block in range(x.shape[0] // 8):
            at = 8 * (count * block + q)
            out_ref[at : at + 8] = mixed[8 * block : 8 * block + 8]


def finish_kernel(width, local_ref, first_ref, second_ref, third_ref, table_ref, step_ref, out_ref):
    count = table_ref.shape[0]
    rows = 8 * count
    blocks = local_ref.shape[0] // rows
    got = first_ref[...].astype(F32) + second_ref[...].astype(F32) + third_ref[...].astype(F32)
    incoming = join_three(got[:rows], width)
    zeros = jnp.zeros((8, LANES), F32)
    parts = []
    for q in range(count):
        at = slice(8 * q, 8 * q + 8)
        step = step_ref[at]
        state = incoming[at]
        states = []
        for block in range(blocks):
            states.append(state)
            state = state * step
        mixed = dot(two_parts(jnp.concatenate(states, 0), width), table_ref[q, 6])
        last_but_one, last = got[rows:][at], got[2 * rows :][at]
        before = jnp.concatenate([last, zeros], 0).astype(BF16)
        earlier = jnp.concatenate([last_but_one, last], 0).astype(BF16)
        start = dot(before, table_ref[q, 2]) + dot(earlier, table_ref[q, 3])
        mixed = jnp.concatenate([mixed[:16] + start, mixed[16:]], 0)
        parts.append(mixed.reshape(blocks, 8, LANES))
    total = local_ref[...] + jnp.concatenate(parts, 1).reshape(local_ref.shape)
    out_ref[...] = total.astype(BF16)


def hidden_kernel(mixed_ref, outer_ref, residual_ref, hidden_ref, sum_ref):
    rows, channels = outer_ref.shape
    squares = jnp.zeros((rows, LANES), F32)
    for tile in range(channels // LANES):
        lanes = tile_lanes(tile)
        slabs = mixed_ref[tile * (LANES // 2) : (tile + 1) * (LANES // 2)].astype(F32)
        other = pltpu.roll(slabs, LANES // 2, 1)
        groups = LANES // 16
        both = jnp.concatenate([slabs.reshape(groups, 8, LANES), other.reshape(groups, 8, LANES)], 1)
        mixed = both.reshape(LANES, LANES).T[:rows]
        hidden = residual_ref[:, lanes].astype(F32) + outer_ref[:, lanes] * mixed
        hidden_ref[:, lanes] = hidden
        squares = squares + hidden * hidden
    tall = jnp.concatenate([squares, jnp.zeros_like(squares)], 0).T
    line = jnp.sum(tall, 0, keepdims=True)
    sum_ref[...] = jnp.broadcast_to(line, sum_ref.shape)


def norm_kernel(hidden_ref, sum_ref, gain_ref, out_ref):
    rows, channels = hidden_ref.shape
    parts = sum_ref[...].reshape(sum_ref.shape[0] // 8, 8, LANES)
    line = jnp.sum(parts, 0)
    scale = 1.0 / jnp.sqrt(line / D + 1e-05)
    tall = jnp.broadcast_to(scale[:1], (LANES, LANES)).T[:rows]
    for tile in range(channels // LANES):
        lanes = slice(tile * LANES, (tile + 1) * LANES)
        out_ref[:, lanes] = (hidden_ref[:, lanes] * gain_ref[:, lanes].astype(F32) * tall).astype(BF16)


def on_device(
    outer_input,
    inner_input,
    value_input,
    feature_taps,
    medium_taps,
    decay_rates,
    residues,
    residual,
    norm_gain,
):
    rows, channels = outer_input.shape
    groups, modes = decay_rates.shape
    size = lax.axis_size("ctx")
    parts = lax.axis_size("tp")
    tiles = channels // LANES
    vmem = pl.BlockSpec(memory_space=pltpu.VMEM)
    smem = pl.BlockSpec(memory_space=pltpu.SMEM)

    def call(kernel, name, out, *arrays, scalars=(), scratch=()):
        return pl.pallas_call(
            kernel,
            in_specs=[smem] * len(scalars) + [vmem] * len(arrays),
            out_specs=jax.tree.map(lambda _: vmem, out),
            out_shape=out,
            scratch_shapes=scratch,
            name=name,
        )(*scalars, *in_vmem(*arrays))

    slab_rows = rows * channels // LANES
    count = groups // NEAR
    width = 2 * modes
    far = size // NEAR
    pack = 8 * count
    with_width = lambda kernel: functools.partial(kernel, width)

    sent = jnp.concatenate([a[rows - HALO :] for a in (outer_input, inner_input, value_input)], 0)
    halo = lax.ppermute(sent, "ctx", [(i, i + 1) for i in range(size - 1)])
    body, head = call(
        body_kernel,
        "body",
        [pltpu.VMEM((rows - HALO, channels), F32), pltpu.VMEM((2, HALO, channels), F32)],
        inner_input,
        value_input,
        feature_taps,
        scratch=[pltpu.VMEM((2, tiles, rows, LANES), F32)],
    )
    slabs = call(
        product_kernel,
        "product",
        pltpu.VMEM((slab_rows, LANES), BF16),
        halo,
        head,
        body,
        feature_taps,
        scratch=[pltpu.VMEM((2, tiles, 2 * HALO, LANES), F32)],
    )
    neighbours = [[NEAR * f + n for n in range(NEAR)] for f in range(far)]

    def exchange(x):
        slab = (NEAR, slab_rows // NEAR, LANES)
        y = lax.all_to_all(x.reshape(slab), "ctx", 0, 0, axis_index_groups=neighbours)
        return y.reshape(slab_rows, LANES)

    place = (lax.axis_index("ctx") % NEAR).reshape(1).astype(jnp.int32)
    table, step, jump = call(
        tables_kernel,
        "tables",
        [
            pltpu.VMEM((count, 7, LANES, LANES), BF16),
            pltpu.VMEM((pack, LANES), F32),
            pltpu.VMEM((pack, LANES), F32),
        ],
        decay_rates.T,
        residues.T,
        medium_taps.T,
        scalars=(place,),
    )
    outer_feat = call(
        outer_kernel,
        "outer",
        pltpu.VMEM((rows, channels), F32),
        halo,
        outer_input,
        feature_taps,
        scratch=[pltpu.VMEM((tiles, HALO + rows, LANES), F32)],
    )
    arrived = exchange(slabs)
    packet = pltpu.VMEM((3 * pack, LANES), BF16)
    states, end, packed = call(
        with_width(states_kernel),
        "states",
        [pltpu.VMEM((slab_rows, LANES), F32), pltpu.VMEM((pack, LANES), F32), packet],
        arrived,
        table,
        step,
    )
    local = call(
        with_width(local_kernel),
        "local",
        pltpu.VMEM((slab_rows, LANES), F32),
        arrived,
        table,
        states,
    )
    got = []
    for f in range(far - 1):
        if got:
            packed = call(with_width(chain_kernel), "chain", packet, got[-1], end, jump, packed)
        pairs = [(NEAR * f + n, NEAR * (f + 1) + n) for n in range(NEAR)]
        got.append(lax.ppermute(packed, "ctx", pairs))
    mixed = call(
        with_width(finish_kernel),
        "finish",
        pltpu.VMEM((slab_rows, LANES), BF16),
        local,
        *got,
        table,
        step,
    )
    hidden, sums = call(
        hidden_kernel,
        "hidden",
        [pltpu.VMEM((rows, channels), F32), pltpu.VMEM((8 * parts, LANES), F32)],
        exchange(mixed),
        outer_feat,
        residual,
    )
    all_sums = lax.all_to_all(sums.reshape(parts, 8, LANES), "tp", 0, 0)
    return call(
        norm_kernel,
        "norm",
        jax.ShapeDtypeStruct((rows, channels), BF16),
        hidden,
        all_sums.reshape(8 * parts, LANES),
        norm_gain.reshape(1, channels),
    )


def solution(mesh):
    return jax.shard_map(
        on_device,
        mesh=mesh,
        in_specs=(
            P("ctx", "tp"),
            P("ctx", "tp"),
            P("ctx", "tp"),
            P(None, None, "tp"),
            P(None, "tp"),
            P("tp", None),
            P("tp", None),
            P("ctx", "tp"),
            P("tp"),
        ),
        out_specs=P("ctx", "tp"),
        check_vma=False,
    )
```

```python
import functools

import jax
import jax.numpy as jnp
from jax import lax
from jax.experimental import pallas as pl
from jax.experimental.pallas import tpu as pltpu
from jax.sharding import PartitionSpec as P

D = 8192
F32 = jnp.float32
BF16 = jnp.bfloat16
LANES = 128
HALO = 8
NEAR = 16


def iota(shape, axis):
    return lax.broadcasted_iota(jnp.int32, shape, axis)


def in_vmem(*arrays):
    return [pltpu.with_memory_space_constraint(a, pltpu.VMEM) for a in arrays]


def split(x):
    high = x.astype(BF16)
    return high, (x - high.astype(F32)).astype(BF16)


def split_three(x, width):
    high, rest = split(x)
    middle, _ = split(x - high.astype(F32))
    low = x - high.astype(F32) - middle.astype(F32)
    copy = iota(x.shape, 1) // width
    part = jnp.where(copy == 0, high.astype(F32), jnp.where(copy == 1, middle.astype(F32), low))
    return jnp.where(copy < 3, part, 0.0).astype(BF16)


def join_three(parts, width):
    x = parts.astype(F32)
    x = x + pltpu.roll(x, width, 1)
    return x + pltpu.roll(x, 2 * width, 1)


def two_parts(x, width):
    high, low = split(x)
    copy = iota(x.shape, 1) // width
    return jnp.where(copy == 1, low.astype(F32), high.astype(F32)).astype(BF16)


def tables_kernel(place, decay_ref, residue_ref, medium_ref, table_ref, step_ref, jump_ref):
    modes, groups = decay_ref.shape
    square = (LANES, LANES)
    block = LANES // 2
    row, lane = iota(square, 0), iota(square, 1)
    same = row // block == lane // block
    pick = iota((modes, LANES), 0) == iota((modes, LANES), 1) % modes
    lag = iota((modes, LANES), 1).astype(F32)
    zero_row = jnp.zeros((1, LANES), F32)
    width = 2 * modes
    count = table_ref.shape[0]

    def along_lanes(x):
        return jnp.sum(jnp.where(pick, x, 0.0), 0, keepdims=True)

    def along_rows(x):
        return jnp.sum(jnp.where(row == lane, along_lanes(x), 0.0), 1, keepdims=True)

    def toeplitz(filter_row):
        wide = jnp.concatenate([filter_row, zero_row], 1)
        wide = jnp.broadcast_to(wide, (LANES, 2 * LANES))
        return pltpu.roll(wide, 0, 1, stride=1, stride_axis=0)

    for q in range(count):
        group = place[0] * count + q
        mine = iota((modes, groups), 1) == group
        rate = jnp.sum(jnp.where(mine, decay_ref[...], 0.0), 1, keepdims=True)
        weight = jnp.sum(jnp.where(mine, residue_ref[...], 0.0), 1, keepdims=True)
        weight = weight * jnp.sqrt(2.0 * rate / modes)
        long_row = jnp.sum(weight * jnp.exp(-rate * lag), 0, keepdims=True)
        chosen = iota(medium_ref.shape, 0) == group
        medium_row = jnp.sum(jnp.where(chosen, medium_ref[...].astype(F32), 0.0), 0, keepdims=True)
        medium_wide = toeplitz(medium_row)
        near = jnp.where(same, medium_wide[:, :LANES] + toeplitz(long_row)[:, :LANES], 0.0)
        table_ref[q, 0], table_ref[q, 1] = split(near)
        middle = [medium_wide[:, block:LANES], medium_wide[:, LANES : LANES + block]]
        table_ref[q, 2] = jnp.where(same, jnp.concatenate(middle, 1), 0.0).astype(BF16)
        table_ref[q, 3] = jnp.where(same, medium_wide[:, LANES:], 0.0).astype(BF16)
        rate_lanes, rate_rows, weight_rows = along_lanes(rate), along_rows(rate), along_rows(weight)
        to_end = jnp.exp(-rate_lanes * (block - 1 - row % block).astype(F32))
        kept = ((lane // modes) % 2 == row // block) & (lane < 3 * width)
        table_ref[q, 4], table_ref[q, 5] = split(jnp.where(kept, to_end, 0.0))
        from_start = weight_rows * jnp.exp(-rate_rows * (lane % block + 1).astype(F32))
        kept = ((row // modes) % 2 == lane // block) & (row < 3 * width)
        high, low = split(jnp.where(kept, from_start, 0.0))
        both = jnp.where(row < 2 * width, high.astype(F32), low.astype(F32))
        table_ref[q, 6] = both.astype(BF16)
        rows = slice(8 * q, 8 * q + 8)
        step_ref[rows] = jnp.broadcast_to(jnp.exp(-rate_lanes * block), (8, LANES))
        jump_ref[rows] = jnp.broadcast_to(jnp.exp(-rate_lanes * (block * NEAR)), (8, LANES))


def featurized(tap_ref, which, lanes, padded, rows):
    total = None
    for k in range(tap_ref.shape[1]):
        term = tap_ref[which, k : k + 1, lanes].astype(F32) * padded[HALO - k : HALO - k + rows, :]
        total = term if total is None else total + term
    return total


def tile_lanes(tile):
    return slice(tile * LANES, (tile + 1) * LANES)


def body_kernel(inner_ref, value_ref, tap_ref, out_ref, head_ref, padded):
    rows, channels = inner_ref.shape
    for tile in range(channels // LANES):
        lanes = tile_lanes(tile)
        feats = []
        for n, ref in enumerate((inner_ref, value_ref)):
            wide = ref[:, lanes].astype(F32)
            padded[n, tile] = wide
            head_ref[n, :, lanes] = wide[:HALO]
            feats.append(featurized(tap_ref, n + 1, lanes, padded.at[n, tile], rows - HALO))
        out_ref[:, lanes] = feats[0] * feats[1]


def product_kernel(halo_ref, head_ref, body_ref, tap_ref, out_ref, padded):
    channels = body_ref.shape[1]
    for tile in range(channels // LANES):
        lanes = tile_lanes(tile)
        feats = []
        for n in range(2):
            padded[n, tile, :HALO] = halo_ref[HALO * (n + 1) : HALO * (n + 2), lanes].astype(F32)
            padded[n, tile, HALO:] = head_ref[n, :, lanes]
            feats.append(featurized(tap_ref, n + 1, lanes, padded.at[n, tile], HALO))
        product = jnp.concatenate([feats[0] * feats[1], body_ref[:, lanes]], 0)
        product = product.astype(BF16).astype(F32)
        both = jnp.concatenate([product, pltpu.roll(product, LANES - 8, 1)], 0).T
        slabs = both.reshape(LANES // 16, 16, LANES)[:, :8].reshape(LANES // 2, LANES)
        out_ref[tile * (LANES // 2) : (tile + 1) * (LANES // 2)] = slabs.astype(BF16)


def outer_kernel(halo_ref, outer_ref, tap_ref, out_ref, padded):
    rows, channels = outer_ref.shape
    for tile in range(channels // LANES):
        lanes = tile_lanes(tile)
        padded[tile, :HALO] = halo_ref[:HALO, lanes].astype(F32)
        padded[tile, HALO:] = outer_ref[:, lanes].astype(F32)
        out_ref[:, lanes] = featurized(tap_ref, 0, lanes, padded.at[tile], rows)


def dot(a, b):
    return jnp.dot(a, b, preferred_element_type=F32)


def of_group(x, q, count):
    return x.reshape(x.shape[0] // (8 * count), count, 8, LANES)[:, q].reshape(-1, LANES)


def states_kernel(width, x_ref, table_ref, step_ref, state_ref, end_ref, send_ref):
    count = table_ref.shape[0]
    blocks = x_ref.shape[0] // (8 * count)
    wide = x_ref[...].astype(F32)
    ends = []
    for q in range(count):
        x = of_group(wide, q, count).astype(BF16)
        local = dot(x, table_ref[q, 4]) + dot(x, table_ref[q, 5])
        step = step_ref[8 * q : 8 * q + 8]
        carry = jnp.zeros((8, LANES), F32)
        for block in range(blocks):
            at = 8 * (count * block + q)
            state_ref[at : at + 8] = carry
            carry = carry * step + local[8 * block : 8 * block + 8]
        ends.append(carry)
    end = jnp.concatenate(ends, 0)
    end_ref[...] = end
    rows = 8 * count
    send_ref[:rows] = split_three(end, width)
    send_ref[rows:] = x_ref[(blocks - 2) * rows :]


def chain_kernel(width, got_ref, end_ref, jump_ref, send_ref, next_ref, state_ref):
    rows = end_ref.shape[0]
    end = end_ref[...] + jump_ref[...] * join_three(got_ref[:rows], width)
    state = split_three(end, width)
    state_ref[...] = state
    next_ref[:rows] = state
    next_ref[rows:] = send_ref[rows:]


def local_kernel(width, x_ref, table_ref, state_ref, out_ref):
    count = table_ref.shape[0]
    wide = x_ref[...].astype(F32)
    states = state_ref[...]
    zeros = jnp.zeros((8, LANES), F32)
    for q in range(count):
        x = of_group(wide, q, count)
        before = jnp.concatenate([zeros, x[:-8]], 0).astype(BF16)
        earlier = jnp.concatenate([zeros, zeros, x[:-16]], 0).astype(BF16)
        x = x.astype(BF16)
        mixed = dot(x, table_ref[q, 0]) + dot(x, table_ref[q, 1])
        mixed = mixed + dot(before, table_ref[q, 2]) + dot(earlier, table_ref[q, 3])
        mixed = mixed + dot(two_parts(of_group(states, q, count), width), table_ref[q, 6])
        for block in range(x.shape[0] // 8):
            at = 8 * (count * block + q)
            out_ref[at : at + 8] = mixed[8 * block : 8 * block + 8]


def finish_kernel(
    width, local_ref, got_01, got_23, got_12, got_13, table_ref, step_ref, jump_ref, out_ref
):
    count = table_ref.shape[0]
    rows = 8 * count
    blocks = local_ref.shape[0] // rows
    got = got_01[...].astype(F32) + got_23[...].astype(F32) + got_12[...].astype(F32)
    incoming = join_three(got[:rows], width) + jump_ref[...] * join_three(got_13[...], width)
    zeros = jnp.zeros((8, LANES), F32)
    parts = []
    for q in range(count):
        at = slice(8 * q, 8 * q + 8)
        step = step_ref[at]
        state = incoming[at]
        states = []
        for block in range(blocks):
            states.append(state)
            state = state * step
        mixed = dot(two_parts(jnp.concatenate(states, 0), width), table_ref[q, 6])
        last_but_one, last = got[rows:][at], got[2 * rows :][at]
        before = jnp.concatenate([last, zeros], 0).astype(BF16)
        earlier = jnp.concatenate([last_but_one, last], 0).astype(BF16)
        start = dot(before, table_ref[q, 2]) + dot(earlier, table_ref[q, 3])
        mixed = jnp.concatenate([mixed[:16] + start, mixed[16:]], 0)
        parts.append(mixed.reshape(blocks, 8, LANES))
    total = local_ref[...] + jnp.concatenate(parts, 1).reshape(local_ref.shape)
    out_ref[...] = total.astype(BF16)


def hidden_kernel(mixed_ref, outer_ref, residual_ref, hidden_ref, sum_ref):
    rows, channels = outer_ref.shape
    squares = jnp.zeros((rows, LANES), F32)
    for tile in range(channels // LANES):
        lanes = tile_lanes(tile)
        slabs = mixed_ref[tile * (LANES // 2) : (tile + 1) * (LANES // 2)].astype(F32)
        other = pltpu.roll(slabs, LANES // 2, 1)
        groups = LANES // 16
        both = jnp.concatenate([slabs.reshape(groups, 8, LANES), other.reshape(groups, 8, LANES)], 1)
        mixed = both.reshape(LANES, LANES).T[:rows]
        hidden = residual_ref[:, lanes].astype(F32) + outer_ref[:, lanes] * mixed
        hidden_ref[:, lanes] = hidden
        squares = squares + hidden * hidden
    tall = jnp.concatenate([squares, jnp.zeros_like(squares)], 0).T
    line = jnp.sum(tall, 0, keepdims=True)
    sum_ref[...] = jnp.broadcast_to(line, sum_ref.shape)


def norm_kernel(hidden_ref, sum_ref, gain_ref, out_ref):
    rows, channels = hidden_ref.shape
    parts = sum_ref[...].reshape(sum_ref.shape[0] // 8, 8, LANES)
    line = jnp.sum(parts, 0)
    scale = 1.0 / jnp.sqrt(line / D + 1e-05)
    tall = jnp.broadcast_to(scale[:1], (LANES, LANES)).T[:rows]
    for tile in range(channels // LANES):
        lanes = slice(tile * LANES, (tile + 1) * LANES)
        out_ref[:, lanes] = (hidden_ref[:, lanes] * gain_ref[:, lanes].astype(F32) * tall).astype(BF16)


def on_device(
    outer_input,
    inner_input,
    value_input,
    feature_taps,
    medium_taps,
    decay_rates,
    residues,
    residual,
    norm_gain,
):
    rows, channels = outer_input.shape
    groups, modes = decay_rates.shape
    size = lax.axis_size("ctx")
    parts = lax.axis_size("tp")
    tiles = channels // LANES
    vmem = pl.BlockSpec(memory_space=pltpu.VMEM)
    smem = pl.BlockSpec(memory_space=pltpu.SMEM)

    def call(kernel, name, out, *arrays, scalars=(), scratch=()):
        return pl.pallas_call(
            kernel,
            in_specs=[smem] * len(scalars) + [vmem] * len(arrays),
            out_specs=jax.tree.map(lambda _: vmem, out),
            out_shape=out,
            scratch_shapes=scratch,
            name=name,
        )(*scalars, *in_vmem(*arrays))

    slab_rows = rows * channels // LANES
    count = groups // NEAR
    width = 2 * modes
    far = size // NEAR
    assert far == 4
    pack = 8 * count
    with_width = lambda kernel: functools.partial(kernel, width)

    sent = jnp.concatenate([a[rows - HALO :] for a in (outer_input, inner_input, value_input)], 0)
    halo = lax.ppermute(sent, "ctx", [(i, i + 1) for i in range(size - 1)])
    body, head = call(
        body_kernel,
        "body",
        [pltpu.VMEM((rows - HALO, channels), F32), pltpu.VMEM((2, HALO, channels), F32)],
        inner_input,
        value_input,
        feature_taps,
        scratch=[pltpu.VMEM((2, tiles, rows, LANES), F32)],
    )
    slabs = call(
        product_kernel,
        "product",
        pltpu.VMEM((slab_rows, LANES), BF16),
        halo,
        head,
        body,
        feature_taps,
        scratch=[pltpu.VMEM((2, tiles, 2 * HALO, LANES), F32)],
    )
    neighbours = [[NEAR * f + n for n in range(NEAR)] for f in range(far)]

    def exchange(x):
        slab = (NEAR, slab_rows // NEAR, LANES)
        y = lax.all_to_all(x.reshape(slab), "ctx", 0, 0, axis_index_groups=neighbours)
        return y.reshape(slab_rows, LANES)

    place = (lax.axis_index("ctx") % NEAR).reshape(1).astype(jnp.int32)
    table, step, jump = call(
        tables_kernel,
        "tables",
        [
            pltpu.VMEM((count, 7, LANES, LANES), BF16),
            pltpu.VMEM((pack, LANES), F32),
            pltpu.VMEM((pack, LANES), F32),
        ],
        decay_rates.T,
        residues.T,
        medium_taps.T,
        scalars=(place,),
    )
    outer_feat = call(
        outer_kernel,
        "outer",
        pltpu.VMEM((rows, channels), F32),
        halo,
        outer_input,
        feature_taps,
        scratch=[pltpu.VMEM((tiles, HALO + rows, LANES), F32)],
    )
    arrived = exchange(slabs)
    packet = pltpu.VMEM((3 * pack, LANES), BF16)
    states, end, packed = call(
        with_width(states_kernel),
        "states",
        [pltpu.VMEM((slab_rows, LANES), F32), pltpu.VMEM((pack, LANES), F32), packet],
        arrived,
        table,
        step,
    )
    local = call(
        with_width(local_kernel),
        "local",
        pltpu.VMEM((slab_rows, LANES), F32),
        arrived,
        table,
        states,
    )
    def passed(x, start, end):
        pairs = [(NEAR * start + n, NEAR * end + n) for n in range(NEAR)]
        return lax.ppermute(x, "ctx", pairs)

    got_01 = passed(packed, 0, 1)
    got_23 = passed(packed, 2, 3)
    repacked, state = call(
        with_width(chain_kernel),
        "chain",
        [packet, pltpu.VMEM((pack, LANES), BF16)],
        got_01,
        end,
        jump,
        packed,
    )
    got_13 = passed(state, 1, 3)
    got_12 = passed(repacked, 1, 2)
    mixed = call(
        with_width(finish_kernel),
        "finish",
        pltpu.VMEM((slab_rows, LANES), BF16),
        local,
        got_01,
        got_23,
        got_12,
        got_13,
        table,
        step,
        jump,
    )
    hidden, sums = call(
        hidden_kernel,
        "hidden",
        [pltpu.VMEM((rows, channels), F32), pltpu.VMEM((8 * parts, LANES), F32)],
        exchange(mixed),
        outer_feat,
        residual,
    )
    all_sums = lax.all_to_all(sums.reshape(parts, 8, LANES), "tp", 0, 0)
    return call(
        norm_kernel,
        "norm",
        jax.ShapeDtypeStruct((rows, channels), BF16),
        hidden,
        all_sums.reshape(8 * parts, LANES),
        norm_gain.reshape(1, channels),
    )


def solution(mesh):
    return jax.shard_map(
        on_device,
        mesh=mesh,
        in_specs=(
            P("ctx", "tp"),
            P("ctx", "tp"),
            P("ctx", "tp"),
            P(None, None, "tp"),
            P(None, "tp"),
            P("tp", None),
            P("tp", None),
            P("ctx", "tp"),
            P("tp"),
        ),
        out_specs=P("ctx", "tp"),
        check_vma=False,
    )
```

```python
import functools

import jax
import jax.numpy as jnp
from jax import lax
from jax.experimental import pallas as pl
from jax.experimental.pallas import tpu as pltpu
from jax.sharding import PartitionSpec as P

D = 8192
F32 = jnp.float32
BF16 = jnp.bfloat16
LANES = 128
HALO = 8
FEAT = 7
EDGE = 16
NEAR = 16


def iota(shape, axis):
    return lax.broadcasted_iota(jnp.int32, shape, axis)


def in_vmem(*arrays):
    return [pltpu.with_memory_space_constraint(a, pltpu.VMEM) for a in arrays]


def dot(a, b):
    return jnp.dot(a, b, preferred_element_type=F32)


def split(x):
    high = x.astype(BF16)
    return high, (x - high.astype(F32)).astype(BF16)


def split_three(x, width):
    high, rest = split(x)
    middle, _ = split(x - high.astype(F32))
    low = x - high.astype(F32) - middle.astype(F32)
    copy = iota(x.shape, 1) // width
    part = jnp.where(copy == 0, high.astype(F32), jnp.where(copy == 1, middle.astype(F32), low))
    return jnp.where(copy < 3, part, 0.0).astype(BF16)


def join_three(parts, width):
    x = parts.astype(F32)
    x = x + pltpu.roll(x, width, 1)
    return x + pltpu.roll(x, 2 * width, 1)


def two_parts(x, width):
    high, low = split(x)
    copy = iota(x.shape, 1) // width
    return jnp.where(copy == 1, low.astype(F32), high.astype(F32)).astype(BF16)


def tables_kernel(
    place, decay_ref, residue_ref, medium_ref, tap_ref, table_ref, step_ref, jump_ref, rest_ref, mine_ref
):
    channels = tap_ref.shape[2]
    half = LANES // 2
    at, to = iota((channels, LANES), 0), iota((channels, LANES), 1)
    chosen = at == place[0] * half + to % half
    for_inner = jnp.where(chosen & (to < half), 1.0, 0.0).astype(BF16)
    for_value = jnp.where(chosen & (to >= half), 1.0, 0.0).astype(BF16)
    mine_ref[...] = dot(tap_ref[1], for_inner) + dot(tap_ref[2], for_value)
    modes, groups = decay_ref.shape
    square = (LANES, LANES)
    block = LANES // 2
    row, lane = iota(square, 0), iota(square, 1)
    same = row // block == lane // block
    pick = iota((modes, LANES), 0) == iota((modes, LANES), 1) % modes
    lag = iota((modes, LANES), 1).astype(F32)
    zero_row = jnp.zeros((1, LANES), F32)
    width = 2 * modes
    count = table_ref.shape[0]

    def along_lanes(x):
        return jnp.sum(jnp.where(pick, x, 0.0), 0, keepdims=True)

    def along_rows(x):
        return jnp.sum(jnp.where(row == lane, along_lanes(x), 0.0), 1, keepdims=True)

    def toeplitz(filter_row):
        wide = jnp.concatenate([filter_row, zero_row], 1)
        wide = jnp.broadcast_to(wide, (LANES, 2 * LANES))
        return pltpu.roll(wide, 0, 1, stride=1, stride_axis=0)

    for q in range(count):
        group = place[0] * count + q
        mine = iota((modes, groups), 1) == group
        rate = jnp.sum(jnp.where(mine, decay_ref[...], 0.0), 1, keepdims=True)
        weight = jnp.sum(jnp.where(mine, residue_ref[...], 0.0), 1, keepdims=True)
        weight = weight * jnp.sqrt(2.0 * rate / modes)
        long_row = jnp.sum(weight * jnp.exp(-rate * lag), 0, keepdims=True)
        chosen = iota(medium_ref.shape, 0) == group
        medium_row = jnp.sum(jnp.where(chosen, medium_ref[...].astype(F32), 0.0), 0, keepdims=True)
        medium_wide = toeplitz(medium_row)
        near = jnp.where(same, medium_wide[:, :LANES] + toeplitz(long_row)[:, :LANES], 0.0)
        table_ref[q, 0], table_ref[q, 1] = split(near)
        middle = [medium_wide[:, block:LANES], medium_wide[:, LANES : LANES + block]]
        table_ref[q, 2] = jnp.where(same, jnp.concatenate(middle, 1), 0.0).astype(BF16)
        table_ref[q, 3] = jnp.where(same, medium_wide[:, LANES:], 0.0).astype(BF16)
        rate_lanes, rate_rows, weight_rows = along_lanes(rate), along_rows(rate), along_rows(weight)
        to_end = jnp.exp(-rate_lanes * (block - 1 - row % block).astype(F32))
        kept = ((lane // modes) % 2 == row // block) & (lane < 3 * width)
        table_ref[q, 4], table_ref[q, 5] = split(jnp.where(kept, to_end, 0.0))
        from_start = weight_rows * jnp.exp(-rate_rows * (lane % block + 1).astype(F32))
        kept = ((row // modes) % 2 == lane // block) & (row < 3 * width)
        high, low = split(jnp.where(kept, from_start, 0.0))
        both = jnp.where(row < 2 * width, high.astype(F32), low.astype(F32))
        table_ref[q, 6] = both.astype(BF16)
        rows = slice(8 * q, 8 * q + 8)
        step_ref[rows] = jnp.broadcast_to(jnp.exp(-rate_lanes * block), (8, LANES))
        jump_ref[rows] = jnp.broadcast_to(jnp.exp(-rate_lanes * (block * NEAR)), (8, LANES))
        rest_ref[rows] = jnp.broadcast_to(jnp.exp(-rate_lanes * (block * (NEAR - 1))), (8, LANES))


def featurized(tap_ref, which, lanes, padded, rows):
    total = None
    for k in range(tap_ref.shape[1]):
        term = tap_ref[which, k : k + 1, lanes].astype(F32) * padded[HALO - k : HALO - k + rows, :]
        total = term if total is None else total + term
    return total


def tile_lanes(tile):
    return slice(tile * LANES, (tile + 1) * LANES)


def pack_kernel(inner_ref, value_ref, outer_ref, out_ref, tail_ref):
    tail_ref[...] = outer_ref[...]
    rows, channels = inner_ref.shape
    half = LANES // 2
    low = iota((rows, LANES), 1) < half
    for tile in range(channels // LANES):
        lanes = tile_lanes(tile)
        inner = inner_ref[:, lanes].astype(F32)
        value = value_ref[:, lanes].astype(F32)
        first = jnp.where(low, inner, pltpu.roll(value, half, 1))
        second = jnp.where(low, pltpu.roll(inner, half, 1), value)
        out_ref[2 * tile * rows : (2 * tile + 1) * rows] = first.astype(BF16)
        out_ref[(2 * tile + 1) * rows : (2 * tile + 2) * rows] = second.astype(BF16)


def outer_kernel(halo_ref, outer_ref, tap_ref, out_ref, padded):
    rows, channels = outer_ref.shape
    for tile in range(channels // LANES):
        lanes = tile_lanes(tile)
        padded[tile, :HALO] = halo_ref[:HALO, lanes].astype(F32)
        padded[tile, HALO:] = outer_ref[:, lanes].astype(F32)
        out_ref[:, lanes] = featurized(tap_ref, 0, lanes, padded.at[tile], rows)


def of_group(x, q, count):
    return x.reshape(x.shape[0] // (8 * count), count, 8, LANES)[:, q].reshape(-1, LANES)


def gated(tap_ref, padded, rows):
    total = None
    for k in range(FEAT):
        term = tap_ref[k : k + 1] * padded[HALO - k : HALO - k + rows]
        total = term if total is None else total + term
    return (total * pltpu.roll(total, LANES // 2, 1)).astype(BF16).astype(F32)


def slabs_of(product):
    both = jnp.concatenate([product, pltpu.roll(product, LANES - 8, 1)], 0).T
    return both.reshape(LANES // 16, 16, LANES)[:, :8].reshape(LANES // 2, LANES)


def missing(tap_ref, tail, head):
    block = LANES // 2
    product = gated(tap_ref, jnp.concatenate([tail[-HALO:], head[:HALO]], 0), HALO)
    kept = (iota(product.shape, 0) < FEAT - 1) & (iota(product.shape, 1) < block)
    product = jnp.where(kept, product, 0.0)
    return slabs_of(jnp.concatenate([product, jnp.zeros((block - HALO, LANES), F32)], 0))[: block // 2]


def to_states(table_ref, slab):
    count = table_ref.shape[0]
    parts = []
    for q in range(count):
        x = slab[8 * q : 8 * q + 8].astype(BF16)
        parts.append(dot(x, table_ref[q, 4]) + dot(x, table_ref[q, 5]))
    return jnp.concatenate(parts, 0)


def states_kernel(
    width, place, raw_ref, tap_ref, table_ref, step_ref, x_ref, state_ref, end_ref, send_ref, padded
):
    count = table_ref.shape[0]
    block = LANES // 2
    blocks = raw_ref.shape[0] // block
    padded[:HALO] = jnp.zeros((HALO, LANES), F32)
    padded[HALO:] = raw_ref[...].astype(F32)
    low = iota((block, LANES), 1) < block
    early = (iota((block, LANES), 0) < FEAT - 1) & (place[1] > 0)
    rows = 8 * count
    slabs = []
    for pair in range(blocks // 2):
        products = []
        for b in (2 * pair, 2 * pair + 1):
            product = gated(tap_ref, padded.at[b * block : (b + 1) * block + HALO], block)
            products.append(jnp.where(early, 0.0, product) if b == 0 else product)
        slabs.append(slabs_of(jnp.where(low, products[0], products[1])))
    wide = jnp.concatenate(slabs, 0)
    x_ref[...] = wide.astype(BF16)
    ends = []
    for q in range(count):
        x = of_group(wide, q, count).astype(BF16)
        local = dot(x, table_ref[q, 4]) + dot(x, table_ref[q, 5])
        step = step_ref[8 * q : 8 * q + 8]
        carry = jnp.zeros((8, LANES), F32)
        for b in range(blocks):
            at = rows * b + 8 * q
            state_ref[at : at + 8] = carry
            carry = carry * step + local[8 * b : 8 * b + 8]
        ends.append(carry)
    end = jnp.concatenate(ends, 0)
    end_ref[...] = end
    send_ref[:rows] = split_three(end, width)
    send_ref[rows : 3 * rows] = wide[(blocks - 2) * rows :].astype(BF16)
    send_ref[3 * rows : 3 * rows + EDGE] = raw_ref[blocks * block - EDGE :]
    send_ref[3 * rows + EDGE :] = raw_ref[:EDGE]


def chain_kernel(
    width, got_ref, raw_ref, tap_ref, table_ref, end_ref, jump_ref, rest_ref, send_ref, next_ref, short_ref
):
    rows = end_ref.shape[0]
    tail = got_ref[3 * rows : 3 * rows + EDGE].astype(F32)
    slab = missing(tap_ref, tail, raw_ref[:EDGE].astype(F32))
    end = end_ref[...] + rest_ref[...] * to_states(table_ref, slab)
    end = end + jump_ref[...] * join_three(got_ref[:rows], width)
    state = split_three(end, width)
    short_ref[:rows] = state
    short_ref[rows:] = send_ref[3 * rows : 3 * rows + EDGE]
    next_ref[:rows] = state
    next_ref[rows:] = send_ref[rows:]


def local_kernel(width, x_ref, table_ref, state_ref, out_ref):
    count = table_ref.shape[0]
    wide = x_ref[...].astype(F32)
    states = state_ref[...]
    zeros = jnp.zeros((8, LANES), F32)
    for q in range(count):
        x = of_group(wide, q, count)
        before = jnp.concatenate([zeros, x[:-8]], 0).astype(BF16)
        earlier = jnp.concatenate([zeros, zeros, x[:-16]], 0).astype(BF16)
        x = x.astype(BF16)
        mixed = dot(x, table_ref[q, 0]) + dot(x, table_ref[q, 1])
        mixed = mixed + dot(before, table_ref[q, 2]) + dot(earlier, table_ref[q, 3])
        mixed = mixed + dot(two_parts(of_group(states, q, count), width), table_ref[q, 6])
        for block in range(x.shape[0] // 8):
            at = 8 * (count * block + q)
            out_ref[at : at + 8] = mixed[8 * block : 8 * block + 8]


def finish_kernel(
    width,
    place,
    local_ref,
    got_01,
    got_23,
    got_12,
    got_13,
    raw_ref,
    tap_ref,
    table_ref,
    step_ref,
    jump_ref,
    rest_ref,
    out_ref,
):
    count = table_ref.shape[0]
    rows = 8 * count
    blocks = local_ref.shape[0] // rows
    got = got_01[...].astype(F32) + got_23[...].astype(F32) + got_12[...].astype(F32)
    edge = slice(3 * rows, 3 * rows + EDGE)
    far_tail = got_13[rows:].astype(F32)
    far_slab = missing(tap_ref, far_tail, got_23[3 * rows + EDGE :].astype(F32))
    own_slab = missing(tap_ref, got[edge], raw_ref[:EDGE].astype(F32))
    own_slab = jnp.where(place[1] > 0, own_slab, 0.0)
    incoming = join_three(got[:rows], width) + rest_ref[...] * to_states(table_ref, far_slab)
    incoming = incoming + jump_ref[...] * join_three(got_13[:rows], width)
    added = to_states(table_ref, own_slab)
    zeros = jnp.zeros((8, LANES), F32)
    parts = []
    for q in range(count):
        at = slice(8 * q, 8 * q + 8)
        step = step_ref[at]
        state = incoming[at]
        states = []
        for block in range(blocks):
            states.append(state)
            state = state * step
            if block == 0:
                state = state + added[at]
        mixed = dot(two_parts(jnp.concatenate(states, 0), width), table_ref[q, 6])
        last_but_one, last, first = got[rows:][at], got[2 * rows :][at], own_slab[at]
        now = jnp.concatenate([first, zeros, zeros, zeros], 0).astype(BF16)
        before = jnp.concatenate([last, first, zeros, zeros], 0).astype(BF16)
        earlier = jnp.concatenate([last_but_one, last, first, zeros], 0).astype(BF16)
        start = dot(now, table_ref[q, 0]) + dot(now, table_ref[q, 1])
        start = start + dot(before, table_ref[q, 2]) + dot(earlier, table_ref[q, 3])
        mixed = jnp.concatenate([mixed[:32] + start, mixed[32:]], 0)
        parts.append(mixed.reshape(blocks, 8, LANES))
    total = local_ref[...] + jnp.concatenate(parts, 1).reshape(local_ref.shape)
    out_ref[...] = total.astype(BF16)


def hidden_kernel(mixed_ref, outer_ref, residual_ref, hidden_ref, sum_ref):
    rows, channels = outer_ref.shape
    squares = jnp.zeros((rows, LANES), F32)
    for tile in range(channels // LANES):
        lanes = tile_lanes(tile)
        slabs = mixed_ref[tile * (LANES // 2) : (tile + 1) * (LANES // 2)].astype(F32)
        other = pltpu.roll(slabs, LANES // 2, 1)
        groups = LANES // 16
        both = jnp.concatenate([slabs.reshape(groups, 8, LANES), other.reshape(groups, 8, LANES)], 1)
        mixed = both.reshape(LANES, LANES).T[:rows]
        hidden = residual_ref[:, lanes].astype(F32) + outer_ref[:, lanes] * mixed
        hidden_ref[:, lanes] = hidden
        squares = squares + hidden * hidden
    tall = jnp.concatenate([squares, jnp.zeros_like(squares)], 0).T
    line = jnp.sum(tall, 0, keepdims=True)
    sum_ref[...] = jnp.broadcast_to(line, sum_ref.shape)


def norm_kernel(hidden_ref, sum_ref, gain_ref, out_ref):
    rows, channels = hidden_ref.shape
    parts = sum_ref[...].reshape(sum_ref.shape[0] // 8, 8, LANES)
    line = jnp.sum(parts, 0)
    scale = 1.0 / jnp.sqrt(line / D + 1e-05)
    tall = jnp.broadcast_to(scale[:1], (LANES, LANES)).T[:rows]
    for tile in range(channels // LANES):
        lanes = slice(tile * LANES, (tile + 1) * LANES)
        out_ref[:, lanes] = (hidden_ref[:, lanes] * gain_ref[:, lanes].astype(F32) * tall).astype(BF16)


def on_device(
    outer_input,
    inner_input,
    value_input,
    feature_taps,
    medium_taps,
    decay_rates,
    residues,
    residual,
    norm_gain,
):
    rows, channels = outer_input.shape
    groups, modes = decay_rates.shape
    size = lax.axis_size("ctx")
    parts = lax.axis_size("tp")
    tiles = channels // LANES
    vmem = pl.BlockSpec(memory_space=pltpu.VMEM)
    smem = pl.BlockSpec(memory_space=pltpu.SMEM)

    def call(kernel, name, out, *arrays, scalars=(), scratch=()):
        return pl.pallas_call(
            kernel,
            in_specs=[smem] * len(scalars) + [vmem] * len(arrays),
            out_specs=jax.tree.map(lambda _: vmem, out),
            out_shape=out,
            scratch_shapes=scratch,
            name=name,
        )(*scalars, *in_vmem(*arrays))

    slab_rows = rows * channels // LANES
    count = groups // NEAR
    width = 2 * modes
    far = size // NEAR
    assert far == 4
    pack = 8 * count
    with_width = lambda kernel: functools.partial(kernel, width)

    raw, outer_tail = pl.pallas_call(
        pack_kernel,
        grid=(1,),
        in_specs=[
            pl.BlockSpec((rows, channels), lambda i: (0, 0)),
            pl.BlockSpec((rows, channels), lambda i: (0, 0)),
            pl.BlockSpec((HALO, channels), lambda i: (rows // HALO - 1, 0)),
        ],
        out_shape=[pltpu.VMEM((NEAR * rows, LANES), BF16), pltpu.VMEM((HALO, channels), BF16)],
        out_specs=[vmem, vmem],
        name="pack",
    )(inner_input, value_input, outer_input)
    neighbours = [[NEAR * f + n for n in range(NEAR)] for f in range(far)]

    def exchange(x):
        slab = (NEAR, x.shape[0] // NEAR, LANES)
        y = lax.all_to_all(x.reshape(slab), "ctx", 0, 0, axis_index_groups=neighbours)
        return y.reshape(x.shape)

    arrived = exchange(raw)
    halo = lax.ppermute(outer_tail, "ctx", [(i, i + 1) for i in range(size - 1)])
    arrived, halo = lax.optimization_barrier((arrived, halo))
    index = lax.axis_index("ctx")
    place = jnp.stack([index % NEAR, index // NEAR]).astype(jnp.int32)
    table, step, jump, rest, taps = call(
        tables_kernel,
        "tables",
        [
            pltpu.VMEM((count, 7, LANES, LANES), BF16),
            pltpu.VMEM((pack, LANES), F32),
            pltpu.VMEM((pack, LANES), F32),
            pltpu.VMEM((pack, LANES), F32),
            pltpu.VMEM((FEAT, LANES), F32),
        ],
        decay_rates.T,
        residues.T,
        medium_taps.T,
        feature_taps,
        scalars=(place,),
    )
    outer_feat = call(
        outer_kernel,
        "outer",
        pltpu.VMEM((rows, channels), F32),
        halo,
        outer_input,
        feature_taps,
        scratch=[pltpu.VMEM((tiles, HALO + rows, LANES), F32)],
    )
    packet = pltpu.VMEM((3 * pack + 2 * EDGE, LANES), BF16)
    x, states, end, packed = call(
        with_width(states_kernel),
        "states",
        [
            pltpu.VMEM((slab_rows, LANES), BF16),
            pltpu.VMEM((slab_rows, LANES), F32),
            pltpu.VMEM((pack, LANES), F32),
            packet,
        ],
        arrived,
        taps,
        table,
        step,
        scalars=(place,),
        scratch=[pltpu.VMEM((HALO + NEAR * rows, LANES), F32)],
    )
    local = call(
        with_width(local_kernel),
        "local",
        pltpu.VMEM((slab_rows, LANES), F32),
        x,
        table,
        states,
    )

    def passed(x, start, end):
        pairs = [(NEAR * start + n, NEAR * end + n) for n in range(NEAR)]
        return lax.ppermute(x, "ctx", pairs)

    got_01 = passed(packed, 0, 1)
    got_23 = passed(packed, 2, 3)
    repacked, state = call(
        with_width(chain_kernel),
        "chain",
        [packet, pltpu.VMEM((pack + EDGE, LANES), BF16)],
        got_01,
        arrived,
        taps,
        table,
        end,
        jump,
        rest,
        packed,
    )
    got_13 = passed(state, 1, 3)
    got_12 = passed(repacked, 1, 2)
    mixed = call(
        with_width(finish_kernel),
        "finish",
        pltpu.VMEM((slab_rows, LANES), BF16),
        local,
        got_01,
        got_23,
        got_12,
        got_13,
        arrived,
        taps,
        table,
        step,
        jump,
        rest,
        scalars=(place,),
    )
    hidden, sums = call(
        hidden_kernel,
        "hidden",
        [pltpu.VMEM((rows, channels), F32), pltpu.VMEM((8 * parts, LANES), F32)],
        exchange(mixed),
        outer_feat,
        residual,
    )
    all_sums = lax.all_to_all(sums.reshape(parts, 8, LANES), "tp", 0, 0)
    return call(
        norm_kernel,
        "norm",
        jax.ShapeDtypeStruct((rows, channels), BF16),
        hidden,
        all_sums.reshape(8 * parts, LANES),
        norm_gain.reshape(1, channels),
    )


def solution(mesh):
    return jax.shard_map(
        on_device,
        mesh=mesh,
        in_specs=(
            P("ctx", "tp"),
            P("ctx", "tp"),
            P("ctx", "tp"),
            P(None, None, "tp"),
            P(None, "tp"),
            P("tp", None),
            P("tp", None),
            P("ctx", "tp"),
            P("tp"),
        ),
        out_specs=P("ctx", "tp"),
        check_vma=False,
    )
```

```python
import functools

import jax
import jax.numpy as jnp
from jax import lax
from jax.experimental import pallas as pl
from jax.experimental.pallas import tpu as pltpu
from jax.sharding import PartitionSpec as P


D = 8192
F32 = jnp.float32
BF16 = jnp.bfloat16
LANES = 128
HALO = 8
FEAT = 7
EDGE = 16
NEAR = 16


def iota(shape, axis):
    return lax.broadcasted_iota(jnp.int32, shape, axis)


def in_vmem(*arrays):
    return [pltpu.with_memory_space_constraint(a, pltpu.VMEM) for a in arrays]


def dot(a, b):
    return jnp.dot(a, b, preferred_element_type=F32)


def split(x):
    high = x.astype(BF16)
    return high, (x - high.astype(F32)).astype(BF16)


def split_three(x, width):
    high, _ = split(x)
    middle, _ = split(x - high.astype(F32))
    low = x - high.astype(F32) - middle.astype(F32)
    copy = iota(x.shape, 1) // width
    part = jnp.where(copy == 0, high.astype(F32), jnp.where(copy == 1, middle.astype(F32), low))
    return jnp.where(copy < 3, part, 0.0).astype(BF16)


def join_three(parts, width):
    x = parts.astype(F32)
    x = x + pltpu.roll(x, width, 1)
    return x + pltpu.roll(x, 2 * width, 1)


def two_parts(x, width):
    high, low = split(x)
    copy = iota(x.shape, 1) // width
    return jnp.where(copy == 1, low.astype(F32), high.astype(F32)).astype(BF16)


def tables_kernel(
    place, decay_ref, residue_ref, medium_ref, tap_ref, table_ref, step_ref, jump_ref, rest_ref, mine_ref
):
    channels = tap_ref.shape[2]
    half = LANES // 2
    at, to = iota((channels, LANES), 0), iota((channels, LANES), 1)
    position = lax.rem(place[0], NEAR)
    chosen = at == position * half + to % half
    for_inner = jnp.where(chosen & (to < half), 1.0, 0.0).astype(BF16)
    for_value = jnp.where(chosen & (to >= half), 1.0, 0.0).astype(BF16)
    mine_ref[...] = dot(tap_ref[1], for_inner) + dot(tap_ref[2], for_value)
    modes, groups = decay_ref.shape
    square = (LANES, LANES)
    block = LANES // 2
    row, lane = iota(square, 0), iota(square, 1)
    same = row // block == lane // block
    pick = iota((modes, LANES), 0) == iota((modes, LANES), 1) % modes
    lag = iota((modes, LANES), 1).astype(F32)
    zero_row = jnp.zeros((1, LANES), F32)
    width = 2 * modes
    count = table_ref.shape[0]

    def along_lanes(x):
        return jnp.sum(jnp.where(pick, x, 0.0), 0, keepdims=True)

    def along_rows(x):
        return jnp.sum(jnp.where(row == lane, along_lanes(x), 0.0), 1, keepdims=True)

    def toeplitz(filter_row):
        wide = jnp.concatenate([filter_row, zero_row], 1)
        wide = jnp.broadcast_to(wide, (LANES, 2 * LANES))
        return pltpu.roll(wide, 0, 1, stride=1, stride_axis=0)

    for q in range(count):
        group = position * count + q
        mine = iota((modes, groups), 1) == group
        rate = jnp.sum(jnp.where(mine, decay_ref[...], 0.0), 1, keepdims=True)
        weight = jnp.sum(jnp.where(mine, residue_ref[...], 0.0), 1, keepdims=True)
        weight = weight * jnp.sqrt(2.0 * rate / modes)
        long_row = jnp.sum(weight * jnp.exp(-rate * lag), 0, keepdims=True)
        chosen = iota(medium_ref.shape, 0) == group
        medium_row = jnp.sum(jnp.where(chosen, medium_ref[...].astype(F32), 0.0), 0, keepdims=True)
        medium_wide = toeplitz(medium_row)
        near = jnp.where(same, medium_wide[:, :LANES] + toeplitz(long_row)[:, :LANES], 0.0)
        table_ref[q, 0], table_ref[q, 1] = split(near)
        middle = [medium_wide[:, block:LANES], medium_wide[:, LANES : LANES + block]]
        table_ref[q, 2] = jnp.where(same, jnp.concatenate(middle, 1), 0.0).astype(BF16)
        table_ref[q, 3] = jnp.where(same, medium_wide[:, LANES:], 0.0).astype(BF16)
        rate_lanes, rate_rows, weight_rows = along_lanes(rate), along_rows(rate), along_rows(weight)
        to_end = jnp.exp(-rate_lanes * (block - 1 - row % block).astype(F32))
        kept = ((lane // modes) % 2 == row // block) & (lane < 3 * width)
        table_ref[q, 4], table_ref[q, 5] = split(jnp.where(kept, to_end, 0.0))
        from_start = weight_rows * jnp.exp(-rate_rows * (lane % block + 1).astype(F32))
        kept = ((row // modes) % 2 == lane // block) & (row < 3 * width)
        high, low = split(jnp.where(kept, from_start, 0.0))
        both = jnp.where(row < 2 * width, high.astype(F32), low.astype(F32))
        table_ref[q, 6] = both.astype(BF16)
        rows = slice(8 * q, 8 * q + 8)
        step_ref[rows] = jnp.broadcast_to(jnp.exp(-rate_lanes * block), (8, LANES))
        jump_ref[rows] = jnp.broadcast_to(jnp.exp(-rate_lanes * (block * NEAR)), (8, LANES))
        rest_ref[rows] = jnp.broadcast_to(jnp.exp(-rate_lanes * (block * (NEAR - 1))), (8, LANES))


def featurized(tap_ref, which, lanes, padded, rows):
    total = None
    for k in range(tap_ref.shape[1]):
        term = tap_ref[which, k : k + 1, lanes].astype(F32) * padded[HALO - k : HALO - k + rows, :]
        total = term if total is None else total + term
    return total


def tile_lanes(tile):
    return slice(tile * LANES, (tile + 1) * LANES)


def pack_kernel(inner_ref, value_ref, outer_ref, out_ref, tail_ref):
    tail_ref[...] = outer_ref[...]
    rows, channels = inner_ref.shape
    half = LANES // 2
    low = iota((rows, LANES), 1) < half
    for tile in range(channels // LANES):
        lanes = tile_lanes(tile)
        inner = inner_ref[:, lanes].astype(F32)
        value = value_ref[:, lanes].astype(F32)
        first = jnp.where(low, inner, pltpu.roll(value, half, 1))
        second = jnp.where(low, pltpu.roll(inner, half, 1), value)
        out_ref[2 * tile * rows : (2 * tile + 1) * rows] = first.astype(BF16)
        out_ref[(2 * tile + 1) * rows : (2 * tile + 2) * rows] = second.astype(BF16)


def outer_kernel(halo_ref, outer_ref, tap_ref, out_ref, padded):
    rows, channels = outer_ref.shape
    for tile in range(channels // LANES):
        lanes = tile_lanes(tile)
        padded[tile, :HALO] = halo_ref[:HALO, lanes].astype(F32)
        padded[tile, HALO:] = outer_ref[:, lanes].astype(F32)
        out_ref[:, lanes] = featurized(tap_ref, 0, lanes, padded.at[tile], rows)


def of_group(x, q, count):
    return x.reshape(x.shape[0] // (8 * count), count, 8, LANES)[:, q].reshape(-1, LANES)


def gated(tap_ref, padded, rows):
    total = None
    for k in range(FEAT):
        term = tap_ref[k : k + 1] * padded[HALO - k : HALO - k + rows]
        total = term if total is None else total + term
    return (total * pltpu.roll(total, LANES // 2, 1)).astype(BF16).astype(F32)


def slabs_of(product):
    both = jnp.concatenate([product, pltpu.roll(product, LANES - 8, 1)], 0).T
    return both.reshape(LANES // 16, 16, LANES)[:, :8].reshape(LANES // 2, LANES)


def missing(tap_ref, tail, head):
    block = LANES // 2
    product = gated(tap_ref, jnp.concatenate([tail[-HALO:], head[:HALO]], 0), HALO)
    kept = (iota(product.shape, 0) < FEAT - 1) & (iota(product.shape, 1) < block)
    product = jnp.where(kept, product, 0.0)
    return slabs_of(jnp.concatenate([product, jnp.zeros((block - HALO, LANES), F32)], 0))[: block // 2]


def to_states(table_ref, slab):
    count = table_ref.shape[0]
    parts = []
    for q in range(count):
        x = slab[8 * q : 8 * q + 8].astype(BF16)
        parts.append(dot(x, table_ref[q, 4]) + dot(x, table_ref[q, 5]))
    return jnp.concatenate(parts, 0)


def find_states(
    width, later, raw_ref, tap_ref, table_ref, step_ref, x_ref, state_ref, end_ref, send_ref, padded
):
    count = table_ref.shape[0]
    block = LANES // 2
    blocks = raw_ref.shape[0] // block
    padded[:HALO] = jnp.zeros((HALO, LANES), F32)
    padded[HALO:] = raw_ref[...].astype(F32)
    low = iota((block, LANES), 1) < block
    early = (iota((block, LANES), 0) < FEAT - 1)
    rows = 8 * count
    slabs = []
    for pair in range(blocks // 2):
        products = []
        for b in (2 * pair, 2 * pair + 1):
            product = gated(tap_ref, padded.at[b * block : (b + 1) * block + HALO], block)
            products.append(jnp.where(early, 0.0, product) if later and b == 0 else product)
        slabs.append(slabs_of(jnp.where(low, products[0], products[1])))
    wide = jnp.concatenate(slabs, 0)
    x_ref[...] = wide.astype(BF16)
    ends = []
    for q in range(count):
        x = of_group(wide, q, count).astype(BF16)
        local = dot(x, table_ref[q, 4]) + dot(x, table_ref[q, 5])
        step = step_ref[8 * q : 8 * q + 8]
        carry = jnp.zeros((8, LANES), F32)
        for b in range(blocks):
            at = rows * b + 8 * q
            state_ref[at : at + 8] = carry
            carry = carry * step + local[8 * b : 8 * b + 8]
        ends.append(carry)
    end = jnp.concatenate(ends, 0)
    end_ref[...] = end
    send_ref[:rows] = split_three(end, width)
    send_ref[rows : 3 * rows] = wide[(blocks - 2) * rows :].astype(BF16)
    send_ref[3 * rows : 3 * rows + EDGE] = raw_ref[blocks * block - EDGE :]
    send_ref[3 * rows + EDGE :] = raw_ref[:EDGE]


def super_block(place):
    return lax.div(place[0], NEAR)


def first_states_kernel(width, place, *refs):
    @pl.when(super_block(place) == 0)
    def _():
        find_states(width, False, *refs)


def later_states_kernel(width, place, raw_ref, tap_ref, table_ref, step_ref, x_in, state_in, *refs):
    @pl.when(super_block(place) > 0)
    def _():
        find_states(width, True, raw_ref, tap_ref, table_ref, step_ref, *refs)


def chain_kernel(
    width,
    place,
    got_ref,
    raw_ref,
    tap_ref,
    table_ref,
    end_ref,
    jump_ref,
    rest_ref,
    send_ref,
    short_ref,
    next_ref,
):
    rows = end_ref.shape[0]

    @pl.when(super_block(place) == 1)
    def _():
        tail = got_ref[3 * rows : 3 * rows + EDGE].astype(F32)
        slab = missing(tap_ref, tail, raw_ref[:EDGE].astype(F32))
        end = end_ref[...] + rest_ref[...] * to_states(table_ref, slab)
        end = end + jump_ref[...] * join_three(got_ref[:rows], width)
        state = split_three(end, width)
        short_ref[:rows] = state
        short_ref[rows:] = send_ref[3 * rows : 3 * rows + EDGE]
        next_ref[:rows] = state
        next_ref[rows:] = send_ref[rows:]


def local_kernel(width, x_ref, table_ref, state_ref, out_ref):
    count = table_ref.shape[0]
    wide = x_ref[...].astype(F32)
    states = state_ref[...]
    zeros = jnp.zeros((8, LANES), F32)
    for q in range(count):
        x = of_group(wide, q, count)
        before = jnp.concatenate([zeros, x[:-8]], 0).astype(BF16)
        earlier = jnp.concatenate([zeros, zeros, x[:-16]], 0).astype(BF16)
        x = x.astype(BF16)
        mixed = dot(x, table_ref[q, 0]) + dot(x, table_ref[q, 1])
        mixed = mixed + dot(before, table_ref[q, 2]) + dot(earlier, table_ref[q, 3])
        mixed = mixed + dot(two_parts(of_group(states, q, count), width), table_ref[q, 6])
        for block in range(x.shape[0] // 8):
            at = 8 * (count * block + q)
            out_ref[at : at + 8] = mixed[8 * block : 8 * block + 8]


def finish_kernel(
    width,
    place,
    local_ref,
    got_01,
    got_23,
    got_12,
    got_13,
    raw_ref,
    tap_ref,
    table_ref,
    step_ref,
    jump_ref,
    rest_ref,
    out_ref,
    incoming_ref,
):
    here = super_block(place)

    @pl.when(here == 0)
    def _():
        out_ref[...] = local_ref[...].astype(BF16)

    @pl.when(here > 0)
    def _():
        count = table_ref.shape[0]
        rows = 8 * count
        blocks = local_ref.shape[0] // rows
        got = got_01[...].astype(F32) + got_23[...].astype(F32) + got_12[...].astype(F32)
        edge = slice(3 * rows, 3 * rows + EDGE)
        own_slab = missing(tap_ref, got[edge], raw_ref[:EDGE].astype(F32))
        incoming_ref[...] = join_three(got[:rows], width)

        @pl.when(here == 3)
        def _():
            far_tail = got_13[rows:].astype(F32)
            far_slab = missing(tap_ref, far_tail, got_23[3 * rows + EDGE :].astype(F32))
            more = rest_ref[...] * to_states(table_ref, far_slab)
            incoming_ref[...] += more + jump_ref[...] * join_three(got_13[:rows], width)

        incoming = incoming_ref[...]
        added = to_states(table_ref, own_slab)
        zeros = jnp.zeros((8, LANES), F32)
        parts = []
        for q in range(count):
            at = slice(8 * q, 8 * q + 8)
            step = step_ref[at]
            state = incoming[at]
            states = []
            for block in range(blocks):
                states.append(state)
                state = state * step
                if block == 0:
                    state = state + added[at]
            mixed = dot(two_parts(jnp.concatenate(states, 0), width), table_ref[q, 6])
            last_but_one, last, first = got[rows:][at], got[2 * rows :][at], own_slab[at]
            now = jnp.concatenate([first, zeros, zeros, zeros], 0).astype(BF16)
            before = jnp.concatenate([last, first, zeros, zeros], 0).astype(BF16)
            earlier = jnp.concatenate([last_but_one, last, first, zeros], 0).astype(BF16)
            start = dot(now, table_ref[q, 0]) + dot(now, table_ref[q, 1])
            start = start + dot(before, table_ref[q, 2]) + dot(earlier, table_ref[q, 3])
            mixed = jnp.concatenate([mixed[:32] + start, mixed[32:]], 0)
            parts.append(mixed.reshape(blocks, 8, LANES))
        total = local_ref[...] + jnp.concatenate(parts, 1).reshape(local_ref.shape)
        out_ref[...] = total.astype(BF16)


def hidden_kernel(mixed_ref, outer_ref, residual_ref, hidden_ref, sum_ref):
    rows, channels = outer_ref.shape
    squares = jnp.zeros((rows, LANES), F32)
    for tile in range(channels // LANES):
        lanes = tile_lanes(tile)
        slabs = mixed_ref[tile * (LANES // 2) : (tile + 1) * (LANES // 2)].astype(F32)
        other = pltpu.roll(slabs, LANES // 2, 1)
        groups = LANES // 16
        both = jnp.concatenate([slabs.reshape(groups, 8, LANES), other.reshape(groups, 8, LANES)], 1)
        mixed = both.reshape(LANES, LANES).T[:rows]
        hidden = residual_ref[:, lanes].astype(F32) + outer_ref[:, lanes] * mixed
        hidden_ref[:, lanes] = hidden
        squares = squares + hidden * hidden
    tall = jnp.concatenate([squares, jnp.zeros_like(squares)], 0).T
    line = jnp.sum(tall, 0, keepdims=True)
    sum_ref[...] = jnp.broadcast_to(line, sum_ref.shape)


def norm_kernel(hidden_ref, sum_ref, gain_ref, out_ref):
    rows, channels = hidden_ref.shape
    parts = sum_ref[...].reshape(sum_ref.shape[0] // 8, 8, LANES)
    line = jnp.sum(parts, 0)
    scale = 1.0 / jnp.sqrt(line / D + 1e-05)
    tall = jnp.broadcast_to(scale[:1], (LANES, LANES)).T[:rows]
    for tile in range(channels // LANES):
        lanes = slice(tile * LANES, (tile + 1) * LANES)
        out_ref[:, lanes] = (hidden_ref[:, lanes] * gain_ref[:, lanes].astype(F32) * tall).astype(BF16)


def on_device(
    outer_input,
    inner_input,
    value_input,
    feature_taps,
    medium_taps,
    decay_rates,
    residues,
    residual,
    norm_gain,
):
    rows, channels = outer_input.shape
    groups, modes = decay_rates.shape
    size = lax.axis_size("ctx")
    parts = lax.axis_size("tp")
    tiles = channels // LANES
    vmem = pl.BlockSpec(memory_space=pltpu.VMEM)
    smem = pl.BlockSpec(memory_space=pltpu.SMEM)

    def call(kernel, out, *arrays, scalars=(), scratch=(), aliases={}):
        return pl.pallas_call(
            kernel,
            in_specs=[smem] * len(scalars) + [vmem] * len(arrays),
            out_specs=jax.tree.map(lambda _: vmem, out),
            out_shape=out,
            scratch_shapes=scratch,
            input_output_aliases=aliases,
        )(*scalars, *in_vmem(*arrays))

    slab_rows = rows * channels // LANES
    count = groups // NEAR
    width = 2 * modes
    far = size // NEAR
    assert far == 4
    pack = 8 * count
    with_width = lambda kernel: functools.partial(kernel, width)

    raw, outer_tail = pl.pallas_call(
        pack_kernel,
        grid=(1,),
        in_specs=[
            pl.BlockSpec((rows, channels), lambda i: (0, 0)),
            pl.BlockSpec((rows, channels), lambda i: (0, 0)),
            pl.BlockSpec((HALO, channels), lambda i: (rows // HALO - 1, 0)),
        ],
        out_shape=[pltpu.VMEM((NEAR * rows, LANES), BF16), pltpu.VMEM((HALO, channels), BF16)],
        out_specs=[vmem, vmem],
        name="pack",
    )(inner_input, value_input, outer_input)
    neighbours = [[NEAR * f + n for n in range(NEAR)] for f in range(far)]

    def exchange(x):
        slab = (NEAR, x.shape[0] // NEAR, LANES)
        y = lax.all_to_all(x.reshape(slab), "ctx", 0, 0, axis_index_groups=neighbours)
        return y.reshape(x.shape)

    arrived = exchange(raw)
    halo = lax.ppermute(outer_tail, "ctx", [(i, i + 1) for i in range(size - 1)])
    arrived, halo = lax.optimization_barrier((arrived, halo))
    place = lax.axis_index("ctx").reshape(1).astype(jnp.int32)
    table, step, jump, rest, taps = call(
        tables_kernel,
        [
            pltpu.VMEM((count, 7, LANES, LANES), BF16),
            pltpu.VMEM((pack, LANES), F32),
            pltpu.VMEM((pack, LANES), F32),
            pltpu.VMEM((pack, LANES), F32),
            pltpu.VMEM((FEAT, LANES), F32),
        ],
        decay_rates.T,
        residues.T,
        medium_taps.T,
        feature_taps,
        scalars=(place,),
    )
    outer_feat = call(
        outer_kernel,
        pltpu.VMEM((rows, channels), F32),
        halo,
        outer_input,
        feature_taps,
        scratch=[pltpu.VMEM((tiles, HALO + rows, LANES), F32)],
    )
    packet = pltpu.VMEM((3 * pack + 2 * EDGE, LANES), BF16)
    found = [
        pltpu.VMEM((slab_rows, LANES), BF16),
        pltpu.VMEM((slab_rows, LANES), F32),
        pltpu.VMEM((pack, LANES), F32),
        packet,
    ]
    padded = [pltpu.VMEM((HALO + NEAR * rows, LANES), F32)]
    known = (arrived, taps, table, step)
    x, states, _, first_packed = call(
        with_width(first_states_kernel), found, *known, scalars=(place,), scratch=padded
    )
    x, states, end, packed = call(
        with_width(later_states_kernel),
        found,
        *known,
        x,
        states,
        scalars=(place,),
        scratch=padded,
        aliases={5: 0, 6: 1},
    )
    local = call(with_width(local_kernel), pltpu.VMEM((slab_rows, LANES), F32), x, table, states)

    def passed(x, start, end):
        pairs = [(NEAR * start + n, NEAR * end + n) for n in range(NEAR)]
        return lax.ppermute(x, "ctx", pairs)

    got_01 = passed(first_packed, 0, 1)
    got_23 = passed(packed, 2, 3)
    state, repacked = call(
        with_width(chain_kernel),
        [pltpu.VMEM((pack + EDGE, LANES), BF16), packet],
        got_01,
        arrived,
        taps,
        table,
        end,
        jump,
        rest,
        packed,
        scalars=(place,),
    )
    got_13 = passed(state, 1, 3)
    got_12 = passed(repacked, 1, 2)
    mixed = call(
        with_width(finish_kernel),
        pltpu.VMEM((slab_rows, LANES), BF16),
        local,
        got_01,
        got_23,
        got_12,
        got_13,
        arrived,
        taps,
        table,
        step,
        jump,
        rest,
        scalars=(place,),
        scratch=[pltpu.VMEM((pack, LANES), F32)],
    )
    hidden, sums = call(
        hidden_kernel,
        [pltpu.VMEM((rows, channels), F32), pltpu.VMEM((8 * parts, LANES), F32)],
        exchange(mixed),
        outer_feat,
        residual,
    )
    all_sums = lax.all_to_all(sums.reshape(parts, 8, LANES), "tp", 0, 0)
    return call(
        norm_kernel,
        jax.ShapeDtypeStruct((rows, channels), BF16),
        hidden,
        all_sums.reshape(8 * parts, LANES),
        norm_gain.reshape(1, channels),
    )


def solution(mesh):
    return jax.shard_map(
        on_device,
        mesh=mesh,
        in_specs=(
            P("ctx", "tp"),
            P("ctx", "tp"),
            P("ctx", "tp"),
            P(None, None, "tp"),
            P(None, "tp"),
            P("tp", None),
            P("tp", None),
            P("ctx", "tp"),
            P("tp"),
        ),
        out_specs=P("ctx", "tp"),
        check_vma=False,
    )
```

```python
import functools

import jax
import jax.numpy as jnp
from jax import lax
from jax.experimental import pallas as pl
from jax.experimental.pallas import tpu as pltpu
from jax.sharding import PartitionSpec as P


D = 8192
F32 = jnp.float32
BF16 = jnp.bfloat16
LANES = 128
HALO = 8
FEAT = 7
EDGE = 16
NEAR = 16


def iota(shape, axis):
    return lax.broadcasted_iota(jnp.int32, shape, axis)


def in_vmem(*arrays):
    return [pltpu.with_memory_space_constraint(a, pltpu.VMEM) for a in arrays]


def dot(a, b):
    return jnp.dot(a, b, preferred_element_type=F32)


def split(x):
    high = x.astype(BF16)
    return high, (x - high.astype(F32)).astype(BF16)


def split_three(x, width):
    high, _ = split(x)
    middle, _ = split(x - high.astype(F32))
    low = x - high.astype(F32) - middle.astype(F32)
    copy = iota(x.shape, 1) // width
    part = jnp.where(copy == 0, high.astype(F32), jnp.where(copy == 1, middle.astype(F32), low))
    return jnp.where(copy < 3, part, 0.0).astype(BF16)


def join_three(parts, width):
    x = parts.astype(F32)
    x = x + pltpu.roll(x, width, 1)
    return x + pltpu.roll(x, 2 * width, 1)


def two_parts(x, width):
    high, low = split(x)
    copy = iota(x.shape, 1) // width
    return jnp.where(copy == 1, low.astype(F32), high.astype(F32)).astype(BF16)


def tables_kernel(
    place,
    decay_ref,
    residue_ref,
    medium_ref,
    tap_ref,
    gain_in,
    table_ref,
    step_ref,
    jump_ref,
    rest_ref,
    mine_ref,
    gain_ref,
):
    gain_ref[...] = gain_in[...].astype(F32)
    channels = tap_ref.shape[2]
    half = LANES // 2
    at, to = iota((channels, LANES), 0), iota((channels, LANES), 1)
    position = lax.rem(place[0], NEAR)
    chosen = at == position * half + to % half
    for_inner = jnp.where(chosen & (to < half), 1.0, 0.0).astype(BF16)
    for_value = jnp.where(chosen & (to >= half), 1.0, 0.0).astype(BF16)
    mine_ref[...] = dot(tap_ref[1], for_inner) + dot(tap_ref[2], for_value)
    modes, groups = decay_ref.shape
    square = (LANES, LANES)
    block = LANES // 2
    row, lane = iota(square, 0), iota(square, 1)
    same = row // block == lane // block
    pick = iota((modes, LANES), 0) == iota((modes, LANES), 1) % modes
    lag = iota((modes, LANES), 1).astype(F32)
    zero_row = jnp.zeros((1, LANES), F32)
    width = 2 * modes
    count = table_ref.shape[0]

    def along_lanes(x):
        return jnp.sum(jnp.where(pick, x, 0.0), 0, keepdims=True)

    def along_rows(x):
        return jnp.sum(jnp.where(row == lane, along_lanes(x), 0.0), 1, keepdims=True)

    def toeplitz(filter_row):
        wide = jnp.concatenate([filter_row, zero_row], 1)
        wide = jnp.broadcast_to(wide, (LANES, 2 * LANES))
        return pltpu.roll(wide, 0, 1, stride=1, stride_axis=0)

    for q in range(count):
        group = position * count + q
        mine = iota((modes, groups), 1) == group
        rate = jnp.sum(jnp.where(mine, decay_ref[...], 0.0), 1, keepdims=True)
        weight = jnp.sum(jnp.where(mine, residue_ref[...], 0.0), 1, keepdims=True)
        weight = weight * jnp.sqrt(2.0 * rate / modes)
        long_row = jnp.sum(weight * jnp.exp(-rate * lag), 0, keepdims=True)
        chosen = iota(medium_ref.shape, 0) == group
        medium_row = jnp.sum(jnp.where(chosen, medium_ref[...].astype(F32), 0.0), 0, keepdims=True)
        medium_wide = toeplitz(medium_row)
        near = jnp.where(same, medium_wide[:, :LANES] + toeplitz(long_row)[:, :LANES], 0.0)
        table_ref[q, 0], table_ref[q, 1] = split(near)
        middle = [medium_wide[:, block:LANES], medium_wide[:, LANES : LANES + block]]
        table_ref[q, 2] = jnp.where(same, jnp.concatenate(middle, 1), 0.0).astype(BF16)
        table_ref[q, 3] = jnp.where(same, medium_wide[:, LANES:], 0.0).astype(BF16)
        rate_lanes, rate_rows, weight_rows = along_lanes(rate), along_rows(rate), along_rows(weight)
        to_end = jnp.exp(-rate_lanes * (block - 1 - row % block).astype(F32))
        kept = ((lane // modes) % 2 == row // block) & (lane < 3 * width)
        table_ref[q, 4], table_ref[q, 5] = split(jnp.where(kept, to_end, 0.0))
        from_start = weight_rows * jnp.exp(-rate_rows * (lane % block + 1).astype(F32))
        kept = ((row // modes) % 2 == lane // block) & (row < 3 * width)
        high, low = split(jnp.where(kept, from_start, 0.0))
        both = jnp.where(row < 2 * width, high.astype(F32), low.astype(F32))
        table_ref[q, 6] = both.astype(BF16)
        rows = slice(8 * q, 8 * q + 8)
        step_ref[rows] = jnp.broadcast_to(jnp.exp(-rate_lanes * block), (8, LANES))
        jump_ref[rows] = jnp.broadcast_to(jnp.exp(-rate_lanes * (block * NEAR)), (8, LANES))
        rest_ref[rows] = jnp.broadcast_to(jnp.exp(-rate_lanes * (block * (NEAR - 1))), (8, LANES))


def featurized(tap_ref, which, lanes, padded, rows):
    total = None
    for k in range(tap_ref.shape[1]):
        term = tap_ref[which, k : k + 1, lanes].astype(F32) * padded[HALO - k : HALO - k + rows, :]
        total = term if total is None else total + term
    return total


def tile_lanes(tile):
    return slice(tile * LANES, (tile + 1) * LANES)


def pack_kernel(inner_ref, value_ref, outer_ref, out_ref, tail_ref):
    tail_ref[...] = outer_ref[...]
    rows, channels = inner_ref.shape
    half = LANES // 2
    low = iota((rows, LANES), 1) < half
    for tile in range(channels // LANES):
        lanes = tile_lanes(tile)
        inner = inner_ref[:, lanes].astype(F32)
        value = value_ref[:, lanes].astype(F32)
        first = jnp.where(low, inner, pltpu.roll(value, half, 1))
        second = jnp.where(low, pltpu.roll(inner, half, 1), value)
        out_ref[2 * tile * rows : (2 * tile + 1) * rows] = first.astype(BF16)
        out_ref[(2 * tile + 1) * rows : (2 * tile + 2) * rows] = second.astype(BF16)


def outer_kernel(halo_ref, outer_ref, tap_ref, out_ref, padded):
    rows, channels = outer_ref.shape
    for tile in range(channels // LANES):
        lanes = tile_lanes(tile)
        padded[tile, :HALO] = halo_ref[:HALO, lanes].astype(F32)
        padded[tile, HALO:] = outer_ref[:, lanes].astype(F32)
        out_ref[:, lanes] = featurized(tap_ref, 0, lanes, padded.at[tile], rows)


def of_group(x, q, count):
    return x.reshape(x.shape[0] // (8 * count), count, 8, LANES)[:, q].reshape(-1, LANES)


def gated(tap_ref, padded, rows):
    total = None
    for k in range(FEAT):
        term = tap_ref[k : k + 1] * padded[HALO - k : HALO - k + rows]
        total = term if total is None else total + term
    return (total * pltpu.roll(total, LANES // 2, 1)).astype(BF16).astype(F32)


def slabs_of(product):
    both = jnp.concatenate([product, pltpu.roll(product, LANES - 8, 1)], 0).T
    return both.reshape(LANES // 16, 16, LANES)[:, :8].reshape(LANES // 2, LANES)


def missing(tap_ref, tail, head):
    block = LANES // 2
    product = gated(tap_ref, jnp.concatenate([tail[-HALO:], head[:HALO]], 0), HALO)
    kept = (iota(product.shape, 0) < FEAT - 1) & (iota(product.shape, 1) < block)
    product = jnp.where(kept, product, 0.0)
    return slabs_of(jnp.concatenate([product, jnp.zeros((block - HALO, LANES), F32)], 0))[: block // 2]


def to_states(table_ref, slab):
    count = table_ref.shape[0]
    parts = []
    for q in range(count):
        x = slab[8 * q : 8 * q + 8].astype(BF16)
        parts.append(dot(x, table_ref[q, 4]) + dot(x, table_ref[q, 5]))
    return jnp.concatenate(parts, 0)


def find_states(
    width, later, raw_ref, tap_ref, table_ref, step_ref, x_ref, state_ref, end_ref, send_ref, padded
):
    count = table_ref.shape[0]
    block = LANES // 2
    blocks = raw_ref.shape[0] // block
    padded[:HALO] = jnp.zeros((HALO, LANES), F32)
    padded[HALO:] = raw_ref[...].astype(F32)
    low = iota((block, LANES), 1) < block
    early = (iota((block, LANES), 0) < FEAT - 1)
    rows = 8 * count
    slabs = []
    for pair in range(blocks // 2):
        products = []
        for b in (2 * pair, 2 * pair + 1):
            product = gated(tap_ref, padded.at[b * block : (b + 1) * block + HALO], block)
            products.append(jnp.where(early, 0.0, product) if later and b == 0 else product)
        slabs.append(slabs_of(jnp.where(low, products[0], products[1])))
    wide = jnp.concatenate(slabs, 0)
    x_ref[...] = wide.astype(BF16)
    ends = []
    for q in range(count):
        x = of_group(wide, q, count).astype(BF16)
        local = dot(x, table_ref[q, 4]) + dot(x, table_ref[q, 5])
        step = step_ref[8 * q : 8 * q + 8]
        carry = jnp.zeros((8, LANES), F32)
        for b in range(blocks):
            at = rows * b + 8 * q
            state_ref[at : at + 8] = carry
            carry = carry * step + local[8 * b : 8 * b + 8]
        ends.append(carry)
    end = jnp.concatenate(ends, 0)
    end_ref[...] = end
    send_ref[:rows] = split_three(end, width)
    send_ref[rows : 3 * rows] = wide[(blocks - 2) * rows :].astype(BF16)
    send_ref[3 * rows : 3 * rows + EDGE] = raw_ref[blocks * block - EDGE :]
    send_ref[3 * rows + EDGE :] = raw_ref[:EDGE]


def super_block(place):
    return lax.div(place[0], NEAR)


def first_states_kernel(
    width, place, raw_ref, tap_ref, table_ref, step_ref, x_ref, state_ref, send_ref, padded, end
):
    @pl.when(super_block(place) == 0)
    def _():
        known = (raw_ref, tap_ref, table_ref, step_ref)
        find_states(width, False, *known, x_ref, state_ref, end, send_ref, padded)


def later_states_kernel(width, place, raw_ref, tap_ref, table_ref, step_ref, x_in, state_in, *refs):
    @pl.when(super_block(place) > 0)
    def _():
        find_states(width, True, raw_ref, tap_ref, table_ref, step_ref, *refs)


def chain_kernel(
    width,
    place,
    got_ref,
    raw_ref,
    tap_ref,
    table_ref,
    end_ref,
    jump_ref,
    rest_ref,
    send_ref,
    short_ref,
    next_ref,
):
    rows = end_ref.shape[0]

    @pl.when(super_block(place) == 1)
    def _():
        tail = got_ref[3 * rows : 3 * rows + EDGE].astype(F32)
        slab = missing(tap_ref, tail, raw_ref[:EDGE].astype(F32))
        end = end_ref[...] + rest_ref[...] * to_states(table_ref, slab)
        end = end + jump_ref[...] * join_three(got_ref[:rows], width)
        state = split_three(end, width)
        short_ref[:rows] = state
        short_ref[rows:] = send_ref[3 * rows : 3 * rows + EDGE]
        next_ref[:rows] = state
        next_ref[rows:] = send_ref[rows:]


def local_kernel(width, x_ref, table_ref, state_ref, out_ref):
    count = table_ref.shape[0]
    wide = x_ref[...].astype(F32)
    states = state_ref[...]
    zeros = jnp.zeros((8, LANES), F32)
    for q in range(count):
        x = of_group(wide, q, count)
        before = jnp.concatenate([zeros, x[:-8]], 0).astype(BF16)
        earlier = jnp.concatenate([zeros, zeros, x[:-16]], 0).astype(BF16)
        x = x.astype(BF16)
        mixed = dot(x, table_ref[q, 0]) + dot(x, table_ref[q, 1])
        mixed = mixed + dot(before, table_ref[q, 2]) + dot(earlier, table_ref[q, 3])
        mixed = mixed + dot(two_parts(of_group(states, q, count), width), table_ref[q, 6])
        for block in range(x.shape[0] // 8):
            at = 8 * (count * block + q)
            out_ref[at : at + 8] = mixed[8 * block : 8 * block + 8]


def finish_kernel(
    width,
    place,
    local_ref,
    got_01,
    got_23,
    got_12,
    got_13,
    raw_ref,
    tap_ref,
    table_ref,
    step_ref,
    jump_ref,
    rest_ref,
    out_ref,
    incoming_ref,
):
    here = super_block(place)

    @pl.when(here == 0)
    def _():
        out_ref[...] = local_ref[...].astype(BF16)

    @pl.when(here > 0)
    def _():
        count = table_ref.shape[0]
        rows = 8 * count
        blocks = local_ref.shape[0] // rows
        got = got_01[...].astype(F32) + got_23[...].astype(F32) + got_12[...].astype(F32)
        edge = slice(3 * rows, 3 * rows + EDGE)
        own_slab = missing(tap_ref, got[edge], raw_ref[:EDGE].astype(F32))
        incoming_ref[...] = join_three(got[:rows], width)

        @pl.when(here == 3)
        def _():
            far_tail = got_13[rows:].astype(F32)
            far_slab = missing(tap_ref, far_tail, got_23[3 * rows + EDGE :].astype(F32))
            more = rest_ref[...] * to_states(table_ref, far_slab)
            incoming_ref[...] += more + jump_ref[...] * join_three(got_13[:rows], width)

        incoming = incoming_ref[...]
        added = to_states(table_ref, own_slab)
        zeros = jnp.zeros((8, LANES), F32)
        parts = []
        for q in range(count):
            at = slice(8 * q, 8 * q + 8)
            step = step_ref[at]
            state = incoming[at]
            states = []
            for block in range(blocks):
                states.append(state)
                state = state * step
                if block == 0:
                    state = state + added[at]
            mixed = dot(two_parts(jnp.concatenate(states, 0), width), table_ref[q, 6])
            last_but_one, last, first = got[rows:][at], got[2 * rows :][at], own_slab[at]
            now = jnp.concatenate([first, zeros, zeros, zeros], 0).astype(BF16)
            before = jnp.concatenate([last, first, zeros, zeros], 0).astype(BF16)
            earlier = jnp.concatenate([last_but_one, last, first, zeros], 0).astype(BF16)
            start = dot(now, table_ref[q, 0]) + dot(now, table_ref[q, 1])
            start = start + dot(before, table_ref[q, 2]) + dot(earlier, table_ref[q, 3])
            mixed = jnp.concatenate([mixed[:32] + start, mixed[32:]], 0)
            parts.append(mixed.reshape(blocks, 8, LANES))
        total = local_ref[...] + jnp.concatenate(parts, 1).reshape(local_ref.shape)
        out_ref[...] = total.astype(BF16)


def hidden_kernel(mixed_ref, outer_ref, residual_ref, hidden_ref, sum_ref):
    rows, channels = outer_ref.shape
    squares = jnp.zeros((rows, LANES), F32)
    for tile in range(channels // LANES):
        lanes = tile_lanes(tile)
        slabs = mixed_ref[tile * (LANES // 2) : (tile + 1) * (LANES // 2)].astype(F32)
        other = pltpu.roll(slabs, LANES // 2, 1)
        groups = LANES // 16
        both = jnp.concatenate([slabs.reshape(groups, 8, LANES), other.reshape(groups, 8, LANES)], 1)
        mixed = both.reshape(LANES, LANES).T[:rows]
        hidden = residual_ref[:, lanes].astype(F32) + outer_ref[:, lanes] * mixed
        hidden_ref[:, lanes] = hidden
        squares = squares + hidden * hidden
    tall = jnp.concatenate([squares, jnp.zeros_like(squares)], 0).T
    line = jnp.sum(tall, 0, keepdims=True)
    sum_ref[...] = jnp.broadcast_to(line, sum_ref.shape)


def norm_kernel(hidden_ref, sum_ref, gain_ref, out_ref):
    rows, channels = hidden_ref.shape
    parts = sum_ref[...].reshape(sum_ref.shape[0] // 8, 8, LANES)
    line = jnp.sum(parts, 0)
    scale = 1.0 / jnp.sqrt(line / D + 1e-05)
    tall = jnp.broadcast_to(scale[:1], (LANES, LANES)).T[:rows]
    for tile in range(channels // LANES):
        lanes = slice(tile * LANES, (tile + 1) * LANES)
        out_ref[:, lanes] = (hidden_ref[:, lanes] * gain_ref[:, lanes] * tall).astype(BF16)


def on_device(
    outer_input,
    inner_input,
    value_input,
    feature_taps,
    medium_taps,
    decay_rates,
    residues,
    residual,
    norm_gain,
):
    rows, channels = outer_input.shape
    groups, modes = decay_rates.shape
    size = lax.axis_size("ctx")
    parts = lax.axis_size("tp")
    tiles = channels // LANES
    vmem = pl.BlockSpec(memory_space=pltpu.VMEM)
    smem = pl.BlockSpec(memory_space=pltpu.SMEM)

    def call(kernel, out, *arrays, scalars=(), scratch=(), aliases={}):
        return pl.pallas_call(
            kernel,
            in_specs=[smem] * len(scalars) + [vmem] * len(arrays),
            out_specs=jax.tree.map(lambda _: vmem, out),
            out_shape=out,
            scratch_shapes=scratch,
            input_output_aliases=aliases,
        )(*scalars, *in_vmem(*arrays))

    slab_rows = rows * channels // LANES
    count = groups // NEAR
    width = 2 * modes
    far = size // NEAR
    assert far == 4
    pack = 8 * count
    with_width = lambda kernel: functools.partial(kernel, width)

    raw, outer_tail = pl.pallas_call(
        pack_kernel,
        grid=(1,),
        in_specs=[
            pl.BlockSpec((rows, channels), lambda i: (0, 0)),
            pl.BlockSpec((rows, channels), lambda i: (0, 0)),
            pl.BlockSpec((HALO, channels), lambda i: (rows // HALO - 1, 0)),
        ],
        out_shape=[pltpu.VMEM((NEAR * rows, LANES), BF16), pltpu.VMEM((HALO, channels), BF16)],
        out_specs=[vmem, vmem],
        name="pack",
    )(inner_input, value_input, outer_input)
    neighbours = [[NEAR * f + n for n in range(NEAR)] for f in range(far)]

    def exchange(x):
        slab = (NEAR, x.shape[0] // NEAR, LANES)
        y = lax.all_to_all(x.reshape(slab), "ctx", 0, 0, axis_index_groups=neighbours)
        return y.reshape(x.shape)

    arrived = exchange(raw)
    halo = lax.ppermute(outer_tail, "ctx", [(i, i + 1) for i in range(size - 1)])
    arrived, halo = lax.optimization_barrier((arrived, halo))
    place = lax.axis_index("ctx").reshape(1).astype(jnp.int32)
    table, step, jump, rest, taps, gain = call(
        tables_kernel,
        [
            pltpu.VMEM((count, 7, LANES, LANES), BF16),
            pltpu.VMEM((pack, LANES), F32),
            pltpu.VMEM((pack, LANES), F32),
            pltpu.VMEM((pack, LANES), F32),
            pltpu.VMEM((FEAT, LANES), F32),
            pltpu.VMEM((1, channels), F32),
        ],
        decay_rates.T,
        residues.T,
        medium_taps.T,
        feature_taps,
        norm_gain.reshape(1, channels),
        scalars=(place,),
    )
    outer_feat = call(
        outer_kernel,
        pltpu.VMEM((rows, channels), F32),
        halo,
        outer_input,
        feature_taps,
        scratch=[pltpu.VMEM((tiles, HALO + rows, LANES), F32)],
    )
    packet = pltpu.VMEM((3 * pack + 2 * EDGE, LANES), BF16)
    found = [
        pltpu.VMEM((slab_rows, LANES), BF16),
        pltpu.VMEM((slab_rows, LANES), F32),
        pltpu.VMEM((pack, LANES), F32),
        packet,
    ]
    padded = [pltpu.VMEM((HALO + NEAR * rows, LANES), F32)]
    known = (arrived, taps, table, step)
    x, states, first_packed = call(
        with_width(first_states_kernel),
        [found[0], found[1], packet],
        *known,
        scalars=(place,),
        scratch=padded + [pltpu.VMEM((pack, LANES), F32)],
    )
    x, states, end, packed = call(
        with_width(later_states_kernel),
        found,
        *known,
        x,
        states,
        scalars=(place,),
        scratch=padded,
        aliases={5: 0, 6: 1},
    )
    local = call(with_width(local_kernel), pltpu.VMEM((slab_rows, LANES), F32), x, table, states)

    local, outer_feat = lax.optimization_barrier((local, outer_feat))

    def passed(x, start, end):
        pairs = [(NEAR * start + n, NEAR * end + n) for n in range(NEAR)]
        return lax.ppermute(x, "ctx", pairs)

    got_01 = passed(first_packed, 0, 1)
    got_23 = passed(packed, 2, 3)
    state, repacked = call(
        with_width(chain_kernel),
        [pltpu.VMEM((pack + EDGE, LANES), BF16), packet],
        got_01,
        arrived,
        taps,
        table,
        end,
        jump,
        rest,
        packed,
        scalars=(place,),
    )
    got_13 = passed(state, 1, 3)
    got_12 = passed(repacked, 1, 2)
    mixed = call(
        with_width(finish_kernel),
        pltpu.VMEM((slab_rows, LANES), BF16),
        local,
        got_01,
        got_23,
        got_12,
        got_13,
        arrived,
        taps,
        table,
        step,
        jump,
        rest,
        scalars=(place,),
        scratch=[pltpu.VMEM((pack, LANES), F32)],
    )
    hidden, sums = call(
        hidden_kernel,
        [pltpu.VMEM((rows, channels), F32), pltpu.VMEM((8 * parts, LANES), F32)],
        exchange(mixed),
        outer_feat,
        residual,
    )
    all_sums = lax.all_to_all(sums.reshape(parts, 8, LANES), "tp", 0, 0)
    return call(
        norm_kernel,
        jax.ShapeDtypeStruct((rows, channels), BF16),
        hidden,
        all_sums.reshape(8 * parts, LANES),
        gain,
    )


def solution(mesh):
    return jax.shard_map(
        on_device,
        mesh=mesh,
        in_specs=(
            P("ctx", "tp"),
            P("ctx", "tp"),
            P("ctx", "tp"),
            P(None, None, "tp"),
            P(None, "tp"),
            P("tp", None),
            P("tp", None),
            P("ctx", "tp"),
            P("tp"),
        ),
        out_specs=P("ctx", "tp"),
        check_vma=False,
    )
```

```python
import functools

import jax
import jax.numpy as jnp
from jax import lax
from jax.experimental import pallas as pl
from jax.experimental.pallas import tpu as pltpu
from jax.sharding import PartitionSpec as P


D = 8192
F32 = jnp.float32
BF16 = jnp.bfloat16
LANES = 128
HALO = 8
FEAT = 7
EDGE = 16
NEAR = 16


def iota(shape, axis):
    return lax.broadcasted_iota(jnp.int32, shape, axis)


def in_vmem(*arrays):
    return [pltpu.with_memory_space_constraint(a, pltpu.VMEM) for a in arrays]


def dot(a, b):
    return jnp.dot(a, b, preferred_element_type=F32)


def split(x):
    high = x.astype(BF16)
    return high, (x - high.astype(F32)).astype(BF16)


def split_three(x, width):
    high, _ = split(x)
    middle, _ = split(x - high.astype(F32))
    low = x - high.astype(F32) - middle.astype(F32)
    copy = iota(x.shape, 1) // width
    part = jnp.where(copy == 0, high.astype(F32), jnp.where(copy == 1, middle.astype(F32), low))
    return jnp.where(copy < 3, part, 0.0).astype(BF16)


def join_three(parts, width):
    x = parts.astype(F32)
    x = x + pltpu.roll(x, width, 1)
    return x + pltpu.roll(x, 2 * width, 1)


def two_parts(x, width):
    high, low = split(x)
    copy = iota(x.shape, 1) // width
    return jnp.where(copy == 1, low.astype(F32), high.astype(F32)).astype(BF16)


def tables_kernel(
    place,
    decay_ref,
    residue_ref,
    medium_ref,
    tap_ref,
    gain_in,
    table_ref,
    step_ref,
    jump_ref,
    rest_ref,
    mine_ref,
    gain_ref,
):
    gain_ref[...] = gain_in[...].astype(F32)
    channels = tap_ref.shape[2]
    half = LANES // 2
    at, to = iota((channels, LANES), 0), iota((channels, LANES), 1)
    position = lax.rem(place[0], NEAR)
    chosen = at == position * half + to % half
    for_inner = jnp.where(chosen & (to < half), 1.0, 0.0).astype(BF16)
    for_value = jnp.where(chosen & (to >= half), 1.0, 0.0).astype(BF16)
    mine_ref[...] = dot(tap_ref[1], for_inner) + dot(tap_ref[2], for_value)
    modes, groups = decay_ref.shape
    square = (LANES, LANES)
    block = LANES // 2
    row, lane = iota(square, 0), iota(square, 1)
    same = row // block == lane // block
    pick = iota((modes, LANES), 0) == iota((modes, LANES), 1) % modes
    lag = iota((modes, LANES), 1).astype(F32)
    zero_row = jnp.zeros((1, LANES), F32)
    width = 2 * modes
    count = table_ref.shape[0]

    def along_lanes(x):
        return jnp.sum(jnp.where(pick, x, 0.0), 0, keepdims=True)

    def along_rows(x):
        return jnp.sum(jnp.where(row == lane, along_lanes(x), 0.0), 1, keepdims=True)

    def toeplitz(filter_row):
        wide = jnp.concatenate([filter_row, zero_row], 1)
        wide = jnp.broadcast_to(wide, (LANES, 2 * LANES))
        return pltpu.roll(wide, 0, 1, stride=1, stride_axis=0)

    for q in range(count):
        group = position * count + q
        mine = iota((modes, groups), 1) == group
        rate = jnp.sum(jnp.where(mine, decay_ref[...], 0.0), 1, keepdims=True)
        weight = jnp.sum(jnp.where(mine, residue_ref[...], 0.0), 1, keepdims=True)
        weight = weight * jnp.sqrt(2.0 * rate / modes)
        long_row = jnp.sum(weight * jnp.exp(-rate * lag), 0, keepdims=True)
        chosen = iota(medium_ref.shape, 0) == group
        medium_row = jnp.sum(jnp.where(chosen, medium_ref[...].astype(F32), 0.0), 0, keepdims=True)
        medium_wide = toeplitz(medium_row)
        near = jnp.where(same, medium_wide[:, :LANES] + toeplitz(long_row)[:, :LANES], 0.0)
        table_ref[q, 0], table_ref[q, 1] = split(near)
        middle = [medium_wide[:, block:LANES], medium_wide[:, LANES : LANES + block]]
        table_ref[q, 2] = jnp.where(same, jnp.concatenate(middle, 1), 0.0).astype(BF16)
        table_ref[q, 3] = jnp.where(same, medium_wide[:, LANES:], 0.0).astype(BF16)
        rate_lanes, rate_rows, weight_rows = along_lanes(rate), along_rows(rate), along_rows(weight)
        to_end = jnp.exp(-rate_lanes * (block - 1 - row % block).astype(F32))
        kept = ((lane // modes) % 2 == row // block) & (lane < 3 * width)
        table_ref[q, 4], table_ref[q, 5] = split(jnp.where(kept, to_end, 0.0))
        from_start = weight_rows * jnp.exp(-rate_rows * (lane % block + 1).astype(F32))
        kept = ((row // modes) % 2 == lane // block) & (row < 3 * width)
        high, low = split(jnp.where(kept, from_start, 0.0))
        both = jnp.where(row < 2 * width, high.astype(F32), low.astype(F32))
        table_ref[q, 6] = both.astype(BF16)
        rows = slice(8 * q, 8 * q + 8)
        step_ref[rows] = jnp.broadcast_to(jnp.exp(-rate_lanes * block), (8, LANES))
        jump_ref[rows] = jnp.broadcast_to(jnp.exp(-rate_lanes * (block * NEAR)), (8, LANES))
        rest_ref[rows] = jnp.broadcast_to(jnp.exp(-rate_lanes * (block * (NEAR - 1))), (8, LANES))


def featurized(tap_ref, which, lanes, padded, rows):
    total = None
    for k in range(tap_ref.shape[1]):
        term = tap_ref[which, k : k + 1, lanes].astype(F32) * padded[HALO - k : HALO - k + rows, :]
        total = term if total is None else total + term
    return total


def tile_lanes(tile):
    return slice(tile * LANES, (tile + 1) * LANES)


def pack_kernel(inner_ref, value_ref, outer_ref, out_ref, tail_ref):
    tail_ref[...] = outer_ref[...]
    rows, channels = inner_ref.shape
    half = LANES // 2
    low = iota((rows, LANES), 1) < half
    for tile in range(channels // LANES):
        lanes = tile_lanes(tile)
        inner = inner_ref[:, lanes].astype(F32)
        value = value_ref[:, lanes].astype(F32)
        first = jnp.where(low, inner, pltpu.roll(value, half, 1))
        second = jnp.where(low, pltpu.roll(inner, half, 1), value)
        out_ref[2 * tile * rows : (2 * tile + 1) * rows] = first.astype(BF16)
        out_ref[(2 * tile + 1) * rows : (2 * tile + 2) * rows] = second.astype(BF16)


def outer_kernel(halo_ref, outer_ref, tap_ref, out_ref, padded):
    rows, channels = outer_ref.shape
    for tile in range(channels // LANES):
        lanes = tile_lanes(tile)
        padded[tile, :HALO] = halo_ref[:HALO, lanes].astype(F32)
        padded[tile, HALO:] = outer_ref[:, lanes].astype(F32)
        out_ref[:, lanes] = featurized(tap_ref, 0, lanes, padded.at[tile], rows)


def of_group(x, q, count):
    return x.reshape(x.shape[0] // (8 * count), count, 8, LANES)[:, q].reshape(-1, LANES)


def gated(tap_ref, padded, rows):
    total = None
    for k in range(FEAT):
        term = tap_ref[k : k + 1] * padded[HALO - k : HALO - k + rows]
        total = term if total is None else total + term
    return (total * pltpu.roll(total, LANES // 2, 1)).astype(BF16).astype(F32)


def slabs_of(product):
    both = jnp.concatenate([product, pltpu.roll(product, LANES - 8, 1)], 0).T
    return both.reshape(LANES // 16, 16, LANES)[:, :8].reshape(LANES // 2, LANES)


def missing(tap_ref, tail, head):
    block = LANES // 2
    product = gated(tap_ref, jnp.concatenate([tail[-HALO:], head[:HALO]], 0), HALO)
    kept = (iota(product.shape, 0) < FEAT - 1) & (iota(product.shape, 1) < block)
    product = jnp.where(kept, product, 0.0)
    return slabs_of(jnp.concatenate([product, jnp.zeros((block - HALO, LANES), F32)], 0))[: block // 2]


def to_states(table_ref, slab):
    count = table_ref.shape[0]
    parts = []
    for q in range(count):
        x = slab[8 * q : 8 * q + 8].astype(BF16)
        parts.append(dot(x, table_ref[q, 4]) + dot(x, table_ref[q, 5]))
    return jnp.concatenate(parts, 0)


def find_local(width, wide, table_ref, states, out_ref):
    count = table_ref.shape[0]
    zeros = jnp.zeros((8, LANES), F32)
    for q in range(count):
        x = of_group(wide, q, count)
        before = jnp.concatenate([zeros, x[:-8]], 0).astype(BF16)
        earlier = jnp.concatenate([zeros, zeros, x[:-16]], 0).astype(BF16)
        x = x.astype(BF16)
        mixed = dot(x, table_ref[q, 0]) + dot(x, table_ref[q, 1])
        mixed = mixed + dot(before, table_ref[q, 2]) + dot(earlier, table_ref[q, 3])
        mixed = mixed + dot(two_parts(of_group(states, q, count), width), table_ref[q, 6])
        for block in range(x.shape[0] // 8):
            at = 8 * (count * block + q)
            out_ref[at : at + 8] = mixed[8 * block : 8 * block + 8]


def find_states(
    width, later, raw_ref, tap_ref, table_ref, step_ref, local_ref, end_ref, send_ref, padded, state_ref
):
    count = table_ref.shape[0]
    block = LANES // 2
    blocks = raw_ref.shape[0] // block
    padded[:HALO] = jnp.zeros((HALO, LANES), F32)
    padded[HALO:] = raw_ref[...].astype(F32)
    low = iota((block, LANES), 1) < block
    early = (iota((block, LANES), 0) < FEAT - 1)
    rows = 8 * count
    slabs = []
    for pair in range(blocks // 2):
        products = []
        for b in (2 * pair, 2 * pair + 1):
            product = gated(tap_ref, padded.at[b * block : (b + 1) * block + HALO], block)
            products.append(jnp.where(early, 0.0, product) if later and b == 0 else product)
        slabs.append(slabs_of(jnp.where(low, products[0], products[1])))
    wide = jnp.concatenate(slabs, 0)
    ends = []
    for q in range(count):
        x = of_group(wide, q, count).astype(BF16)
        local = dot(x, table_ref[q, 4]) + dot(x, table_ref[q, 5])
        step = step_ref[8 * q : 8 * q + 8]
        carry = jnp.zeros((8, LANES), F32)
        for b in range(blocks):
            at = rows * b + 8 * q
            state_ref[at : at + 8] = carry
            carry = carry * step + local[8 * b : 8 * b + 8]
        ends.append(carry)
    end = jnp.concatenate(ends, 0)
    end_ref[...] = end
    send_ref[:rows] = split_three(end, width)
    send_ref[rows : 3 * rows] = wide[(blocks - 2) * rows :].astype(BF16)
    send_ref[3 * rows : 3 * rows + EDGE] = raw_ref[blocks * block - EDGE :]
    send_ref[3 * rows + EDGE :] = raw_ref[:EDGE]
    find_local(width, wide, table_ref, state_ref[...], local_ref)


def super_block(place):
    return lax.div(place[0], NEAR)


def first_states_kernel(width, place, *refs):
    raw_ref, tap_ref, table_ref, step_ref, local_ref, send_ref, padded, state_ref, end_ref = refs

    @pl.when(super_block(place) == 0)
    def _():
        known = (raw_ref, tap_ref, table_ref, step_ref)
        find_states(width, False, *known, local_ref, end_ref, send_ref, padded, state_ref)


def later_states_kernel(width, place, raw_ref, tap_ref, table_ref, step_ref, local_in, *refs):
    @pl.when(super_block(place) > 0)
    def _():
        find_states(width, True, raw_ref, tap_ref, table_ref, step_ref, *refs)


def chain_kernel(
    width,
    place,
    got_ref,
    raw_ref,
    tap_ref,
    table_ref,
    end_ref,
    jump_ref,
    rest_ref,
    send_ref,
    short_ref,
    next_ref,
):
    rows = end_ref.shape[0]

    @pl.when(super_block(place) == 1)
    def _():
        tail = got_ref[3 * rows : 3 * rows + EDGE].astype(F32)
        slab = missing(tap_ref, tail, raw_ref[:EDGE].astype(F32))
        end = end_ref[...] + rest_ref[...] * to_states(table_ref, slab)
        end = end + jump_ref[...] * join_three(got_ref[:rows], width)
        state = split_three(end, width)
        short_ref[:rows] = state
        short_ref[rows:] = send_ref[3 * rows : 3 * rows + EDGE]
        next_ref[:rows] = state
        next_ref[rows:] = send_ref[rows:]


def spread(width, state, step, table, blocks, added=None):
    states = []
    for block in range(blocks):
        states.append(state)
        state = state * step
        if block == 0 and added is not None:
            state = state + added
    return dot(two_parts(jnp.concatenate(states, 0), width), table)


def join_kernel(
    width, place, local_ref, got_01, got_23, got_12, raw_ref, tap_ref, table_ref, step_ref, out_ref
):
    @pl.when(super_block(place) > 0)
    def _():
        count = table_ref.shape[0]
        rows = 8 * count
        blocks = local_ref.shape[0] // rows
        got = got_01[...].astype(F32) + got_23[...].astype(F32) + got_12[...].astype(F32)
        edge = slice(3 * rows, 3 * rows + EDGE)
        own_slab = missing(tap_ref, got[edge], raw_ref[:EDGE].astype(F32))
        incoming = join_three(got[:rows], width)
        added = to_states(table_ref, own_slab)
        zeros = jnp.zeros((8, LANES), F32)
        parts = []
        for q in range(count):
            at = slice(8 * q, 8 * q + 8)
            mixed = spread(width, incoming[at], step_ref[at], table_ref[q, 6], blocks, added[at])
            last_but_one, last, first = got[rows:][at], got[2 * rows :][at], own_slab[at]
            now = jnp.concatenate([first, zeros, zeros, zeros], 0).astype(BF16)
            before = jnp.concatenate([last, first, zeros, zeros], 0).astype(BF16)
            earlier = jnp.concatenate([last_but_one, last, first, zeros], 0).astype(BF16)
            start = dot(now, table_ref[q, 0]) + dot(now, table_ref[q, 1])
            start = start + dot(before, table_ref[q, 2]) + dot(earlier, table_ref[q, 3])
            mixed = jnp.concatenate([mixed[:32] + start, mixed[32:]], 0)
            parts.append(mixed.reshape(blocks, 8, LANES))
        out_ref[...] = local_ref[...] + jnp.concatenate(parts, 1).reshape(local_ref.shape)


def finish_kernel(
    width,
    place,
    near_ref,
    got_23,
    got_13,
    tap_ref,
    table_ref,
    step_ref,
    jump_ref,
    rest_ref,
    out_ref,
):
    here = super_block(place)

    @pl.when(here != 3)
    def _():
        out_ref[...] = near_ref[...].astype(BF16)

    @pl.when(here == 3)
    def _():
        count = table_ref.shape[0]
        rows = 8 * count
        blocks = near_ref.shape[0] // rows
        far_tail = got_13[rows:].astype(F32)
        far_slab = missing(tap_ref, far_tail, got_23[3 * rows + EDGE :].astype(F32))
        incoming = rest_ref[...] * to_states(table_ref, far_slab)
        incoming = incoming + jump_ref[...] * join_three(got_13[:rows], width)
        parts = []
        for q in range(count):
            at = slice(8 * q, 8 * q + 8)
            mixed = spread(width, incoming[at], step_ref[at], table_ref[q, 6], blocks)
            parts.append(mixed.reshape(blocks, 8, LANES))
        total = near_ref[...] + jnp.concatenate(parts, 1).reshape(near_ref.shape)
        out_ref[...] = total.astype(BF16)


def hidden_kernel(mixed_ref, outer_ref, residual_ref, hidden_ref, sum_ref):
    rows, channels = outer_ref.shape
    squares = jnp.zeros((rows, LANES), F32)
    for tile in range(channels // LANES):
        lanes = tile_lanes(tile)
        slabs = mixed_ref[tile * (LANES // 2) : (tile + 1) * (LANES // 2)].astype(F32)
        other = pltpu.roll(slabs, LANES // 2, 1)
        groups = LANES // 16
        both = jnp.concatenate([slabs.reshape(groups, 8, LANES), other.reshape(groups, 8, LANES)], 1)
        mixed = both.reshape(LANES, LANES).T[:rows]
        hidden = residual_ref[:, lanes].astype(F32) + outer_ref[:, lanes] * mixed
        hidden_ref[:, lanes] = hidden
        squares = squares + hidden * hidden
    tall = jnp.concatenate([squares, jnp.zeros_like(squares)], 0).T
    line = jnp.sum(tall, 0, keepdims=True)
    sum_ref[...] = jnp.broadcast_to(line, sum_ref.shape)


def norm_kernel(hidden_ref, sum_ref, gain_ref, out_ref):
    rows, channels = hidden_ref.shape
    parts = sum_ref[...].reshape(sum_ref.shape[0] // 8, 8, LANES)
    line = jnp.sum(parts, 0)
    scale = 1.0 / jnp.sqrt(line / D + 1e-05)
    tall = jnp.broadcast_to(scale[:1], (LANES, LANES)).T[:rows]
    for tile in range(channels // LANES):
        lanes = slice(tile * LANES, (tile + 1) * LANES)
        out_ref[:, lanes] = (hidden_ref[:, lanes] * gain_ref[:, lanes] * tall).astype(BF16)


def on_device(
    outer_input,
    inner_input,
    value_input,
    feature_taps,
    medium_taps,
    decay_rates,
    residues,
    residual,
    norm_gain,
):
    rows, channels = outer_input.shape
    groups, modes = decay_rates.shape
    size = lax.axis_size("ctx")
    parts = lax.axis_size("tp")
    tiles = channels // LANES
    vmem = pl.BlockSpec(memory_space=pltpu.VMEM)
    smem = pl.BlockSpec(memory_space=pltpu.SMEM)

    def call(kernel, out, *arrays, scalars=(), scratch=(), aliases={}):
        return pl.pallas_call(
            kernel,
            in_specs=[smem] * len(scalars) + [vmem] * len(arrays),
            out_specs=jax.tree.map(lambda _: vmem, out),
            out_shape=out,
            scratch_shapes=scratch,
            input_output_aliases=aliases,
        )(*scalars, *in_vmem(*arrays))

    slab_rows = rows * channels // LANES
    count = groups // NEAR
    width = 2 * modes
    far = size // NEAR
    assert far == 4
    pack = 8 * count
    with_width = lambda kernel: functools.partial(kernel, width)

    steps = 4
    part = pl.BlockSpec((rows, channels // steps), lambda i: (0, i))
    raw, outer_tail = pl.pallas_call(
        pack_kernel,
        grid=(steps,),
        in_specs=[
            part,
            part,
            pl.BlockSpec((HALO, channels // steps), lambda i: (rows // HALO - 1, i)),
        ],
        out_specs=[
            pl.BlockSpec((NEAR * rows // steps, LANES), lambda i: (i, 0)),
            pl.BlockSpec((HALO, channels // steps), lambda i: (0, i)),
        ],
        out_shape=[
            jax.ShapeDtypeStruct((NEAR * rows, LANES), BF16),
            jax.ShapeDtypeStruct((HALO, channels), BF16),
        ],
        name="pack",
    )(inner_input, value_input, outer_input)
    neighbours = [[NEAR * f + n for n in range(NEAR)] for f in range(far)]

    def exchange(x):
        slab = (NEAR, x.shape[0] // NEAR, LANES)
        y = lax.all_to_all(x.reshape(slab), "ctx", 0, 0, axis_index_groups=neighbours)
        return y.reshape(x.shape)

    arrived = exchange(raw)
    halo = lax.ppermute(outer_tail, "ctx", [(i, i + 1) for i in range(size - 1)])
    arrived, halo = lax.optimization_barrier((arrived, halo))
    place = lax.axis_index("ctx").reshape(1).astype(jnp.int32)
    table, step, jump, rest, taps, gain = call(
        tables_kernel,
        [
            pltpu.VMEM((count, 7, LANES, LANES), BF16),
            pltpu.VMEM((pack, LANES), F32),
            pltpu.VMEM((pack, LANES), F32),
            pltpu.VMEM((pack, LANES), F32),
            pltpu.VMEM((FEAT, LANES), F32),
            pltpu.VMEM((1, channels), F32),
        ],
        decay_rates.T,
        residues.T,
        medium_taps.T,
        feature_taps,
        norm_gain.reshape(1, channels),
        scalars=(place,),
    )
    outer_feat = call(
        outer_kernel,
        pltpu.VMEM((rows, channels), F32),
        halo,
        outer_input,
        feature_taps,
        scratch=[pltpu.VMEM((tiles, HALO + rows, LANES), F32)],
    )
    packet = pltpu.VMEM((3 * pack + 2 * EDGE, LANES), BF16)
    whole = pltpu.VMEM((slab_rows, LANES), F32)
    ends = pltpu.VMEM((pack, LANES), F32)
    scratch = [pltpu.VMEM((HALO + NEAR * rows, LANES), F32), whole]
    known = (arrived, taps, table, step)
    local, first_packed = call(
        with_width(first_states_kernel),
        [whole, packet],
        *known,
        scalars=(place,),
        scratch=scratch + [ends],
    )
    local, end, packed = call(
        with_width(later_states_kernel),
        [whole, ends, packet],
        *known,
        local,
        scalars=(place,),
        scratch=scratch,
        aliases={5: 0},
    )

    local, outer_feat = lax.optimization_barrier((local, outer_feat))

    def passed(x, start, end):
        pairs = [(NEAR * start + n, NEAR * end + n) for n in range(NEAR)]
        return lax.ppermute(x, "ctx", pairs)

    got_01 = passed(first_packed, 0, 1)
    got_23 = passed(packed, 2, 3)
    state, repacked = call(
        with_width(chain_kernel),
        [pltpu.VMEM((pack + EDGE, LANES), BF16), packet],
        got_01,
        arrived,
        taps,
        table,
        end,
        jump,
        rest,
        packed,
        scalars=(place,),
    )
    got_13 = passed(state, 1, 3)
    got_12 = passed(repacked, 1, 2)
    near = call(
        with_width(join_kernel),
        whole,
        local,
        got_01,
        got_23,
        got_12,
        arrived,
        taps,
        table,
        step,
        scalars=(place,),
        aliases={1: 0},
    )
    mixed = call(
        with_width(finish_kernel),
        pltpu.VMEM((slab_rows, LANES), BF16),
        near,
        got_23,
        got_13,
        taps,
        table,
        step,
        jump,
        rest,
        scalars=(place,),
    )
    hidden, sums = call(
        hidden_kernel,
        [pltpu.VMEM((rows, channels), F32), pltpu.VMEM((8 * parts, LANES), F32)],
        exchange(mixed),
        outer_feat,
        residual,
    )
    all_sums = lax.all_to_all(sums.reshape(parts, 8, LANES), "tp", 0, 0)
    return call(
        norm_kernel,
        jax.ShapeDtypeStruct((rows, channels), BF16),
        hidden,
        all_sums.reshape(8 * parts, LANES),
        gain,
    )


def solution(mesh):
    return jax.shard_map(
        on_device,
        mesh=mesh,
        in_specs=(
            P("ctx", "tp"),
            P("ctx", "tp"),
            P("ctx", "tp"),
            P(None, None, "tp"),
            P(None, "tp"),
            P("tp", None),
            P("tp", None),
            P("ctx", "tp"),
            P("tp"),
        ),
        out_specs=P("ctx", "tp"),
        check_vma=False,
    )
```

```python
import functools

import jax
import jax.numpy as jnp
from jax import lax
from jax.experimental import pallas as pl
from jax.experimental.pallas import tpu as pltpu
from jax.sharding import PartitionSpec as P


D = 8192
F32 = jnp.float32
BF16 = jnp.bfloat16
LANES = 128
HALO = 8
FEAT = 7
EDGE = 8
NEAR = 16


def iota(shape, axis):
    return lax.broadcasted_iota(jnp.int32, shape, axis)


def in_vmem(*arrays):
    return [pltpu.with_memory_space_constraint(a, pltpu.VMEM) for a in arrays]


def dot(a, b):
    return jnp.dot(a, b, preferred_element_type=F32)


def split(x):
    high = x.astype(BF16)
    return high, (x - high.astype(F32)).astype(BF16)


def pack_state(x, width):
    high, low = split(x)
    copy = iota(x.shape, 1) // width
    part = jnp.where(copy % 2 == 0, high.astype(F32), low.astype(F32))
    half = x.shape[0] // 2
    return jnp.where(copy[:half] < 2, part[:half], part[half:]).astype(BF16)


def unpack_state(packed, width):
    x = packed.astype(F32)
    both = x + pltpu.roll(x, width, 1)
    copy = iota(x.shape, 1) // width
    parts = []
    for place in (1, 3):
        y = jnp.where(copy == place, both, 0.0)
        y = y + pltpu.roll(y, width, 1)
        parts.append(y + pltpu.roll(y, 2 * width, 1))
    return jnp.concatenate(parts, 0)


def two_parts(x, width):
    high, low = split(x)
    copy = iota(x.shape, 1) // width
    return jnp.where(copy == 1, low.astype(F32), high.astype(F32)).astype(BF16)


def tables_kernel(
    place,
    decay_ref,
    residue_ref,
    medium_ref,
    tap_ref,
    gain_in,
    table_ref,
    step_ref,
    jump_ref,
    rest_ref,
    mine_ref,
    gain_ref,
):
    gain_ref[...] = gain_in[...].astype(F32)
    channels = tap_ref.shape[2]
    half = LANES // 2
    at, to = iota((channels, LANES), 0), iota((channels, LANES), 1)
    position = lax.rem(place[0], NEAR)
    chosen = at == position * half + to % half
    for_inner = jnp.where(chosen & (to < half), 1.0, 0.0).astype(BF16)
    for_value = jnp.where(chosen & (to >= half), 1.0, 0.0).astype(BF16)
    mine_ref[...] = dot(tap_ref[1], for_inner) + dot(tap_ref[2], for_value)
    modes, groups = decay_ref.shape
    square = (LANES, LANES)
    block = LANES // 2
    row, lane = iota(square, 0), iota(square, 1)
    same = row // block == lane // block
    pick = iota((modes, LANES), 0) == iota((modes, LANES), 1) % modes
    lag = iota((modes, LANES), 1).astype(F32)
    zero_row = jnp.zeros((1, LANES), F32)
    width = 2 * modes
    count = table_ref.shape[0]

    def along_lanes(x):
        return jnp.sum(jnp.where(pick, x, 0.0), 0, keepdims=True)

    def along_rows(x):
        return jnp.sum(jnp.where(row == lane, along_lanes(x), 0.0), 1, keepdims=True)

    def toeplitz(filter_row):
        wide = jnp.concatenate([filter_row, zero_row], 1)
        wide = jnp.broadcast_to(wide, (LANES, 2 * LANES))
        return pltpu.roll(wide, 0, 1, stride=1, stride_axis=0)

    for q in range(count):
        group = position * count + q
        mine = iota((modes, groups), 1) == group
        rate = jnp.sum(jnp.where(mine, decay_ref[...], 0.0), 1, keepdims=True)
        weight = jnp.sum(jnp.where(mine, residue_ref[...], 0.0), 1, keepdims=True)
        weight = weight * jnp.sqrt(2.0 * rate / modes)
        long_row = jnp.sum(weight * jnp.exp(-rate * lag), 0, keepdims=True)
        chosen = iota(medium_ref.shape, 0) == group
        medium_row = jnp.sum(jnp.where(chosen, medium_ref[...].astype(F32), 0.0), 0, keepdims=True)
        medium_wide = toeplitz(medium_row)
        near = jnp.where(same, medium_wide[:, :LANES] + toeplitz(long_row)[:, :LANES], 0.0)
        table_ref[q, 0], table_ref[q, 1] = split(near)
        middle = [medium_wide[:, block:LANES], medium_wide[:, LANES : LANES + block]]
        table_ref[q, 2] = jnp.where(same, jnp.concatenate(middle, 1), 0.0).astype(BF16)
        table_ref[q, 3] = jnp.where(same, medium_wide[:, LANES:], 0.0).astype(BF16)
        rate_lanes, rate_rows, weight_rows = along_lanes(rate), along_rows(rate), along_rows(weight)
        to_end = jnp.exp(-rate_lanes * (block - 1 - row % block).astype(F32))
        kept = (lane // modes) % 2 == row // block
        table_ref[q, 4], table_ref[q, 5] = split(jnp.where(kept, to_end, 0.0))
        from_start = weight_rows * jnp.exp(-rate_rows * (lane % block + 1).astype(F32))
        kept = ((row // modes) % 2 == lane // block) & (row < 3 * width)
        high, low = split(jnp.where(kept, from_start, 0.0))
        both = jnp.where(row < 2 * width, high.astype(F32), low.astype(F32))
        table_ref[q, 6] = both.astype(BF16)
        rows = slice(8 * q, 8 * q + 8)
        step_ref[rows] = jnp.broadcast_to(jnp.exp(-rate_lanes * block), (8, LANES))
        jump_ref[rows] = jnp.broadcast_to(jnp.exp(-rate_lanes * (block * NEAR)), (8, LANES))
        rest_ref[rows] = jnp.broadcast_to(jnp.exp(-rate_lanes * (block * (NEAR - 1))), (8, LANES))


def featurized(tap_ref, which, lanes, padded, rows):
    total = None
    for k in range(tap_ref.shape[1]):
        term = tap_ref[which, k : k + 1, lanes].astype(F32) * padded[HALO - k : HALO - k + rows, :]
        total = term if total is None else total + term
    return total


def tile_lanes(tile):
    return slice(tile * LANES, (tile + 1) * LANES)


def pack_kernel(inner_ref, value_ref, outer_ref, out_ref, tail_ref):
    tail_ref[...] = outer_ref[...]
    rows, channels = inner_ref.shape
    half = LANES // 2
    low = iota((rows, LANES), 1) < half
    for tile in range(channels // LANES):
        lanes = tile_lanes(tile)
        inner = inner_ref[:, lanes].astype(F32)
        value = value_ref[:, lanes].astype(F32)
        first = jnp.where(low, inner, pltpu.roll(value, half, 1))
        second = jnp.where(low, pltpu.roll(inner, half, 1), value)
        out_ref[2 * tile * rows : (2 * tile + 1) * rows] = first.astype(BF16)
        out_ref[(2 * tile + 1) * rows : (2 * tile + 2) * rows] = second.astype(BF16)


def outer_kernel(halo_ref, outer_ref, tap_ref, out_ref, padded):
    rows, channels = outer_ref.shape
    for tile in range(channels // LANES):
        lanes = tile_lanes(tile)
        padded[tile, :HALO] = halo_ref[:HALO, lanes].astype(F32)
        padded[tile, HALO:] = outer_ref[:, lanes].astype(F32)
        out_ref[:, lanes] = featurized(tap_ref, 0, lanes, padded.at[tile], rows)


def of_group(x, q, count):
    return x.reshape(x.shape[0] // (8 * count), count, 8, LANES)[:, q].reshape(-1, LANES)


def gated(tap_ref, padded, rows):
    total = None
    for k in range(FEAT):
        term = tap_ref[k : k + 1] * padded[HALO - k : HALO - k + rows]
        total = term if total is None else total + term
    return (total * pltpu.roll(total, LANES // 2, 1)).astype(BF16).astype(F32)


def slabs_of(product):
    both = jnp.concatenate([product, pltpu.roll(product, LANES - 8, 1)], 0).T
    return both.reshape(LANES // 16, 16, LANES)[:, :8].reshape(LANES // 2, LANES)


def missing(tap_ref, tail, head):
    block = LANES // 2
    product = gated(tap_ref, jnp.concatenate([tail[-HALO:], head[:HALO]], 0), HALO)
    kept = (iota(product.shape, 0) < FEAT - 1) & (iota(product.shape, 1) < block)
    product = jnp.where(kept, product, 0.0)
    return slabs_of(jnp.concatenate([product, jnp.zeros((block - HALO, LANES), F32)], 0))[: block // 2]


def to_states(table_ref, slab):
    count = table_ref.shape[0]
    parts = []
    for q in range(count):
        x = slab[8 * q : 8 * q + 8].astype(BF16)
        parts.append(dot(x, table_ref[q, 4]) + dot(x, table_ref[q, 5]))
    return jnp.concatenate(parts, 0)


def find_local(width, wide, table_ref, states, out_ref):
    count = table_ref.shape[0]
    zeros = jnp.zeros((8, LANES), F32)
    for q in range(count):
        x = of_group(wide, q, count)
        before = jnp.concatenate([zeros, x[:-8]], 0).astype(BF16)
        earlier = jnp.concatenate([zeros, zeros, x[:-16]], 0).astype(BF16)
        x = x.astype(BF16)
        mixed = dot(x, table_ref[q, 0]) + dot(x, table_ref[q, 1])
        mixed = mixed + dot(before, table_ref[q, 2]) + dot(earlier, table_ref[q, 3])
        mixed = mixed + dot(two_parts(of_group(states, q, count), width), table_ref[q, 6])
        for block in range(x.shape[0] // 8):
            at = 8 * (count * block + q)
            out_ref[at : at + 8] = mixed[8 * block : 8 * block + 8]


def find_states(
    width, later, raw_ref, tap_ref, table_ref, step_ref, local_ref, end_ref, send_ref, padded, state_ref
):
    count = table_ref.shape[0]
    block = LANES // 2
    blocks = raw_ref.shape[0] // block
    padded[:HALO] = jnp.zeros((HALO, LANES), F32)
    padded[HALO:] = raw_ref[...].astype(F32)
    low = iota((block, LANES), 1) < block
    early = (iota((block, LANES), 0) < FEAT - 1)
    rows = 8 * count
    slabs = []
    for pair in range(blocks // 2):
        products = []
        for b in (2 * pair, 2 * pair + 1):
            product = gated(tap_ref, padded.at[b * block : (b + 1) * block + HALO], block)
            products.append(jnp.where(early, 0.0, product) if later and b == 0 else product)
        slabs.append(slabs_of(jnp.where(low, products[0], products[1])))
    wide = jnp.concatenate(slabs, 0)
    ends = []
    for q in range(count):
        x = of_group(wide, q, count).astype(BF16)
        local = dot(x, table_ref[q, 4]) + dot(x, table_ref[q, 5])
        step = step_ref[8 * q : 8 * q + 8]
        carry = jnp.zeros((8, LANES), F32)
        for b in range(blocks):
            at = rows * b + 8 * q
            state_ref[at : at + 8] = carry
            carry = carry * step + local[8 * b : 8 * b + 8]
        ends.append(carry)
    end = jnp.concatenate(ends, 0)
    end_ref[...] = end
    at = rows // 2
    send_ref[:at] = pack_state(end, width)
    send_ref[at : at + 2 * rows] = wide[(blocks - 2) * rows :].astype(BF16)
    at = at + 2 * rows
    send_ref[at : at + EDGE] = raw_ref[blocks * block - EDGE :]
    if later:
        send_ref[at + EDGE :] = raw_ref[:EDGE]
    find_local(width, wide, table_ref, state_ref[...], local_ref)


def super_block(place):
    return lax.div(place[0], NEAR)


def first_states_kernel(width, place, *refs):
    raw_ref, tap_ref, table_ref, step_ref, local_ref, send_ref, padded, state_ref, end_ref = refs

    @pl.when(super_block(place) == 0)
    def _():
        known = (raw_ref, tap_ref, table_ref, step_ref)
        find_states(width, False, *known, local_ref, end_ref, send_ref, padded, state_ref)


def later_states_kernel(width, place, raw_ref, tap_ref, table_ref, step_ref, local_in, *refs):
    @pl.when(super_block(place) > 0)
    def _():
        find_states(width, True, raw_ref, tap_ref, table_ref, step_ref, *refs)


def chain_kernel(
    width,
    place,
    got_ref,
    raw_ref,
    tap_ref,
    table_ref,
    end_ref,
    jump_ref,
    rest_ref,
    send_ref,
    short_ref,
    next_ref,
):
    rows = end_ref.shape[0]

    @pl.when(super_block(place) == 1)
    def _():
        at = rows // 2 + 2 * rows
        tail = got_ref[at:].astype(F32)
        slab = missing(tap_ref, tail, raw_ref[:EDGE].astype(F32))
        end = end_ref[...] + rest_ref[...] * to_states(table_ref, slab)
        end = end + jump_ref[...] * unpack_state(got_ref[: rows // 2], width)
        state = pack_state(end, width)
        short_ref[: rows // 2] = state
        short_ref[rows // 2 :] = send_ref[at : at + EDGE]
        next_ref[: rows // 2] = state
        next_ref[rows // 2 :] = send_ref[rows // 2 : at + EDGE]


def spread(width, state, step, table, blocks, added=None):
    states = []
    for block in range(blocks):
        states.append(state)
        state = state * step
        if block == 0 and added is not None:
            state = state + added
    return dot(two_parts(jnp.concatenate(states, 0), width), table)


def joined(width, got, local_ref, raw_ref, tap_ref, table_ref, step_ref):
    count = table_ref.shape[0]
    rows = 8 * count
    blocks = local_ref.shape[0] // rows
    one, two, end = rows // 2, rows // 2 + rows, rows // 2 + 2 * rows
    own_slab = missing(tap_ref, got[end : end + EDGE], raw_ref[:EDGE].astype(F32))
    incoming = unpack_state(got[:one], width)
    added = to_states(table_ref, own_slab)
    zeros = jnp.zeros((8, LANES), F32)
    parts = []
    for q in range(count):
        at = slice(8 * q, 8 * q + 8)
        mixed = spread(width, incoming[at], step_ref[at], table_ref[q, 6], blocks, added[at])
        last_but_one, last, first = got[one:two][at], got[two:end][at], own_slab[at]
        now = jnp.concatenate([first, zeros, zeros, zeros], 0).astype(BF16)
        before = jnp.concatenate([last, first, zeros, zeros], 0).astype(BF16)
        earlier = jnp.concatenate([last_but_one, last, first, zeros], 0).astype(BF16)
        start = dot(now, table_ref[q, 0]) + dot(now, table_ref[q, 1])
        start = start + dot(before, table_ref[q, 2]) + dot(earlier, table_ref[q, 3])
        mixed = jnp.concatenate([mixed[:32] + start, mixed[32:]], 0)
        parts.append(mixed.reshape(blocks, 8, LANES))
    return local_ref[...] + jnp.concatenate(parts, 1).reshape(local_ref.shape)


def join_kernel(
    width, place, local_ref, got_01, got_23, raw_ref, tap_ref, table_ref, step_ref, out_ref
):
    @pl.when(lax.rem(super_block(place), 2) == 1)
    def _():
        got = got_01[...].astype(F32) + got_23[: got_01.shape[0]].astype(F32)
        out_ref[...] = joined(width, got, local_ref, raw_ref, tap_ref, table_ref, step_ref)


def finish_kernel(
    width,
    place,
    near_ref,
    got_12,
    got_23,
    got_13,
    raw_ref,
    tap_ref,
    table_ref,
    step_ref,
    jump_ref,
    rest_ref,
    out_ref,
):
    here = super_block(place)

    @pl.when(here < 2)
    def _():
        out_ref[...] = near_ref[...].astype(BF16)

    @pl.when(here == 2)
    def _():
        got = got_12[...].astype(F32)
        total = joined(width, got, near_ref, raw_ref, tap_ref, table_ref, step_ref)
        out_ref[...] = total.astype(BF16)

    @pl.when(here == 3)
    def _():
        count = table_ref.shape[0]
        rows = 8 * count
        blocks = near_ref.shape[0] // rows
        far_tail = got_13[rows // 2 :].astype(F32)
        head = got_23[got_23.shape[0] - EDGE :].astype(F32)
        incoming = rest_ref[...] * to_states(table_ref, missing(tap_ref, far_tail, head))
        incoming = incoming + jump_ref[...] * unpack_state(got_13[: rows // 2], width)
        parts = []
        for q in range(count):
            at = slice(8 * q, 8 * q + 8)
            mixed = spread(width, incoming[at], step_ref[at], table_ref[q, 6], blocks)
            parts.append(mixed.reshape(blocks, 8, LANES))
        total = near_ref[...] + jnp.concatenate(parts, 1).reshape(near_ref.shape)
        out_ref[...] = total.astype(BF16)


def hidden_kernel(mixed_ref, outer_ref, residual_ref, hidden_ref, sum_ref):
    rows, channels = outer_ref.shape
    squares = jnp.zeros((rows, LANES), F32)
    for tile in range(channels // LANES):
        lanes = tile_lanes(tile)
        slabs = mixed_ref[tile * (LANES // 2) : (tile + 1) * (LANES // 2)].astype(F32)
        other = pltpu.roll(slabs, LANES // 2, 1)
        groups = LANES // 16
        both = jnp.concatenate([slabs.reshape(groups, 8, LANES), other.reshape(groups, 8, LANES)], 1)
        mixed = both.reshape(LANES, LANES).T[:rows]
        hidden = residual_ref[:, lanes].astype(F32) + outer_ref[:, lanes] * mixed
        hidden_ref[:, lanes] = hidden
        squares = squares + hidden * hidden
    tall = jnp.concatenate([squares, jnp.zeros_like(squares)], 0).T
    line = jnp.sum(tall, 0, keepdims=True)
    sum_ref[...] = jnp.broadcast_to(line, sum_ref.shape)


def norm_kernel(hidden_ref, sum_ref, gain_ref, out_ref):
    rows, channels = hidden_ref.shape
    parts = sum_ref[...].reshape(sum_ref.shape[0] // 8, 8, LANES)
    line = jnp.sum(parts, 0)
    scale = 1.0 / jnp.sqrt(line / D + 1e-05)
    tall = jnp.broadcast_to(scale[:1], (LANES, LANES)).T[:rows]
    for tile in range(channels // LANES):
        lanes = slice(tile * LANES, (tile + 1) * LANES)
        out_ref[:, lanes] = (hidden_ref[:, lanes] * gain_ref[:, lanes] * tall).astype(BF16)


def on_device(
    outer_input,
    inner_input,
    value_input,
    feature_taps,
    medium_taps,
    decay_rates,
    residues,
    residual,
    norm_gain,
):
    rows, channels = outer_input.shape
    groups, modes = decay_rates.shape
    size = lax.axis_size("ctx")
    parts = lax.axis_size("tp")
    tiles = channels // LANES
    vmem = pl.BlockSpec(memory_space=pltpu.VMEM)
    smem = pl.BlockSpec(memory_space=pltpu.SMEM)

    def call(kernel, out, *arrays, scalars=(), scratch=(), aliases={}):
        return pl.pallas_call(
            kernel,
            in_specs=[smem] * len(scalars) + [vmem] * len(arrays),
            out_specs=jax.tree.map(lambda _: vmem, out),
            out_shape=out,
            scratch_shapes=scratch,
            input_output_aliases=aliases,
        )(*scalars, *in_vmem(*arrays))

    slab_rows = rows * channels // LANES
    count = groups // NEAR
    width = 2 * modes
    far = size // NEAR
    assert far == 4
    pack = 8 * count
    with_width = lambda kernel: functools.partial(kernel, width)

    part = pl.BlockSpec((rows, channels), lambda i: (0, 0))
    raw, outer_tail = pl.pallas_call(
        pack_kernel,
        grid=(1,),
        in_specs=[
            part,
            part,
            pl.BlockSpec((HALO, channels), lambda i: (rows // HALO - 1, 0)),
        ],
        out_specs=[vmem, vmem],
        out_shape=[pltpu.VMEM((NEAR * rows, LANES), BF16), pltpu.VMEM((HALO, channels), BF16)],
        name="pack",
    )(inner_input, value_input, outer_input)
    neighbours = [[NEAR * f + n for n in range(NEAR)] for f in range(far)]

    def exchange(x):
        slab = (NEAR, x.shape[0] // NEAR, LANES)
        y = lax.all_to_all(x.reshape(slab), "ctx", 0, 0, axis_index_groups=neighbours)
        return y.reshape(x.shape)

    arrived = exchange(raw)
    halo = lax.ppermute(outer_tail, "ctx", [(i, i + 1) for i in range(size - 1)])
    arrived, halo = lax.optimization_barrier((arrived, halo))
    place = lax.axis_index("ctx").reshape(1).astype(jnp.int32)
    table, step, jump, rest, taps, gain = call(
        tables_kernel,
        [
            pltpu.VMEM((count, 7, LANES, LANES), BF16),
            pltpu.VMEM((pack, LANES), F32),
            pltpu.VMEM((pack, LANES), F32),
            pltpu.VMEM((pack, LANES), F32),
            pltpu.VMEM((FEAT, LANES), F32),
            pltpu.VMEM((1, channels), F32),
        ],
        decay_rates.T,
        residues.T,
        medium_taps.T,
        feature_taps,
        norm_gain.reshape(1, channels),
        scalars=(place,),
    )
    outer_feat = call(
        outer_kernel,
        pltpu.VMEM((rows, channels), F32),
        halo,
        outer_input,
        feature_taps,
        scratch=[pltpu.VMEM((tiles, HALO + rows, LANES), F32)],
    )
    packet = pltpu.VMEM((pack // 2 + 2 * pack + EDGE, LANES), BF16)
    with_head = pltpu.VMEM((pack // 2 + 2 * pack + 2 * EDGE, LANES), BF16)
    whole = pltpu.VMEM((slab_rows, LANES), F32)
    ends = pltpu.VMEM((pack, LANES), F32)
    scratch = [pltpu.VMEM((HALO + NEAR * rows, LANES), F32), whole]
    known = (arrived, taps, table, step)
    local, first_packed = call(
        with_width(first_states_kernel),
        [whole, packet],
        *known,
        scalars=(place,),
        scratch=scratch + [ends],
    )
    local, end, packed = call(
        with_width(later_states_kernel),
        [whole, ends, with_head],
        *known,
        local,
        scalars=(place,),
        scratch=scratch,
        aliases={5: 0},
    )

    local, outer_feat = lax.optimization_barrier((local, outer_feat))

    def passed(x, start, end):
        pairs = [(NEAR * start + n, NEAR * end + n) for n in range(NEAR)]
        return lax.ppermute(x, "ctx", pairs)

    got_01 = passed(first_packed, 0, 1)
    got_23 = passed(packed, 2, 3)
    state, repacked = call(
        with_width(chain_kernel),
        [pltpu.VMEM((pack // 2 + EDGE, LANES), BF16), packet],
        got_01,
        arrived,
        taps,
        table,
        end,
        jump,
        rest,
        packed,
        scalars=(place,),
    )
    got_13 = passed(state, 1, 3)
    got_12 = passed(repacked, 1, 2)
    near = call(
        with_width(join_kernel),
        whole,
        local,
        got_01,
        got_23,
        arrived,
        taps,
        table,
        step,
        scalars=(place,),
        aliases={1: 0},
    )
    mixed = call(
        with_width(finish_kernel),
        pltpu.VMEM((slab_rows, LANES), BF16),
        near,
        got_12,
        got_23,
        got_13,
        arrived,
        taps,
        table,
        step,
        jump,
        rest,
        scalars=(place,),
    )
    hidden, sums = call(
        hidden_kernel,
        [pltpu.VMEM((rows, channels), F32), pltpu.VMEM((8 * parts, LANES), F32)],
        exchange(mixed),
        outer_feat,
        residual,
    )
    all_sums = lax.all_to_all(sums.reshape(parts, 8, LANES), "tp", 0, 0)
    return call(
        norm_kernel,
        jax.ShapeDtypeStruct((rows, channels), BF16),
        hidden,
        all_sums.reshape(8 * parts, LANES),
        gain,
    )


def solution(mesh):
    return jax.shard_map(
        on_device,
        mesh=mesh,
        in_specs=(
            P("ctx", "tp"),
            P("ctx", "tp"),
            P("ctx", "tp"),
            P(None, None, "tp"),
            P(None, "tp"),
            P("tp", None),
            P("tp", None),
            P("ctx", "tp"),
            P("tp"),
        ),
        out_specs=P("ctx", "tp"),
        check_vma=False,
    )
```

```python
import functools

import jax
import jax.numpy as jnp
from jax import lax
from jax.experimental import pallas as pl
from jax.experimental.pallas import tpu as pltpu
from jax.sharding import PartitionSpec as P


D = 8192
F32 = jnp.float32
BF16 = jnp.bfloat16
LANES = 128
HALO = 8
FEAT = 7
EDGE = 8
NEAR = 16


def iota(shape, axis):
    return lax.broadcasted_iota(jnp.int32, shape, axis)


def in_vmem(*arrays):
    return [pltpu.with_memory_space_constraint(a, pltpu.VMEM) for a in arrays]


def dot(a, b):
    return jnp.dot(a, b, preferred_element_type=F32)


def split(x):
    high = x.astype(BF16)
    return high, (x - high.astype(F32)).astype(BF16)


def pack_state(x, width):
    high, low = split(x)
    copy = iota(x.shape, 1) // width
    part = jnp.where(copy % 2 == 0, high.astype(F32), low.astype(F32))
    half = x.shape[0] // 2
    return jnp.where(copy[:half] < 2, part[:half], part[half:]).astype(BF16)


def unpack_state(packed, width):
    x = packed.astype(F32)
    both = x + pltpu.roll(x, width, 1)
    copy = iota(x.shape, 1) // width
    parts = []
    for place in (1, 3):
        y = jnp.where(copy == place, both, 0.0)
        y = y + pltpu.roll(y, width, 1)
        parts.append(y + pltpu.roll(y, 2 * width, 1))
    return jnp.concatenate(parts, 0)


def two_parts(x, width):
    high, low = split(x)
    copy = iota(x.shape, 1) // width
    return jnp.where(copy == 1, low.astype(F32), high.astype(F32)).astype(BF16)


def tables_kernel(
    place,
    decay_ref,
    residue_ref,
    medium_ref,
    tap_ref,
    table_ref,
    step_ref,
    jump_ref,
    rest_ref,
    mine_ref,
):
    channels = tap_ref.shape[2]
    half = LANES // 2
    at, to = iota((channels, LANES), 0), iota((channels, LANES), 1)
    position = lax.rem(place[0], NEAR)
    chosen = at == position * half + to % half
    for_inner = jnp.where(chosen & (to < half), 1.0, 0.0).astype(BF16)
    for_value = jnp.where(chosen & (to >= half), 1.0, 0.0).astype(BF16)
    mine_ref[...] = dot(tap_ref[1], for_inner) + dot(tap_ref[2], for_value)
    modes, groups = decay_ref.shape
    square = (LANES, LANES)
    block = LANES // 2
    row, lane = iota(square, 0), iota(square, 1)
    same = row // block == lane // block
    pick = iota((modes, LANES), 0) == iota((modes, LANES), 1) % modes
    lag = iota((modes, LANES), 1).astype(F32)
    zero_row = jnp.zeros((1, LANES), F32)
    width = 2 * modes
    count = table_ref.shape[0]

    def along_lanes(x):
        return jnp.sum(jnp.where(pick, x, 0.0), 0, keepdims=True)

    def along_rows(x):
        return jnp.sum(jnp.where(row == lane, along_lanes(x), 0.0), 1, keepdims=True)

    def toeplitz(filter_row):
        wide = jnp.concatenate([filter_row, zero_row], 1)
        wide = jnp.broadcast_to(wide, (LANES, 2 * LANES))
        return pltpu.roll(wide, 0, 1, stride=1, stride_axis=0)

    for q in range(count):
        group = position * count + q
        mine = iota((modes, groups), 1) == group
        rate = jnp.sum(jnp.where(mine, decay_ref[...], 0.0), 1, keepdims=True)
        weight = jnp.sum(jnp.where(mine, residue_ref[...], 0.0), 1, keepdims=True)
        weight = weight * jnp.sqrt(2.0 * rate / modes)
        long_row = jnp.sum(weight * jnp.exp(-rate * lag), 0, keepdims=True)
        chosen = iota(medium_ref.shape, 0) == group
        medium_row = jnp.sum(jnp.where(chosen, medium_ref[...].astype(F32), 0.0), 0, keepdims=True)
        medium_wide = toeplitz(medium_row)
        near = jnp.where(same, medium_wide[:, :LANES] + toeplitz(long_row)[:, :LANES], 0.0)
        table_ref[q, 0], table_ref[q, 1] = split(near)
        middle = [medium_wide[:, block:LANES], medium_wide[:, LANES : LANES + block]]
        table_ref[q, 2] = jnp.where(same, jnp.concatenate(middle, 1), 0.0).astype(BF16)
        table_ref[q, 3] = jnp.where(same, medium_wide[:, LANES:], 0.0).astype(BF16)
        rate_lanes, rate_rows, weight_rows = along_lanes(rate), along_rows(rate), along_rows(weight)
        to_end = jnp.exp(-rate_lanes * (block - 1 - row % block).astype(F32))
        kept = (lane // modes) % 2 == row // block
        table_ref[q, 4], table_ref[q, 5] = split(jnp.where(kept, to_end, 0.0))
        from_start = weight_rows * jnp.exp(-rate_rows * (lane % block + 1).astype(F32))
        kept = ((row // modes) % 2 == lane // block) & (row < 3 * width)
        high, low = split(jnp.where(kept, from_start, 0.0))
        both = jnp.where(row < 2 * width, high.astype(F32), low.astype(F32))
        table_ref[q, 6] = both.astype(BF16)
        rows = slice(8 * q, 8 * q + 8)
        step_ref[rows] = jnp.broadcast_to(jnp.exp(-rate_lanes * block), (8, LANES))
        jump_ref[rows] = jnp.broadcast_to(jnp.exp(-rate_lanes * (block * NEAR)), (8, LANES))
        rest_ref[rows] = jnp.broadcast_to(jnp.exp(-rate_lanes * (block * (NEAR - 1))), (8, LANES))


def begin_kernel(place, inner, value, outer, decay, residue, medium, taps, raw, tail, *tables):
    pack_kernel(inner, value, outer, raw, tail)
    tables_kernel(place, decay, residue, medium, taps, *tables)


def featurized(tap_ref, which, lanes, padded, rows):
    total = None
    for k in range(tap_ref.shape[1]):
        term = tap_ref[which, k : k + 1, lanes].astype(F32) * padded[HALO - k : HALO - k + rows, :]
        total = term if total is None else total + term
    return total


def tile_lanes(tile):
    return slice(tile * LANES, (tile + 1) * LANES)


def pack_kernel(inner_ref, value_ref, outer_ref, out_ref, tail_ref):
    tail_ref[...] = outer_ref[...]
    rows, channels = inner_ref.shape
    half = LANES // 2
    low = iota((rows, LANES), 1) < half
    for tile in range(channels // LANES):
        lanes = tile_lanes(tile)
        inner = inner_ref[:, lanes].astype(F32)
        value = value_ref[:, lanes].astype(F32)
        first = jnp.where(low, inner, pltpu.roll(value, half, 1))
        second = jnp.where(low, pltpu.roll(inner, half, 1), value)
        out_ref[2 * tile * rows : (2 * tile + 1) * rows] = first.astype(BF16)
        out_ref[(2 * tile + 1) * rows : (2 * tile + 2) * rows] = second.astype(BF16)


def outer_kernel(halo_ref, outer_ref, tap_ref, gain_in, out_ref, gain_ref, padded):
    gain_ref[...] = gain_in[...].astype(F32)
    rows, channels = outer_ref.shape
    for tile in range(channels // LANES):
        lanes = tile_lanes(tile)
        padded[tile, :HALO] = halo_ref[:HALO, lanes].astype(F32)
        padded[tile, HALO:] = outer_ref[:, lanes].astype(F32)
        out_ref[:, lanes] = featurized(tap_ref, 0, lanes, padded.at[tile], rows)


def of_group(x, q, count):
    return x.reshape(x.shape[0] // (8 * count), count, 8, LANES)[:, q].reshape(-1, LANES)


def gated(tap_ref, padded, rows):
    total = None
    for k in range(FEAT):
        term = tap_ref[k : k + 1] * padded[HALO - k : HALO - k + rows]
        total = term if total is None else total + term
    return (total * pltpu.roll(total, LANES // 2, 1)).astype(BF16).astype(F32)


def slabs_of(product):
    both = jnp.concatenate([product, pltpu.roll(product, LANES - 8, 1)], 0).T
    return both.reshape(LANES // 16, 16, LANES)[:, :8].reshape(LANES // 2, LANES)


def missing(tap_ref, tail, head):
    block = LANES // 2
    product = gated(tap_ref, jnp.concatenate([tail[-HALO:], head[:HALO]], 0), HALO)
    kept = (iota(product.shape, 0) < FEAT - 1) & (iota(product.shape, 1) < block)
    product = jnp.where(kept, product, 0.0)
    return slabs_of(jnp.concatenate([product, jnp.zeros((block - HALO, LANES), F32)], 0))[: block // 2]


def to_states(table_ref, slab):
    count = table_ref.shape[0]
    parts = []
    for q in range(count):
        x = slab[8 * q : 8 * q + 8].astype(BF16)
        parts.append(dot(x, table_ref[q, 4]) + dot(x, table_ref[q, 5]))
    return jnp.concatenate(parts, 0)


def find_local(width, wide, table_ref, states, out_ref):
    count = table_ref.shape[0]
    zeros = jnp.zeros((8, LANES), F32)
    for q in range(count):
        x = of_group(wide, q, count)
        before = jnp.concatenate([zeros, x[:-8]], 0).astype(BF16)
        earlier = jnp.concatenate([zeros, zeros, x[:-16]], 0).astype(BF16)
        x = x.astype(BF16)
        mixed = dot(x, table_ref[q, 0]) + dot(x, table_ref[q, 1])
        mixed = mixed + dot(before, table_ref[q, 2]) + dot(earlier, table_ref[q, 3])
        mixed = mixed + dot(two_parts(of_group(states, q, count), width), table_ref[q, 6])
        for block in range(x.shape[0] // 8):
            at = 8 * (count * block + q)
            out_ref[at : at + 8] = mixed[8 * block : 8 * block + 8]


def find_states(
    width, later, raw_ref, tap_ref, table_ref, step_ref, local_ref, end_ref, send_ref, padded, state_ref
):
    count = table_ref.shape[0]
    block = LANES // 2
    blocks = raw_ref.shape[0] // block
    padded[:HALO] = jnp.zeros((HALO, LANES), F32)
    padded[HALO:] = raw_ref[...].astype(F32)
    low = iota((block, LANES), 1) < block
    early = (iota((block, LANES), 0) < FEAT - 1)
    rows = 8 * count
    slabs = []
    for pair in range(blocks // 2):
        products = []
        for b in (2 * pair, 2 * pair + 1):
            product = gated(tap_ref, padded.at[b * block : (b + 1) * block + HALO], block)
            products.append(jnp.where(early, 0.0, product) if later and b == 0 else product)
        slabs.append(slabs_of(jnp.where(low, products[0], products[1])))
    wide = jnp.concatenate(slabs, 0)
    ends = []
    for q in range(count):
        x = of_group(wide, q, count).astype(BF16)
        local = dot(x, table_ref[q, 4]) + dot(x, table_ref[q, 5])
        step = step_ref[8 * q : 8 * q + 8]
        carry = jnp.zeros((8, LANES), F32)
        for b in range(blocks):
            at = rows * b + 8 * q
            state_ref[at : at + 8] = carry
            carry = carry * step + local[8 * b : 8 * b + 8]
        ends.append(carry)
    end = jnp.concatenate(ends, 0)
    end_ref[...] = end
    at = rows // 2
    send_ref[:at] = pack_state(end, width)
    send_ref[at : at + 2 * rows] = wide[(blocks - 2) * rows :].astype(BF16)
    at = at + 2 * rows
    send_ref[at : at + EDGE] = raw_ref[blocks * block - EDGE :]
    if send_ref.shape[0] > at + EDGE:
        send_ref[at + EDGE :] = raw_ref[:EDGE]
    find_local(width, wide, table_ref, state_ref[...], local_ref)


def super_block(place):
    return lax.div(place[0], NEAR)


def states_kernel(width, turn, place, raw_ref, tap_ref, table_ref, step_ref, *refs):
    if turn > 0:
        refs = refs[1:]
    if turn == 1:
        local_ref, end_ref, send_ref, padded, state_ref = refs
    elif turn == 3:
        local_ref, padded, state_ref, end_ref, send_ref = refs
    else:
        local_ref, send_ref, padded, state_ref, end_ref = refs

    @pl.when(super_block(place) == turn)
    def _():
        known = (raw_ref, tap_ref, table_ref, step_ref)
        find_states(width, turn > 0, *known, local_ref, end_ref, send_ref, padded, state_ref)


def chain_kernel(
    width,
    place,
    got_ref,
    raw_ref,
    tap_ref,
    table_ref,
    end_ref,
    jump_ref,
    rest_ref,
    send_ref,
    short_ref,
    next_ref,
):
    rows = end_ref.shape[0]

    @pl.when(super_block(place) == 1)
    def _():
        at = rows // 2 + 2 * rows
        tail = got_ref[at:].astype(F32)
        slab = missing(tap_ref, tail, raw_ref[:EDGE].astype(F32))
        end = end_ref[...] + rest_ref[...] * to_states(table_ref, slab)
        end = end + jump_ref[...] * unpack_state(got_ref[: rows // 2], width)
        state = pack_state(end, width)
        short_ref[: rows // 2] = state
        short_ref[rows // 2 :] = send_ref[at : at + EDGE]
        next_ref[: rows // 2] = state
        next_ref[rows // 2 :] = send_ref[rows // 2 : at + EDGE]


def spread(width, state, step, table, blocks, added=None):
    states = []
    for block in range(blocks):
        states.append(state)
        state = state * step
        if block == 0 and added is not None:
            state = state + added
    return dot(two_parts(jnp.concatenate(states, 0), width), table)


def joined(width, got, local_ref, raw_ref, tap_ref, table_ref, step_ref):
    count = table_ref.shape[0]
    rows = 8 * count
    blocks = local_ref.shape[0] // rows
    one, two, end = rows // 2, rows // 2 + rows, rows // 2 + 2 * rows
    own_slab = missing(tap_ref, got[end : end + EDGE], raw_ref[:EDGE].astype(F32))
    incoming = unpack_state(got[:one], width)
    added = to_states(table_ref, own_slab)
    zeros = jnp.zeros((8, LANES), F32)
    parts = []
    for q in range(count):
        at = slice(8 * q, 8 * q + 8)
        mixed = spread(width, incoming[at], step_ref[at], table_ref[q, 6], blocks, added[at])
        last_but_one, last, first = got[one:two][at], got[two:end][at], own_slab[at]
        now = jnp.concatenate([first, zeros, zeros, zeros], 0).astype(BF16)
        before = jnp.concatenate([last, first, zeros, zeros], 0).astype(BF16)
        earlier = jnp.concatenate([last_but_one, last, first, zeros], 0).astype(BF16)
        start = dot(now, table_ref[q, 0]) + dot(now, table_ref[q, 1])
        start = start + dot(before, table_ref[q, 2]) + dot(earlier, table_ref[q, 3])
        mixed = jnp.concatenate([mixed[:32] + start, mixed[32:]], 0)
        parts.append(mixed.reshape(blocks, 8, LANES))
    return local_ref[...] + jnp.concatenate(parts, 1).reshape(local_ref.shape)


def join_kernel(
    width, place, local_ref, got_01, got_23, raw_ref, tap_ref, table_ref, step_ref, out_ref
):
    @pl.when(lax.rem(super_block(place), 2) == 1)
    def _():
        got = got_01[...].astype(F32) + got_23[: got_01.shape[0]].astype(F32)
        out_ref[...] = joined(width, got, local_ref, raw_ref, tap_ref, table_ref, step_ref)


def finish_kernel(
    width,
    place,
    near_ref,
    got_12,
    got_23,
    got_13,
    raw_ref,
    tap_ref,
    table_ref,
    step_ref,
    jump_ref,
    rest_ref,
    out_ref,
):
    here = super_block(place)

    @pl.when(here < 2)
    def _():
        out_ref[...] = near_ref[...].astype(BF16)

    @pl.when(here == 2)
    def _():
        got = got_12[...].astype(F32)
        total = joined(width, got, near_ref, raw_ref, tap_ref, table_ref, step_ref)
        out_ref[...] = total.astype(BF16)

    @pl.when(here == 3)
    def _():
        count = table_ref.shape[0]
        rows = 8 * count
        blocks = near_ref.shape[0] // rows
        far_tail = got_13[rows // 2 :].astype(F32)
        head = got_23[got_23.shape[0] - EDGE :].astype(F32)
        incoming = rest_ref[...] * to_states(table_ref, missing(tap_ref, far_tail, head))
        incoming = incoming + jump_ref[...] * unpack_state(got_13[: rows // 2], width)
        parts = []
        for q in range(count):
            at = slice(8 * q, 8 * q + 8)
            mixed = spread(width, incoming[at], step_ref[at], table_ref[q, 6], blocks)
            parts.append(mixed.reshape(blocks, 8, LANES))
        total = near_ref[...] + jnp.concatenate(parts, 1).reshape(near_ref.shape)
        out_ref[...] = total.astype(BF16)


def hidden_kernel(mixed_ref, outer_ref, residual_ref, hidden_ref, sum_ref):
    rows, channels = outer_ref.shape
    squares = jnp.zeros((rows, LANES), F32)
    for tile in range(channels // LANES):
        lanes = tile_lanes(tile)
        slabs = mixed_ref[tile * (LANES // 2) : (tile + 1) * (LANES // 2)].astype(F32)
        other = pltpu.roll(slabs, LANES // 2, 1)
        groups = LANES // 16
        both = jnp.concatenate([slabs.reshape(groups, 8, LANES), other.reshape(groups, 8, LANES)], 1)
        mixed = both.reshape(LANES, LANES).T[:rows]
        hidden = residual_ref[:, lanes].astype(F32) + outer_ref[:, lanes] * mixed
        hidden_ref[:, lanes] = hidden
        squares = squares + hidden * hidden
    tall = jnp.concatenate([squares, jnp.zeros_like(squares)], 0).T
    line = jnp.sum(tall, 0, keepdims=True)
    sum_ref[...] = jnp.broadcast_to(line, sum_ref.shape)


def norm_kernel(hidden_ref, sum_ref, gain_ref, out_ref):
    rows, channels = hidden_ref.shape
    parts = sum_ref[...].reshape(sum_ref.shape[0] // 8, 8, LANES)
    line = jnp.sum(parts, 0)
    scale = 1.0 / jnp.sqrt(line / D + 1e-05)
    tall = jnp.broadcast_to(scale[:1], (LANES, LANES)).T[:rows]
    for tile in range(channels // LANES):
        lanes = slice(tile * LANES, (tile + 1) * LANES)
        out_ref[:, lanes] = (hidden_ref[:, lanes] * gain_ref[:, lanes] * tall).astype(BF16)


def on_device(
    outer_input,
    inner_input,
    value_input,
    feature_taps,
    medium_taps,
    decay_rates,
    residues,
    residual,
    norm_gain,
):
    rows, channels = outer_input.shape
    groups, modes = decay_rates.shape
    size = lax.axis_size("ctx")
    parts = lax.axis_size("tp")
    tiles = channels // LANES
    vmem = pl.BlockSpec(memory_space=pltpu.VMEM)
    smem = pl.BlockSpec(memory_space=pltpu.SMEM)

    def call(kernel, out, *arrays, scalars=(), scratch=(), aliases={}):
        return pl.pallas_call(
            kernel,
            in_specs=[smem] * len(scalars) + [vmem] * len(arrays),
            out_specs=jax.tree.map(lambda _: vmem, out),
            out_shape=out,
            scratch_shapes=scratch,
            input_output_aliases=aliases,
        )(*scalars, *in_vmem(*arrays))

    slab_rows = rows * channels // LANES
    count = groups // NEAR
    width = 2 * modes
    far = size // NEAR
    assert far == 4
    pack = 8 * count
    with_width = lambda kernel: functools.partial(kernel, width)

    place = lax.axis_index("ctx").reshape(1).astype(jnp.int32)
    small = (decay_rates.T, residues.T, medium_taps.T, feature_taps)
    part = pl.BlockSpec((rows, channels), lambda i: (0, 0))
    lines = pltpu.VMEM((pack, LANES), F32)
    raw, outer_tail, table, step, jump, rest, taps = pl.pallas_call(
        begin_kernel,
        grid=(1,),
        in_specs=[
            smem,
            part,
            part,
            pl.BlockSpec((HALO, channels), lambda i: (rows // HALO - 1, 0)),
            *[pl.BlockSpec(x.shape, lambda i, n=x.ndim: (0,) * n) for x in small],
        ],
        out_specs=[vmem] * 7,
        out_shape=[
            pltpu.VMEM((NEAR * rows, LANES), BF16),
            pltpu.VMEM((HALO, channels), BF16),
            pltpu.VMEM((count, 7, LANES, LANES), BF16),
            lines,
            lines,
            lines,
            pltpu.VMEM((FEAT, LANES), F32),
        ],
        name="begin",
    )(place, inner_input, value_input, outer_input, *small)
    neighbours = [[NEAR * f + n for n in range(NEAR)] for f in range(far)]

    def exchange(x):
        slab = (NEAR, x.shape[0] // NEAR, LANES)
        y = lax.all_to_all(x.reshape(slab), "ctx", 0, 0, axis_index_groups=neighbours)
        return y.reshape(x.shape)

    packet = pltpu.VMEM((pack // 2 + 2 * pack + EDGE, LANES), BF16)
    with_head = pltpu.VMEM((pack // 2 + 2 * pack + 2 * EDGE, LANES), BF16)
    whole = pltpu.VMEM((slab_rows, LANES), F32)
    ends = pltpu.VMEM((pack, LANES), F32)
    scratch = [pltpu.VMEM((HALO + NEAR * rows, LANES), F32), whole]
    here = lax.axis_index("ctx") // NEAR
    swap = lambda kept, fresh: exchange(fresh)
    keep = lambda kept, fresh: kept

    def find(turn, arrived, local, outs):
        unread = {1: [], 3: [ends, packet]}.get(turn, [ends])
        return call(
            functools.partial(states_kernel, width, turn),
            outs,
            arrived,
            taps,
            table,
            step,
            *([] if turn == 0 else [local]),
            scalars=(place,),
            scratch=scratch + unread,
            aliases={} if turn == 0 else {5: 0},
        )

    def passed(x, start, end):
        pairs = [(NEAR * start + n, NEAR * end + n) for n in range(NEAR)]
        return lax.ppermute(x, "ctx", pairs)

    arrived = lax.cond(here == 0, lambda x: exchange(x), lambda x: x, raw)
    local, first_packed = find(0, arrived, None, [whole, packet])
    got_01 = passed(first_packed, 0, 1)
    outer_tail, arrived = lax.optimization_barrier((outer_tail, arrived))
    halo = lax.ppermute(outer_tail, "ctx", [(i, i + 1) for i in range(size - 1)])
    arrived = lax.cond(here == 1, swap, keep, arrived, raw)
    local, end, packed = find(1, arrived, local, [whole, ends, packet])
    state, repacked = call(
        with_width(chain_kernel),
        [pltpu.VMEM((pack // 2 + EDGE, LANES), BF16), packet],
        got_01,
        arrived,
        taps,
        table,
        end,
        jump,
        rest,
        packed,
        scalars=(place,),
    )
    got_13 = passed(state, 1, 3)
    got_12 = passed(repacked, 1, 2)
    arrived = lax.cond(here == 2, swap, keep, arrived, raw)
    local, packed = find(2, arrived, local, [whole, with_head])
    got_23 = passed(packed, 2, 3)
    arrived = lax.cond(here == 3, swap, keep, arrived, raw)
    (local,) = find(3, arrived, local, [whole])
    norm_gain, local = lax.optimization_barrier((norm_gain, local))
    outer_feat, gain = call(
        outer_kernel,
        [pltpu.VMEM((rows, channels), F32), pltpu.VMEM((1, channels), F32)],
        halo,
        outer_input,
        feature_taps,
        norm_gain.reshape(1, channels),
        scratch=[pltpu.VMEM((tiles, HALO + rows, LANES), F32)],
    )

    local, outer_feat, gain = lax.optimization_barrier((local, outer_feat, gain))

    near = call(
        with_width(join_kernel),
        whole,
        local,
        got_01,
        got_23,
        arrived,
        taps,
        table,
        step,
        scalars=(place,),
        aliases={1: 0},
    )
    mixed = call(
        with_width(finish_kernel),
        pltpu.VMEM((slab_rows, LANES), BF16),
        near,
        got_12,
        got_23,
        got_13,
        arrived,
        taps,
        table,
        step,
        jump,
        rest,
        scalars=(place,),
    )
    hidden, sums = call(
        hidden_kernel,
        [pltpu.VMEM((rows, channels), F32), pltpu.VMEM((8 * parts, LANES), F32)],
        exchange(mixed),
        outer_feat,
        residual,
    )
    all_sums = lax.all_to_all(sums.reshape(parts, 8, LANES), "tp", 0, 0)
    return call(
        norm_kernel,
        jax.ShapeDtypeStruct((rows, channels), BF16),
        hidden,
        all_sums.reshape(8 * parts, LANES),
        gain,
    )


def solution(mesh):
    return jax.shard_map(
        on_device,
        mesh=mesh,
        in_specs=(
            P("ctx", "tp"),
            P("ctx", "tp"),
            P("ctx", "tp"),
            P(None, None, "tp"),
            P(None, "tp"),
            P("tp", None),
            P("tp", None),
            P("ctx", "tp"),
            P("tp"),
        ),
        out_specs=P("ctx", "tp"),
        check_vma=False,
    )
```

```python
import functools

import jax
import jax.numpy as jnp
from jax import lax
from jax.experimental import pallas as pl
from jax.experimental.pallas import tpu as pltpu
from jax.sharding import PartitionSpec as P


D = 8192
F32 = jnp.float32
BF16 = jnp.bfloat16
LANES = 128
HALO = 8
FEAT = 7
EDGE = 8
NEAR = 16


def iota(shape, axis):
    return lax.broadcasted_iota(jnp.int32, shape, axis)


def in_vmem(*arrays):
    return [pltpu.with_memory_space_constraint(a, pltpu.VMEM) for a in arrays]


def dot(a, b):
    return jnp.dot(a, b, preferred_element_type=F32)


def split(x):
    high = x.astype(BF16)
    return high, (x - high.astype(F32)).astype(BF16)


def pack_state(x, width):
    high, low = split(x)
    copy = iota(x.shape, 1) // width
    part = jnp.where(copy % 2 == 0, high.astype(F32), low.astype(F32))
    half = x.shape[0] // 2
    return jnp.where(copy[:half] < 2, part[:half], part[half:]).astype(BF16)


def unpack_state(packed, width):
    x = packed.astype(F32)
    both = x + pltpu.roll(x, width, 1)
    copy = iota(x.shape, 1) // width
    parts = []
    for place in (1, 3):
        y = jnp.where(copy == place, both, 0.0)
        y = y + pltpu.roll(y, width, 1)
        parts.append(y + pltpu.roll(y, 2 * width, 1))
    return jnp.concatenate(parts, 0)


def two_parts(x, width):
    high, low = split(x)
    copy = iota(x.shape, 1) // width
    return jnp.where(copy == 1, low.astype(F32), high.astype(F32)).astype(BF16)


def tables_kernel(
    place,
    decay_ref,
    residue_ref,
    medium_ref,
    tap_ref,
    table_ref,
    step_ref,
    jump_ref,
    rest_ref,
    mine_ref,
):
    channels = tap_ref.shape[2]
    half = LANES // 2
    at, to = iota((channels, LANES), 0), iota((channels, LANES), 1)
    position = lax.rem(place[0], NEAR)
    chosen = at == position * half + to % half
    for_inner = jnp.where(chosen & (to < half), 1.0, 0.0).astype(BF16)
    for_value = jnp.where(chosen & (to >= half), 1.0, 0.0).astype(BF16)
    mine_ref[...] = dot(tap_ref[1], for_inner) + dot(tap_ref[2], for_value)
    modes, groups = decay_ref.shape
    square = (LANES, LANES)
    block = LANES // 2
    row, lane = iota(square, 0), iota(square, 1)
    same = row // block == lane // block
    pick = iota((modes, LANES), 0) == iota((modes, LANES), 1) % modes
    lag = iota((modes, LANES), 1).astype(F32)
    zero_row = jnp.zeros((1, LANES), F32)
    width = 2 * modes
    count = table_ref.shape[0]

    def along_lanes(x):
        return jnp.sum(jnp.where(pick, x, 0.0), 0, keepdims=True)

    def along_rows(x):
        return jnp.sum(jnp.where(row == lane, along_lanes(x), 0.0), 1, keepdims=True)

    def toeplitz(filter_row):
        wide = jnp.concatenate([filter_row, zero_row], 1)
        wide = jnp.broadcast_to(wide, (LANES, 2 * LANES))
        return pltpu.roll(wide, 0, 1, stride=1, stride_axis=0)

    for q in range(count):
        group = position * count + q
        mine = iota((modes, groups), 1) == group
        rate = jnp.sum(jnp.where(mine, decay_ref[...], 0.0), 1, keepdims=True)
        weight = jnp.sum(jnp.where(mine, residue_ref[...], 0.0), 1, keepdims=True)
        weight = weight * jnp.sqrt(2.0 * rate / modes)
        long_row = jnp.sum(weight * jnp.exp(-rate * lag), 0, keepdims=True)
        chosen = iota(medium_ref.shape, 0) == group
        medium_row = jnp.sum(jnp.where(chosen, medium_ref[...].astype(F32), 0.0), 0, keepdims=True)
        medium_wide = toeplitz(medium_row)
        near = jnp.where(same, medium_wide[:, :LANES] + toeplitz(long_row)[:, :LANES], 0.0)
        table_ref[q, 0], table_ref[q, 1] = split(near)
        middle = [medium_wide[:, block:LANES], medium_wide[:, LANES : LANES + block]]
        table_ref[q, 2] = jnp.where(same, jnp.concatenate(middle, 1), 0.0).astype(BF16)
        table_ref[q, 3] = jnp.where(same, medium_wide[:, LANES:], 0.0).astype(BF16)
        rate_lanes, rate_rows, weight_rows = along_lanes(rate), along_rows(rate), along_rows(weight)
        to_end = jnp.exp(-rate_lanes * (block - 1 - row % block).astype(F32))
        kept = (lane // modes) % 2 == row // block
        table_ref[q, 4], table_ref[q, 5] = split(jnp.where(kept, to_end, 0.0))
        from_start = weight_rows * jnp.exp(-rate_rows * (lane % block + 1).astype(F32))
        kept = ((row // modes) % 2 == lane // block) & (row < 3 * width)
        high, low = split(jnp.where(kept, from_start, 0.0))
        both = jnp.where(row < 2 * width, high.astype(F32), low.astype(F32))
        table_ref[q, 6] = both.astype(BF16)
        rows = slice(8 * q, 8 * q + 8)
        step_ref[rows] = jnp.broadcast_to(jnp.exp(-rate_lanes * block), (8, LANES))
        jump_ref[rows] = jnp.broadcast_to(jnp.exp(-rate_lanes * (block * NEAR)), (8, LANES))
        rest_ref[rows] = jnp.broadcast_to(jnp.exp(-rate_lanes * (block * (NEAR - 1))), (8, LANES))


def begin_kernel(
    place, inner, value, outer, gain, decay, residue, medium, taps, raw, tail, outer_out, tap_out, gain_out, *tables
):
    outer_out[...] = outer[...]
    tap_out[0] = taps[0].astype(F32)
    gain_out[...] = gain[...]
    pack_kernel(inner, value, outer.at[outer.shape[0] - HALO :], raw, tail)
    tables_kernel(place, decay, residue, medium, taps, *tables)


def featurized(tap_ref, which, lanes, padded, rows):
    total = None
    for k in range(tap_ref.shape[1]):
        term = tap_ref[which, k : k + 1, lanes].astype(F32) * padded[HALO - k : HALO - k + rows, :]
        total = term if total is None else total + term
    return total


def tile_lanes(tile):
    return slice(tile * LANES, (tile + 1) * LANES)


def pack_kernel(inner_ref, value_ref, outer_ref, out_ref, tail_ref):
    tail_ref[...] = outer_ref[...]
    rows, channels = inner_ref.shape
    half = LANES // 2
    low = iota((rows, LANES), 1) < half
    for tile in range(channels // LANES):
        lanes = tile_lanes(tile)
        inner = inner_ref[:, lanes].astype(F32)
        value = value_ref[:, lanes].astype(F32)
        first = jnp.where(low, inner, pltpu.roll(value, half, 1))
        second = jnp.where(low, pltpu.roll(inner, half, 1), value)
        out_ref[2 * tile * rows : (2 * tile + 1) * rows] = first.astype(BF16)
        out_ref[(2 * tile + 1) * rows : (2 * tile + 2) * rows] = second.astype(BF16)


def outer_kernel(halo_ref, outer_ref, tap_ref, gain_in, out_ref, gain_ref, padded):
    gain_ref[...] = gain_in[...].astype(F32)
    rows, channels = outer_ref.shape
    for tile in range(channels // LANES):
        lanes = tile_lanes(tile)
        padded[tile, :HALO] = halo_ref[:HALO, lanes].astype(F32)
        padded[tile, HALO:] = outer_ref[:, lanes].astype(F32)
        out_ref[:, lanes] = featurized(tap_ref, 0, lanes, padded.at[tile], rows)


def of_group(x, q, count):
    return x.reshape(x.shape[0] // (8 * count), count, 8, LANES)[:, q].reshape(-1, LANES)


def gated(tap_ref, padded, rows):
    total = None
    for k in range(FEAT):
        term = tap_ref[k : k + 1] * padded[HALO - k : HALO - k + rows]
        total = term if total is None else total + term
    return (total * pltpu.roll(total, LANES // 2, 1)).astype(BF16).astype(F32)


def slabs_of(product):
    both = jnp.concatenate([product, pltpu.roll(product, LANES - 8, 1)], 0).T
    return both.reshape(LANES // 16, 16, LANES)[:, :8].reshape(LANES // 2, LANES)


def missing(tap_ref, tail, head):
    block = LANES // 2
    product = gated(tap_ref, jnp.concatenate([tail[-HALO:], head[:HALO]], 0), HALO)
    kept = (iota(product.shape, 0) < FEAT - 1) & (iota(product.shape, 1) < block)
    product = jnp.where(kept, product, 0.0)
    return slabs_of(jnp.concatenate([product, jnp.zeros((block - HALO, LANES), F32)], 0))[: block // 2]


def to_states(table_ref, slab):
    count = table_ref.shape[0]
    parts = []
    for q in range(count):
        x = slab[8 * q : 8 * q + 8].astype(BF16)
        parts.append(dot(x, table_ref[q, 4]) + dot(x, table_ref[q, 5]))
    return jnp.concatenate(parts, 0)


def find_local(width, wide, table_ref, states, out_ref):
    count = table_ref.shape[0]
    zeros = jnp.zeros((8, LANES), F32)
    for q in range(count):
        x = of_group(wide, q, count)
        before = jnp.concatenate([zeros, x[:-8]], 0).astype(BF16)
        earlier = jnp.concatenate([zeros, zeros, x[:-16]], 0).astype(BF16)
        x = x.astype(BF16)
        mixed = dot(x, table_ref[q, 0]) + dot(x, table_ref[q, 1])
        mixed = mixed + dot(before, table_ref[q, 2]) + dot(earlier, table_ref[q, 3])
        mixed = mixed + dot(two_parts(of_group(states, q, count), width), table_ref[q, 6])
        for block in range(x.shape[0] // 8):
            at = 8 * (count * block + q)
            out_ref[at : at + 8] = mixed[8 * block : 8 * block + 8]


def find_states(
    width, later, raw_ref, tap_ref, table_ref, step_ref, local_ref, end_ref, send_ref, padded, state_ref
):
    count = table_ref.shape[0]
    block = LANES // 2
    blocks = raw_ref.shape[0] // block
    padded[:HALO] = jnp.zeros((HALO, LANES), F32)
    padded[HALO:] = raw_ref[...].astype(F32)
    low = iota((block, LANES), 1) < block
    early = (iota((block, LANES), 0) < FEAT - 1)
    rows = 8 * count
    slabs = []
    for pair in range(blocks // 2):
        products = []
        for b in (2 * pair, 2 * pair + 1):
            product = gated(tap_ref, padded.at[b * block : (b + 1) * block + HALO], block)
            products.append(jnp.where(early, 0.0, product) if later and b == 0 else product)
        slabs.append(slabs_of(jnp.where(low, products[0], products[1])))
    wide = jnp.concatenate(slabs, 0)
    ends = []
    for q in range(count):
        x = of_group(wide, q, count).astype(BF16)
        local = dot(x, table_ref[q, 4]) + dot(x, table_ref[q, 5])
        step = step_ref[8 * q : 8 * q + 8]
        carry = jnp.zeros((8, LANES), F32)
        for b in range(blocks):
            at = rows * b + 8 * q
            state_ref[at : at + 8] = carry
            carry = carry * step + local[8 * b : 8 * b + 8]
        ends.append(carry)
    end = jnp.concatenate(ends, 0)
    end_ref[...] = end
    at = rows // 2
    send_ref[:at] = pack_state(end, width)
    send_ref[at : at + 2 * rows] = wide[(blocks - 2) * rows :].astype(BF16)
    at = at + 2 * rows
    send_ref[at : at + EDGE] = raw_ref[blocks * block - EDGE :]
    if send_ref.shape[0] > at + EDGE:
        send_ref[at + EDGE :] = raw_ref[:EDGE]
    find_local(width, wide, table_ref, state_ref[...], local_ref)


def super_block(place):
    return lax.div(place[0], NEAR)


def states_kernel(width, turn, place, raw_ref, tap_ref, table_ref, step_ref, *refs):
    if turn > 0:
        refs = refs[1:]
    if turn == 1:
        local_ref, end_ref, send_ref, padded, state_ref = refs
    elif turn == 3:
        local_ref, padded, state_ref, end_ref, send_ref = refs
    else:
        local_ref, send_ref, padded, state_ref, end_ref = refs

    @pl.when(super_block(place) == turn)
    def _():
        known = (raw_ref, tap_ref, table_ref, step_ref)
        find_states(width, turn > 0, *known, local_ref, end_ref, send_ref, padded, state_ref)


def chain_kernel(
    width,
    place,
    got_ref,
    raw_ref,
    tap_ref,
    table_ref,
    end_ref,
    jump_ref,
    rest_ref,
    send_ref,
    short_ref,
    next_ref,
):
    rows = end_ref.shape[0]

    @pl.when(super_block(place) == 1)
    def _():
        at = rows // 2 + 2 * rows
        tail = got_ref[at:].astype(F32)
        slab = missing(tap_ref, tail, raw_ref[:EDGE].astype(F32))
        end = end_ref[...] + rest_ref[...] * to_states(table_ref, slab)
        end = end + jump_ref[...] * unpack_state(got_ref[: rows // 2], width)
        state = pack_state(end, width)
        short_ref[: rows // 2] = state
        short_ref[rows // 2 :] = send_ref[at : at + EDGE]
        next_ref[: rows // 2] = state
        next_ref[rows // 2 :] = send_ref[rows // 2 : at + EDGE]


def spread(width, state, step, table, blocks, added=None):
    states = []
    for block in range(blocks):
        states.append(state)
        state = state * step
        if block == 0 and added is not None:
            state = state + added
    return dot(two_parts(jnp.concatenate(states, 0), width), table)


def joined(width, got, farther, local_ref, raw_ref, tap_ref, table_ref, step_ref):
    count = table_ref.shape[0]
    rows = 8 * count
    blocks = local_ref.shape[0] // rows
    one, two, end = rows // 2, rows // 2 + rows, rows // 2 + 2 * rows
    own_slab = missing(tap_ref, got[end : end + EDGE], raw_ref[:EDGE].astype(F32))
    incoming = unpack_state(got[:one], width) + farther
    added = to_states(table_ref, own_slab)
    zeros = jnp.zeros((8, LANES), F32)
    parts = []
    for q in range(count):
        at = slice(8 * q, 8 * q + 8)
        mixed = spread(width, incoming[at], step_ref[at], table_ref[q, 6], blocks, added[at])
        last_but_one, last, first = got[one:two][at], got[two:end][at], own_slab[at]
        now = jnp.concatenate([first, zeros, zeros, zeros], 0).astype(BF16)
        before = jnp.concatenate([last, first, zeros, zeros], 0).astype(BF16)
        earlier = jnp.concatenate([last_but_one, last, first, zeros], 0).astype(BF16)
        start = dot(now, table_ref[q, 0]) + dot(now, table_ref[q, 1])
        start = start + dot(before, table_ref[q, 2]) + dot(earlier, table_ref[q, 3])
        mixed = jnp.concatenate([mixed[:32] + start, mixed[32:]], 0)
        parts.append(mixed.reshape(blocks, 8, LANES))
    return local_ref[...] + jnp.concatenate(parts, 1).reshape(local_ref.shape)


def join_kernel(width, place, local_ref, got_01, raw_ref, tap_ref, table_ref, step_ref, out_ref):
    @pl.when(super_block(place) == 1)
    def _():
        got = got_01[...].astype(F32)
        out_ref[...] = joined(width, got, 0.0, local_ref, raw_ref, tap_ref, table_ref, step_ref)


def finish_kernel(
    width,
    place,
    near_ref,
    got_12,
    got_23,
    got_13,
    raw_ref,
    tap_ref,
    table_ref,
    step_ref,
    jump_ref,
    rest_ref,
    out_ref,
    farther,
):
    here = super_block(place)
    half = farther.shape[0] // 2

    @pl.when(here < 2)
    def _():
        out_ref[...] = near_ref[...].astype(BF16)

    @pl.when(here == 2)
    def _():
        farther[...] = jnp.zeros_like(farther)

    @pl.when(here == 3)
    def _():
        tail = got_13[half:].astype(F32)
        head = got_23[got_23.shape[0] - EDGE :].astype(F32)
        incoming = rest_ref[...] * to_states(table_ref, missing(tap_ref, tail, head))
        farther[...] = incoming + jump_ref[...] * unpack_state(got_13[:half], width)

    @pl.when(here > 1)
    def _():
        got = got_12[...].astype(F32) + got_23[: got_12.shape[0]].astype(F32)
        known = (near_ref, raw_ref, tap_ref, table_ref, step_ref)
        out_ref[...] = joined(width, got, farther[...], *known).astype(BF16)


def hidden_kernel(mixed_ref, outer_ref, residual_ref, hidden_ref, sum_ref):
    rows, channels = outer_ref.shape
    squares = jnp.zeros((rows, LANES), F32)
    for tile in range(channels // LANES):
        lanes = tile_lanes(tile)
        slabs = mixed_ref[tile * (LANES // 2) : (tile + 1) * (LANES // 2)].astype(F32)
        other = pltpu.roll(slabs, LANES // 2, 1)
        groups = LANES // 16
        both = jnp.concatenate([slabs.reshape(groups, 8, LANES), other.reshape(groups, 8, LANES)], 1)
        mixed = both.reshape(LANES, LANES).T[:rows]
        hidden = residual_ref[:, lanes].astype(F32) + outer_ref[:, lanes] * mixed
        hidden_ref[:, lanes] = hidden
        squares = squares + hidden * hidden
    tall = jnp.concatenate([squares, jnp.zeros_like(squares)], 0).T
    line = jnp.sum(tall, 0, keepdims=True)
    sum_ref[...] = jnp.broadcast_to(line, sum_ref.shape)


def norm_kernel(hidden_ref, sum_ref, gain_ref, out_ref):
    rows, channels = hidden_ref.shape
    parts = sum_ref[...].reshape(sum_ref.shape[0] // 8, 8, LANES)
    line = jnp.sum(parts, 0)
    scale = 1.0 / jnp.sqrt(line / D + 1e-05)
    tall = jnp.broadcast_to(scale[:1], (LANES, LANES)).T[:rows]
    for tile in range(channels // LANES):
        lanes = slice(tile * LANES, (tile + 1) * LANES)
        out_ref[:, lanes] = (hidden_ref[:, lanes] * gain_ref[:, lanes] * tall).astype(BF16)


def on_device(
    outer_input,
    inner_input,
    value_input,
    feature_taps,
    medium_taps,
    decay_rates,
    residues,
    residual,
    norm_gain,
):
    rows, channels = outer_input.shape
    groups, modes = decay_rates.shape
    size = lax.axis_size("ctx")
    parts = lax.axis_size("tp")
    tiles = channels // LANES
    vmem = pl.BlockSpec(memory_space=pltpu.VMEM)
    smem = pl.BlockSpec(memory_space=pltpu.SMEM)

    def call(kernel, out, *arrays, scalars=(), scratch=(), aliases={}):
        return pl.pallas_call(
            kernel,
            in_specs=[smem] * len(scalars) + [vmem] * len(arrays),
            out_specs=jax.tree.map(lambda _: vmem, out),
            out_shape=out,
            scratch_shapes=scratch,
            input_output_aliases=aliases,
        )(*scalars, *in_vmem(*arrays))

    slab_rows = rows * channels // LANES
    count = groups // NEAR
    width = 2 * modes
    far = size // NEAR
    assert far == 4
    pack = 8 * count
    with_width = lambda kernel: functools.partial(kernel, width)

    place = lax.axis_index("ctx").reshape(1).astype(jnp.int32)
    small = (decay_rates.T, residues.T, medium_taps.T, feature_taps)
    part = pl.BlockSpec((rows, channels), lambda i: (0, 0))
    lines = pltpu.VMEM((pack, LANES), F32)
    raw, outer_tail, outer_input, outer_taps, norm_gain, table, step, jump, rest, taps = pl.pallas_call(
        begin_kernel,
        grid=(1,),
        in_specs=[
            smem,
            part,
            part,
            part,
            pl.BlockSpec((channels,), lambda i: (0,)),
            *[pl.BlockSpec(x.shape, lambda i, n=x.ndim: (0,) * n) for x in small],
        ],
        out_specs=[vmem] * 10,
        out_shape=[
            pltpu.VMEM((NEAR * rows, LANES), BF16),
            pltpu.VMEM((HALO, channels), BF16),
            pltpu.VMEM((rows, channels), BF16),
            pltpu.VMEM((1, FEAT, channels), F32),
            pltpu.VMEM((channels,), BF16),
            pltpu.VMEM((count, 7, LANES, LANES), BF16),
            lines,
            lines,
            lines,
            pltpu.VMEM((FEAT, LANES), F32),
        ],
        name="begin",
    )(place, inner_input, value_input, outer_input, norm_gain, *small)
    neighbours = [[NEAR * f + n for n in range(NEAR)] for f in range(far)]

    def exchange(x):
        slab = (NEAR, x.shape[0] // NEAR, LANES)
        y = lax.all_to_all(x.reshape(slab), "ctx", 0, 0, axis_index_groups=neighbours)
        return y.reshape(x.shape)

    packet = pltpu.VMEM((pack // 2 + 2 * pack + EDGE, LANES), BF16)
    with_head = pltpu.VMEM((pack // 2 + 2 * pack + 2 * EDGE, LANES), BF16)
    whole = pltpu.VMEM((slab_rows, LANES), F32)
    ends = pltpu.VMEM((pack, LANES), F32)
    scratch = [pltpu.VMEM((HALO + NEAR * rows, LANES), F32), whole]
    here = lax.axis_index("ctx") // NEAR
    swap = lambda kept, fresh: exchange(fresh)
    keep = lambda kept, fresh: kept

    def find(turn, arrived, local, outs):
        unread = {1: [], 3: [ends, packet]}.get(turn, [ends])
        return call(
            functools.partial(states_kernel, width, turn),
            outs,
            arrived,
            taps,
            table,
            step,
            *([] if turn == 0 else [local]),
            scalars=(place,),
            scratch=scratch + unread,
            aliases={} if turn == 0 else {5: 0},
        )

    def passed(x, start, end):
        pairs = [(NEAR * start + n, NEAR * end + n) for n in range(NEAR)]
        return lax.ppermute(x, "ctx", pairs)

    arrived = lax.cond(here == 0, lambda x: exchange(x), lambda x: x, raw)
    local, first_packed = find(0, arrived, None, [whole, packet])
    got_01 = passed(first_packed, 0, 1)
    outer_tail, arrived = lax.optimization_barrier((outer_tail, arrived))
    halo = lax.ppermute(outer_tail, "ctx", [(i, i + 1) for i in range(size - 1)])
    arrived = lax.cond(here == 1, swap, keep, arrived, raw)
    local, end, packed = find(1, arrived, local, [whole, ends, packet])
    state, repacked = call(
        with_width(chain_kernel),
        [pltpu.VMEM((pack // 2 + EDGE, LANES), BF16), packet],
        got_01,
        arrived,
        taps,
        table,
        end,
        jump,
        rest,
        packed,
        scalars=(place,),
    )
    got_13 = passed(state, 1, 3)
    got_12 = passed(repacked, 1, 2)
    arrived = lax.cond(here == 2, swap, keep, arrived, raw)
    local, packed = find(2, arrived, local, [whole, with_head])
    got_23 = passed(packed, 2, 3)
    arrived = lax.cond(here == 3, swap, keep, arrived, raw)
    (local,) = find(3, arrived, local, [whole])
    norm_gain, local = lax.optimization_barrier((norm_gain, local))
    outer_feat, gain = call(
        outer_kernel,
        [pltpu.VMEM((rows, channels), F32), pltpu.VMEM((1, channels), F32)],
        halo,
        outer_input,
        outer_taps,
        norm_gain.reshape(1, channels),
        scratch=[pltpu.VMEM((tiles, HALO + rows, LANES), F32)],
    )

    local, outer_feat, gain = lax.optimization_barrier((local, outer_feat, gain))

    near = call(
        with_width(join_kernel),
        whole,
        local,
        got_01,
        arrived,
        taps,
        table,
        step,
        scalars=(place,),
        aliases={1: 0},
    )
    mixed = call(
        with_width(finish_kernel),
        pltpu.VMEM((slab_rows, LANES), BF16),
        near,
        got_12,
        got_23,
        got_13,
        arrived,
        taps,
        table,
        step,
        jump,
        rest,
        scalars=(place,),
        scratch=[ends],
    )
    hidden, sums = call(
        hidden_kernel,
        [pltpu.VMEM((rows, channels), F32), pltpu.VMEM((8 * parts, LANES), F32)],
        exchange(mixed),
        outer_feat,
        residual,
    )
    all_sums = lax.all_to_all(sums.reshape(parts, 8, LANES), "tp", 0, 0)
    return call(
        norm_kernel,
        jax.ShapeDtypeStruct((rows, channels), BF16),
        hidden,
        all_sums.reshape(8 * parts, LANES),
        gain,
    )


def solution(mesh):
    return jax.shard_map(
        on_device,
        mesh=mesh,
        in_specs=(
            P("ctx", "tp"),
            P("ctx", "tp"),
            P("ctx", "tp"),
            P(None, None, "tp"),
            P(None, "tp"),
            P("tp", None),
            P("tp", None),
            P("ctx", "tp"),
            P("tp"),
        ),
        out_specs=P("ctx", "tp"),
        check_vma=False,
    )
```

```python
import functools

import jax
import jax.numpy as jnp
from jax import lax
from jax.experimental import pallas as pl
from jax.experimental.pallas import tpu as pltpu
from jax.sharding import PartitionSpec as P


D = 8192
F32 = jnp.float32
BF16 = jnp.bfloat16
LANES = 128
HALO = 8
FEAT = 7
EDGE = 8
NEAR = 16


def iota(shape, axis):
    return lax.broadcasted_iota(jnp.int32, shape, axis)


def in_vmem(*arrays):
    return [pltpu.with_memory_space_constraint(a, pltpu.VMEM) for a in arrays]


def dot(a, b):
    return jnp.dot(a, b, preferred_element_type=F32)


def split(x):
    high = x.astype(BF16)
    return high, (x - high.astype(F32)).astype(BF16)


def pack_state(x, width):
    high, low = split(x)
    copy = iota(x.shape, 1) // width
    part = jnp.where(copy % 2 == 0, high.astype(F32), low.astype(F32))
    half = x.shape[0] // 2
    return jnp.where(copy[:half] < 2, part[:half], part[half:]).astype(BF16)


def unpack_state(packed, width):
    x = packed.astype(F32)
    both = x + pltpu.roll(x, width, 1)
    copy = iota(x.shape, 1) // width
    parts = []
    for place in (1, 3):
        y = jnp.where(copy == place, both, 0.0)
        y = y + pltpu.roll(y, width, 1)
        parts.append(y + pltpu.roll(y, 2 * width, 1))
    return jnp.concatenate(parts, 0)


def two_parts(x, width):
    high, low = split(x)
    copy = iota(x.shape, 1) // width
    return jnp.where(copy == 1, low.astype(F32), high.astype(F32)).astype(BF16)


def tables_kernel(
    place,
    decay_ref,
    residue_ref,
    medium_ref,
    tap_ref,
    table_ref,
    step_ref,
    jump_ref,
    rest_ref,
    mine_ref,
):
    channels = tap_ref.shape[2]
    half = LANES // 2
    at, to = iota((channels, LANES), 0), iota((channels, LANES), 1)
    position = lax.rem(place[0], NEAR)
    chosen = at == position * half + to % half
    for_inner = jnp.where(chosen & (to < half), 1.0, 0.0).astype(BF16)
    for_value = jnp.where(chosen & (to >= half), 1.0, 0.0).astype(BF16)
    mine_ref[...] = dot(tap_ref[1], for_inner) + dot(tap_ref[2], for_value)
    modes, groups = decay_ref.shape
    square = (LANES, LANES)
    block = LANES // 2
    row, lane = iota(square, 0), iota(square, 1)
    same = row // block == lane // block
    pick = iota((modes, LANES), 0) == iota((modes, LANES), 1) % modes
    lag = iota((modes, LANES), 1).astype(F32)
    zero_row = jnp.zeros((1, LANES), F32)
    width = 2 * modes
    count = table_ref.shape[0]

    def along_lanes(x):
        return jnp.sum(jnp.where(pick, x, 0.0), 0, keepdims=True)

    def along_rows(x):
        return jnp.sum(jnp.where(row == lane, along_lanes(x), 0.0), 1, keepdims=True)

    def toeplitz(filter_row):
        wide = jnp.concatenate([filter_row, zero_row], 1)
        wide = jnp.broadcast_to(wide, (LANES, 2 * LANES))
        return pltpu.roll(wide, 0, 1, stride=1, stride_axis=0)

    for q in range(count):
        group = position * count + q
        mine = iota((modes, groups), 1) == group
        rate = jnp.sum(jnp.where(mine, decay_ref[...], 0.0), 1, keepdims=True)
        weight = jnp.sum(jnp.where(mine, residue_ref[...], 0.0), 1, keepdims=True)
        weight = weight * jnp.sqrt(2.0 * rate / modes)
        long_row = jnp.sum(weight * jnp.exp(-rate * lag), 0, keepdims=True)
        chosen = iota(medium_ref.shape, 0) == group
        medium_row = jnp.sum(jnp.where(chosen, medium_ref[...].astype(F32), 0.0), 0, keepdims=True)
        medium_wide = toeplitz(medium_row)
        near = jnp.where(same, medium_wide[:, :LANES] + toeplitz(long_row)[:, :LANES], 0.0)
        table_ref[q, 0], table_ref[q, 1] = split(near)
        middle = [medium_wide[:, block:LANES], medium_wide[:, LANES : LANES + block]]
        table_ref[q, 2] = jnp.where(same, jnp.concatenate(middle, 1), 0.0).astype(BF16)
        table_ref[q, 3] = jnp.where(same, medium_wide[:, LANES:], 0.0).astype(BF16)
        rate_lanes, rate_rows, weight_rows = along_lanes(rate), along_rows(rate), along_rows(weight)
        to_end = jnp.exp(-rate_lanes * (block - 1 - row % block).astype(F32))
        kept = (lane // modes) % 2 == row // block
        table_ref[q, 4], table_ref[q, 5] = split(jnp.where(kept, to_end, 0.0))
        from_start = weight_rows * jnp.exp(-rate_rows * (lane % block + 1).astype(F32))
        kept = ((row // modes) % 2 == lane // block) & (row < 3 * width)
        high, low = split(jnp.where(kept, from_start, 0.0))
        both = jnp.where(row < 2 * width, high.astype(F32), low.astype(F32))
        table_ref[q, 6] = both.astype(BF16)
        rows = slice(8 * q, 8 * q + 8)
        step_ref[rows] = jnp.broadcast_to(jnp.exp(-rate_lanes * block), (8, LANES))
        jump_ref[rows] = jnp.broadcast_to(jnp.exp(-rate_lanes * (block * NEAR)), (8, LANES))
        rest_ref[rows] = jnp.broadcast_to(jnp.exp(-rate_lanes * (block * (NEAR - 1))), (8, LANES))


def begin_kernel(place, inner, value, outer, decay, residue, medium, taps, raw, tail, *tables):
    pack_kernel(inner, value, outer, raw, tail)
    tables_kernel(place, decay, residue, medium, taps, *tables)


def featurized(tap_ref, which, lanes, padded, rows):
    total = None
    for k in range(tap_ref.shape[1]):
        term = tap_ref[which, k : k + 1, lanes].astype(F32) * padded[HALO - k : HALO - k + rows, :]
        total = term if total is None else total + term
    return total


def tile_lanes(tile):
    return slice(tile * LANES, (tile + 1) * LANES)


def pack_kernel(inner_ref, value_ref, outer_ref, out_ref, tail_ref):
    tail_ref[...] = outer_ref[...]
    rows, channels = inner_ref.shape
    half = LANES // 2
    low = iota((rows, LANES), 1) < half
    for tile in range(channels // LANES):
        lanes = tile_lanes(tile)
        inner = inner_ref[:, lanes].astype(F32)
        value = value_ref[:, lanes].astype(F32)
        first = jnp.where(low, inner, pltpu.roll(value, half, 1))
        second = jnp.where(low, pltpu.roll(inner, half, 1), value)
        out_ref[2 * tile * rows : (2 * tile + 1) * rows] = first.astype(BF16)
        out_ref[(2 * tile + 1) * rows : (2 * tile + 2) * rows] = second.astype(BF16)


def outer_kernel(halo_ref, outer_ref, tap_ref, gain_in, out_ref, gain_ref, padded):
    gain_ref[...] = gain_in[...].astype(F32)
    rows, channels = outer_ref.shape
    for tile in range(channels // LANES):
        lanes = tile_lanes(tile)
        padded[tile, :HALO] = halo_ref[:HALO, lanes].astype(F32)
        padded[tile, HALO:] = outer_ref[:, lanes].astype(F32)
        out_ref[:, lanes] = featurized(tap_ref, 0, lanes, padded.at[tile], rows)


def of_group(x, q, count):
    return x.reshape(x.shape[0] // (8 * count), count, 8, LANES)[:, q].reshape(-1, LANES)


def gated(tap_ref, padded, rows):
    total = None
    for k in range(FEAT):
        term = tap_ref[k : k + 1] * padded[HALO - k : HALO - k + rows]
        total = term if total is None else total + term
    return (total * pltpu.roll(total, LANES // 2, 1)).astype(BF16).astype(F32)


def slabs_of(product):
    both = jnp.concatenate([product, pltpu.roll(product, LANES - 8, 1)], 0).T
    return both.reshape(LANES // 16, 16, LANES)[:, :8].reshape(LANES // 2, LANES)


def missing(tap_ref, tail, head):
    block = LANES // 2
    product = gated(tap_ref, jnp.concatenate([tail[-HALO:], head[:HALO]], 0), HALO)
    kept = (iota(product.shape, 0) < FEAT - 1) & (iota(product.shape, 1) < block)
    product = jnp.where(kept, product, 0.0)
    return slabs_of(jnp.concatenate([product, jnp.zeros((block - HALO, LANES), F32)], 0))[: block // 2]


def to_states(table_ref, slab):
    count = table_ref.shape[0]
    parts = []
    for q in range(count):
        x = slab[8 * q : 8 * q + 8].astype(BF16)
        parts.append(dot(x, table_ref[q, 4]) + dot(x, table_ref[q, 5]))
    return jnp.concatenate(parts, 0)


def find_local(width, wide, table_ref, states, out_ref):
    count = table_ref.shape[0]
    zeros = jnp.zeros((8, LANES), F32)
    for q in range(count):
        x = of_group(wide, q, count)
        before = jnp.concatenate([zeros, x[:-8]], 0).astype(BF16)
        earlier = jnp.concatenate([zeros, zeros, x[:-16]], 0).astype(BF16)
        x = x.astype(BF16)
        mixed = dot(x, table_ref[q, 0]) + dot(x, table_ref[q, 1])
        mixed = mixed + dot(before, table_ref[q, 2]) + dot(earlier, table_ref[q, 3])
        mixed = mixed + dot(two_parts(of_group(states, q, count), width), table_ref[q, 6])
        for block in range(x.shape[0] // 8):
            at = 8 * (count * block + q)
            out_ref[at : at + 8] = mixed[8 * block : 8 * block + 8]


def find_states(
    width, later, raw_ref, tap_ref, table_ref, step_ref, local_ref, end_ref, send_ref, padded, state_ref
):
    count = table_ref.shape[0]
    block = LANES // 2
    blocks = raw_ref.shape[0] // block
    padded[:HALO] = jnp.zeros((HALO, LANES), F32)
    padded[HALO:] = raw_ref[...].astype(F32)
    low = iota((block, LANES), 1) < block
    early = (iota((block, LANES), 0) < FEAT - 1)
    rows = 8 * count
    slabs = []
    for pair in range(blocks // 2):
        products = []
        for b in (2 * pair, 2 * pair + 1):
            product = gated(tap_ref, padded.at[b * block : (b + 1) * block + HALO], block)
            products.append(jnp.where(early, 0.0, product) if later and b == 0 else product)
        slabs.append(slabs_of(jnp.where(low, products[0], products[1])))
    wide = jnp.concatenate(slabs, 0)
    ends = []
    for q in range(count):
        x = of_group(wide, q, count).astype(BF16)
        local = dot(x, table_ref[q, 4]) + dot(x, table_ref[q, 5])
        step = step_ref[8 * q : 8 * q + 8]
        carry = jnp.zeros((8, LANES), F32)
        for b in range(blocks):
            at = rows * b + 8 * q
            state_ref[at : at + 8] = carry
            carry = carry * step + local[8 * b : 8 * b + 8]
        ends.append(carry)
    end = jnp.concatenate(ends, 0)
    end_ref[...] = end
    at = rows // 2
    send_ref[:at] = pack_state(end, width)
    send_ref[at : at + 2 * rows] = wide[(blocks - 2) * rows :].astype(BF16)
    at = at + 2 * rows
    send_ref[at : at + EDGE] = raw_ref[blocks * block - EDGE :]
    if send_ref.shape[0] > at + EDGE:
        send_ref[at + EDGE :] = raw_ref[:EDGE]
    find_local(width, wide, table_ref, state_ref[...], local_ref)


def super_block(place):
    return lax.div(place[0], NEAR)


def states_kernel(width, turn, place, raw_ref, tap_ref, table_ref, step_ref, *refs):
    if turn > 0:
        refs = refs[1:]
    if turn == 1:
        local_ref, end_ref, send_ref, padded, state_ref = refs
    elif turn == 3:
        local_ref, padded, state_ref, end_ref, send_ref = refs
    else:
        local_ref, send_ref, padded, state_ref, end_ref = refs

    @pl.when(super_block(place) == turn)
    def _():
        known = (raw_ref, tap_ref, table_ref, step_ref)
        find_states(width, turn > 0, *known, local_ref, end_ref, send_ref, padded, state_ref)


def chain_kernel(
    width,
    place,
    got_ref,
    raw_ref,
    tap_ref,
    table_ref,
    end_ref,
    jump_ref,
    rest_ref,
    send_ref,
    short_ref,
    next_ref,
):
    rows = end_ref.shape[0]

    @pl.when(super_block(place) == 1)
    def _():
        at = rows // 2 + 2 * rows
        tail = got_ref[at:].astype(F32)
        slab = missing(tap_ref, tail, raw_ref[:EDGE].astype(F32))
        end = end_ref[...] + rest_ref[...] * to_states(table_ref, slab)
        end = end + jump_ref[...] * unpack_state(got_ref[: rows // 2], width)
        state = pack_state(end, width)
        short_ref[: rows // 2] = state
        short_ref[rows // 2 :] = send_ref[at : at + EDGE]
        next_ref[: rows // 2] = state
        next_ref[rows // 2 :] = send_ref[rows // 2 : at + EDGE]


def spread(width, state, step, table, blocks, added=None):
    states = []
    for block in range(blocks):
        states.append(state)
        state = state * step
        if block == 0 and added is not None:
            state = state + added
    return dot(two_parts(jnp.concatenate(states, 0), width), table)


def joined(width, got, farther, local_ref, raw_ref, tap_ref, table_ref, step_ref):
    count = table_ref.shape[0]
    rows = 8 * count
    blocks = local_ref.shape[0] // rows
    one, two, end = rows // 2, rows // 2 + rows, rows // 2 + 2 * rows
    own_slab = missing(tap_ref, got[end : end + EDGE], raw_ref[:EDGE].astype(F32))
    incoming = unpack_state(got[:one], width) + farther
    added = to_states(table_ref, own_slab)
    zeros = jnp.zeros((8, LANES), F32)
    parts = []
    for q in range(count):
        at = slice(8 * q, 8 * q + 8)
        mixed = spread(width, incoming[at], step_ref[at], table_ref[q, 6], blocks, added[at])
        last_but_one, last, first = got[one:two][at], got[two:end][at], own_slab[at]
        now = jnp.concatenate([first, zeros, zeros, zeros], 0).astype(BF16)
        before = jnp.concatenate([last, first, zeros, zeros], 0).astype(BF16)
        earlier = jnp.concatenate([last_but_one, last, first, zeros], 0).astype(BF16)
        start = dot(now, table_ref[q, 0]) + dot(now, table_ref[q, 1])
        start = start + dot(before, table_ref[q, 2]) + dot(earlier, table_ref[q, 3])
        mixed = jnp.concatenate([mixed[:32] + start, mixed[32:]], 0)
        parts.append(mixed.reshape(blocks, 8, LANES))
    return local_ref[...] + jnp.concatenate(parts, 1).reshape(local_ref.shape)


def join_kernel(width, place, local_ref, got_01, raw_ref, tap_ref, table_ref, step_ref, out_ref):
    @pl.when(super_block(place) == 1)
    def _():
        got = got_01[...].astype(F32)
        out_ref[...] = joined(width, got, 0.0, local_ref, raw_ref, tap_ref, table_ref, step_ref)


def finish_kernel(
    width,
    place,
    near_ref,
    got_12,
    got_23,
    got_13,
    raw_ref,
    tap_ref,
    table_ref,
    step_ref,
    jump_ref,
    rest_ref,
    out_ref,
    farther,
):
    here = super_block(place)
    half = farther.shape[0] // 2

    @pl.when(here < 2)
    def _():
        out_ref[...] = near_ref[...].astype(BF16)

    @pl.when(here == 2)
    def _():
        farther[...] = jnp.zeros_like(farther)

    @pl.when(here == 3)
    def _():
        tail = got_13[half:].astype(F32)
        head = got_23[got_23.shape[0] - EDGE :].astype(F32)
        incoming = rest_ref[...] * to_states(table_ref, missing(tap_ref, tail, head))
        farther[...] = incoming + jump_ref[...] * unpack_state(got_13[:half], width)

    @pl.when(here > 1)
    def _():
        got = got_12[...].astype(F32) + got_23[: got_12.shape[0]].astype(F32)
        known = (near_ref, raw_ref, tap_ref, table_ref, step_ref)
        out_ref[...] = joined(width, got, farther[...], *known).astype(BF16)


def hidden_kernel(mixed_ref, outer_ref, residual_ref, hidden_ref, sum_ref):
    rows, channels = outer_ref.shape
    squares = jnp.zeros((rows, LANES), F32)
    for tile in range(channels // LANES):
        lanes = tile_lanes(tile)
        slabs = mixed_ref[tile * (LANES // 2) : (tile + 1) * (LANES // 2)].astype(F32)
        other = pltpu.roll(slabs, LANES // 2, 1)
        groups = LANES // 16
        both = jnp.concatenate([slabs.reshape(groups, 8, LANES), other.reshape(groups, 8, LANES)], 1)
        mixed = both.reshape(LANES, LANES).T[:rows]
        hidden = residual_ref[:, lanes].astype(F32) + outer_ref[:, lanes] * mixed
        hidden_ref[:, lanes] = hidden
        squares = squares + hidden * hidden
    tall = jnp.concatenate([squares, jnp.zeros_like(squares)], 0).T
    line = jnp.sum(tall, 0, keepdims=True)
    sum_ref[...] = jnp.broadcast_to(line, sum_ref.shape)


def norm_kernel(hidden_ref, sum_ref, gain_ref, out_ref):
    rows, channels = hidden_ref.shape
    parts = sum_ref[...].reshape(sum_ref.shape[0] // 8, 8, LANES)
    line = jnp.sum(parts, 0)
    scale = 1.0 / jnp.sqrt(line / D + 1e-05)
    tall = jnp.broadcast_to(scale[:1], (LANES, LANES)).T[:rows]
    for tile in range(channels // LANES):
        lanes = slice(tile * LANES, (tile + 1) * LANES)
        out_ref[:, lanes] = (hidden_ref[:, lanes] * gain_ref[:, lanes] * tall).astype(BF16)


def on_device(
    outer_input,
    inner_input,
    value_input,
    feature_taps,
    medium_taps,
    decay_rates,
    residues,
    residual,
    norm_gain,
):
    rows, channels = outer_input.shape
    groups, modes = decay_rates.shape
    size = lax.axis_size("ctx")
    parts = lax.axis_size("tp")
    tiles = channels // LANES
    vmem = pl.BlockSpec(memory_space=pltpu.VMEM)
    smem = pl.BlockSpec(memory_space=pltpu.SMEM)

    def call(kernel, out, *arrays, scalars=(), scratch=(), aliases={}):
        return pl.pallas_call(
            kernel,
            in_specs=[smem] * len(scalars) + [vmem] * len(arrays),
            out_specs=jax.tree.map(lambda _: vmem, out),
            out_shape=out,
            scratch_shapes=scratch,
            input_output_aliases=aliases,
        )(*scalars, *in_vmem(*arrays))

    slab_rows = rows * channels // LANES
    count = groups // NEAR
    width = 2 * modes
    far = size // NEAR
    assert far == 4
    pack = 8 * count
    with_width = lambda kernel: functools.partial(kernel, width)

    place = lax.axis_index("ctx").reshape(1).astype(jnp.int32)
    small = (decay_rates.T, residues.T, medium_taps.T, feature_taps)
    part = pl.BlockSpec((rows, channels), lambda i: (0, 0))
    lines = pltpu.VMEM((pack, LANES), F32)
    raw, outer_tail, table, step, jump, rest, taps = pl.pallas_call(
        begin_kernel,
        grid=(1,),
        in_specs=[
            smem,
            part,
            part,
            pl.BlockSpec((HALO, channels), lambda i: (rows // HALO - 1, 0)),
            *[pl.BlockSpec(x.shape, lambda i, n=x.ndim: (0,) * n) for x in small],
        ],
        out_specs=[vmem] * 7,
        out_shape=[
            pltpu.VMEM((NEAR * rows, LANES), BF16),
            pltpu.VMEM((HALO, channels), BF16),
            pltpu.VMEM((count, 7, LANES, LANES), BF16),
            lines,
            lines,
            lines,
            pltpu.VMEM((FEAT, LANES), F32),
        ],
        name="begin",
    )(place, inner_input, value_input, outer_input, *small)
    neighbours = [[NEAR * f + n for n in range(NEAR)] for f in range(far)]

    def exchange(x):
        slab = (NEAR, x.shape[0] // NEAR, LANES)
        y = lax.all_to_all(x.reshape(slab), "ctx", 0, 0, axis_index_groups=neighbours)
        return y.reshape(x.shape)

    packet = pltpu.VMEM((pack // 2 + 2 * pack + EDGE, LANES), BF16)
    with_head = pltpu.VMEM((pack // 2 + 2 * pack + 2 * EDGE, LANES), BF16)
    whole = pltpu.VMEM((slab_rows, LANES), F32)
    ends = pltpu.VMEM((pack, LANES), F32)
    scratch = [pltpu.VMEM((HALO + NEAR * rows, LANES), F32), whole]
    here = lax.axis_index("ctx") // NEAR
    swap = lambda kept, fresh: exchange(fresh)
    keep = lambda kept, fresh: kept

    def find(turn, arrived, local, outs):
        unread = {1: [], 3: [ends, packet]}.get(turn, [ends])
        return call(
            functools.partial(states_kernel, width, turn),
            outs,
            arrived,
            taps,
            table,
            step,
            *([] if turn == 0 else [local]),
            scalars=(place,),
            scratch=scratch + unread,
            aliases={} if turn == 0 else {5: 0},
        )

    def passed(x, start, end):
        pairs = [(NEAR * start + n, NEAR * end + n) for n in range(NEAR)]
        return lax.ppermute(x, "ctx", pairs)

    arrived = lax.cond(here == 0, lambda x: exchange(x), lambda x: x, raw)
    local, first_packed = find(0, arrived, None, [whole, packet])
    got_01 = passed(first_packed, 0, 1)
    outer_tail, arrived = lax.optimization_barrier((outer_tail, arrived))
    halo = lax.ppermute(outer_tail, "ctx", [(i, i + 1) for i in range(size - 1)])
    arrived = lax.cond(here == 1, swap, keep, arrived, raw)
    local, end, packed = find(1, arrived, local, [whole, ends, packet])
    state, repacked = call(
        with_width(chain_kernel),
        [pltpu.VMEM((pack // 2 + EDGE, LANES), BF16), packet],
        got_01,
        arrived,
        taps,
        table,
        end,
        jump,
        rest,
        packed,
        scalars=(place,),
    )
    got_13 = passed(state, 1, 3)
    got_12 = passed(repacked, 1, 2)
    arrived = lax.cond(here == 2, swap, keep, arrived, raw)
    local, packed = find(2, arrived, local, [whole, with_head])
    got_23 = passed(packed, 2, 3)
    arrived = lax.cond(here == 3, swap, keep, arrived, raw)
    (local,) = find(3, arrived, local, [whole])
    norm_gain, local = lax.optimization_barrier((norm_gain, local))
    outer_feat, gain = call(
        outer_kernel,
        [pltpu.VMEM((rows, channels), F32), pltpu.VMEM((1, channels), F32)],
        halo,
        outer_input,
        feature_taps,
        norm_gain.reshape(1, channels),
        scratch=[pltpu.VMEM((tiles, HALO + rows, LANES), F32)],
    )

    local, outer_feat, gain = lax.optimization_barrier((local, outer_feat, gain))

    near = call(
        with_width(join_kernel),
        whole,
        local,
        got_01,
        arrived,
        taps,
        table,
        step,
        scalars=(place,),
        aliases={1: 0},
    )
    mixed = call(
        with_width(finish_kernel),
        pltpu.VMEM((slab_rows, LANES), BF16),
        near,
        got_12,
        got_23,
        got_13,
        arrived,
        taps,
        table,
        step,
        jump,
        rest,
        scalars=(place,),
        scratch=[ends],
    )
    hidden, sums = call(
        hidden_kernel,
        [pltpu.VMEM((rows, channels), F32), pltpu.VMEM((8 * parts, LANES), F32)],
        exchange(mixed),
        outer_feat,
        residual,
    )
    all_sums = lax.all_to_all(sums.reshape(parts, 8, LANES), "tp", 0, 0)
    return call(
        norm_kernel,
        jax.ShapeDtypeStruct((rows, channels), BF16),
        hidden,
        all_sums.reshape(8 * parts, LANES),
        gain,
    )


def solution(mesh):
    return jax.shard_map(
        on_device,
        mesh=mesh,
        in_specs=(
            P("ctx", "tp"),
            P("ctx", "tp"),
            P("ctx", "tp"),
            P(None, None, "tp"),
            P(None, "tp"),
            P("tp", None),
            P("tp", None),
            P("ctx", "tp"),
            P("tp"),
        ),
        out_specs=P("ctx", "tp"),
        check_vma=False,
    )
```
